32 devices in a mesh: dp: 2 (over core), row: 4 (over z), col: 4 (over y, x).
Axes of the slice: x: 2, y: 2, z: 4, core: 2. Of those that a mesh axis runs over, the one named last changes fastest.
Arguments:
- inputs: bfloat16 [16, 1024, 1024], P(('dp', 'row'), None, 'col'), may hold values from -6 to 6
- out_grad: bfloat16 [16, 1024, 1024], P(('dp', 'row'), None, 'col'), may hold values from -6 to 6
- seq_lengths: int32 [16], P(('dp', 'row')), may hold values from 1 to 1024, 12288 in all
- first_gain: bfloat16 [1024], replicated, may hold values from 0.099609375 to 1.8984375
- query_proj: bfloat16 [1024, 1024], P('row', 'col'), may hold values from -0.1875 to 0.1875
- key_proj: bfloat16 [1024, 1024], P('row', 'col'), may hold values from -0.1875 to 0.1875
- value_proj: bfloat16 [1024, 2048], P('row', 'col'), may hold values from -0.1875 to 0.1875
- decay_proj: bfloat16 [1024, 8], P('row', 'col'), may hold values from -0.1875 to 0.1875
- beta_proj: bfloat16 [1024, 8], P('row', 'col'), may hold values from -0.1875 to 0.1875
- gate_proj: bfloat16 [1024, 2048], P('row', 'col'), may hold values from -0.1875 to 0.1875
- query_conv: bfloat16 [4, 1024], P(None, 'col'), may hold values from -3 to 3
- key_conv: bfloat16 [4, 1024], P(None, 'col'), may hold values from -3 to 3
- value_conv: bfloat16 [4, 2048], P(None, 'col'), may hold values from -3 to 3
- decay_log: float32 [8], P('col'), may hold values from 0 to 2.77
- step_bias: float32 [8], P('col'), may hold values from -6.9 to -2.3
- output_gain: bfloat16 [256], replicated, may hold values from 0.099609375 to 1.8984375
- output_proj: bfloat16 [2048, 1024], P('col', 'row'), may hold values from -0.25 to 0.25
- second_gain: bfloat16 [1024], replicated, may hold values from 0.099609375 to 1.8984375
- hidden_gate: bfloat16 [1024, 2816], P('row', 'col'), may hold values from -0.1875 to 0.1875
- hidden_up: bfloat16 [1024, 2816], P('row', 'col'), may hold values from -0.1875 to 0.1875
- hidden_down: bfloat16 [2816, 1024], P('col', 'row'), may hold values from -0.109375 to 0.109375
Outputs:
- result: bfloat16 [16, 1024, 1024], P(('dp', 'row'), None, 'col')
- input_grad: float32 [16, 1024, 1024], P(('dp', 'row'), None, 'col')
- first_gain_grad: float32 [1024], P('col')
- query_proj_grad: float32 [1024, 1024], P('row', 'col')
- key_proj_grad: float32 [1024, 1024], P('row', 'col')
- value_proj_grad: float32 [1024, 2048], P('row', 'col')
- decay_proj_grad: float32 [1024, 8], P('row', 'col')
- beta_proj_grad: float32 [1024, 8], P('row', 'col')
- gate_proj_grad: float32 [1024, 2048], P('row', 'col')
- query_conv_grad: float32 [4, 1024], P(None, 'col')
- key_conv_grad: float32 [4, 1024], P(None, 'col')
- value_conv_grad: float32 [4, 2048], P(None, 'col')
- decay_log_grad: float32 [8], P('col')
- step_bias_grad: float32 [8], P('col')
- output_gain_grad: float32 [256], replicated
- output_proj_grad: float32 [2048, 1024], P('col', 'row')
- second_gain_grad: float32 [1024], P('col')
- hidden_gate_grad: float32 [1024, 2816], P('row', 'col')
- hidden_up_grad: float32 [1024, 2816], P('row', 'col')
- hidden_down_grad: float32 [2816, 1024], P('col', 'row')
The draws below stay inside these ranges and needn't reach their ends.
Inputs may be any that keep to these rules, and one draw needn't show every extreme that they name: `seq_lengths`: the valid tokens of a sequence come first, the rest is padding; the longest sequence has exactly 1024.
All inputs are finite; a program needn't handle non-finite values. No bound on the sum of `seq_lengths` on one device may be relied on, other than what follows from the above.
Results may differ from the reference program's by a relative error of at most 0.014.
Values may be sent and summed in bfloat16 or wider, within the bound.
No kernel may reach another device: no remote copies, remote signals or barrier semaphores. Data moves between devices by JAX's collectives and lax.ppermute only.
A program may use at most 320 MiB of HBM per device.

```python
import math
import jax
import jax.numpy as jnp
import numpy as np
from jax import lax

D = 1024
H = 8
DK = 128
DV = 256
FF = 2816
CONV = 4
SPAN = 64
LEN = 1024
SEQ_DEV = 2
SEQS = 16


def block_scale(own_key, shape, shards, smallest, top_value):
    factor_of, own = 1.0, jax.random.fold_in(own_key, 6)
    for axis_at, shards_of in shards:
        heights = jnp.exp(jax.random.uniform(jax.random.fold_in(own, axis_at), (shards_of,), jnp.float32, smallest / len(shards), top_value / len(shards)))
        factor_of = factor_of * jnp.repeat(heights, shape[axis_at] // shards_of).reshape([-1 if axis == axis_at else 1 for axis in range(len(shape))])
    return factor_of


def profile(number_of, total, bound, skew):
    loads = [(1 << 20) // math.isqrt(standing ** skew) + 1 for standing in range(2, number_of + 1)]
    spare, given = total - bound - (number_of - 1), [1] * (number_of - 1)
    while spare > 0:
        free = [i for i in range(number_of - 1) if given[i] < bound]
        pool, budget = sum([loads[i] for i in free]), spare
        for i in free:
            more = min(bound - given[i], max(1, budget * loads[i] // pool), spare)
            given[i] = given[i] + more
            spare = spare - more
    return np.array([bound] + given)


def uneven(key, number_of, total, reach, skew):
    if number_of == 2:
        one = jax.random.randint(key, (), max(1, total - reach), min(reach, total - 1) + 1)
        return jnp.stack([one, total - one])
    lengths = jnp.asarray(profile(number_of, total, reach, skew), jnp.int32)
    couples = (number_of - 1) // 2
    giver, taker = lengths[1:1 + 2 * couples:2], lengths[2:2 + 2 * couples:2]
    room = jnp.minimum(giver - 1, reach - taker)
    moved = jax.random.randint(jax.random.fold_in(key, 1), (couples,), 0, 1 << 20) % (room + 1)
    lengths = lengths.at[1:1 + 2 * couples:2].set(giver - moved).at[2:2 + 2 * couples:2].set(taker + moved)
    return lengths[jax.random.permutation(jax.random.fold_in(key, 2), number_of)]


def bell_draw(stream_key, shape, width, most, shards=(), kind=jnp.bfloat16):
    gain = block_scale(stream_key, shape, shards, -0.22, 0.18) if shards else 1.0
    values = jax.random.normal(stream_key, shape, jnp.float32) * width * gain
    return jnp.minimum(jnp.maximum(values, -most), most).astype(kind)


def setup_inputs(seed: int = 0) -> dict:
    key_list = jax.random.split(jax.random.key(seed), 22)
    inputs = bell_draw(key_list[0], (SEQS, LEN, D), 1.0, 6.0, ((0, 8), (2, 4)))
    out_grad = bell_draw(key_list[1], (SEQS, LEN, D), 1.0, 6.0, ((0, 8), (2, 4)))
    seq_lengths = uneven(key_list[2], SEQS, SEQS * LEN * 3 // 4, LEN, 1).astype(jnp.int32)
    first_gain = jnp.clip(1.0 + 0.18 * jax.random.normal(key_list[3], (D,), jnp.float32), 0.099609375, 1.8984375).astype(jnp.bfloat16)
    query_proj = bell_draw(key_list[4], (D, H * DK), D ** -0.5, 0.1875, ((0, 4), (1, 4)))
    key_proj = bell_draw(key_list[5], (D, H * DK), D ** -0.5, 0.1875, ((0, 4), (1, 4)))
    value_proj = bell_draw(key_list[6], (D, H * DV), D ** -0.5, 0.1875, ((0, 4), (1, 4)))
    decay_proj = bell_draw(key_list[7], (D, H), D ** -0.5, 0.1875, ((0, 4), (1, 4)))
    beta_proj = bell_draw(key_list[8], (D, H), D ** -0.5, 0.1875, ((0, 4), (1, 4)))
    gate_proj = bell_draw(key_list[9], (D, H * DV), D ** -0.5, 0.1875, ((0, 4), (1, 4)))
    query_conv = bell_draw(key_list[10], (CONV, H * DK), CONV ** -0.5, 3.0, ((1, 4),))
    key_conv = bell_draw(key_list[11], (CONV, H * DK), CONV ** -0.5, 3.0, ((1, 4),))
    value_conv = bell_draw(key_list[12], (CONV, H * DV), CONV ** -0.5, 3.0, ((1, 4),))
    decay_log = jnp.clip(2.77 * jax.random.uniform(key_list[13], (H,), jnp.float32) ** block_scale(key_list[13], (H,), ((0, 4),), -0.2, 0.2), 0.0, 2.77)
    step_bias = jnp.clip(-6.9 + 4.6000001430511475 * jax.random.uniform(key_list[14], (H,), jnp.float32) ** block_scale(key_list[14], (H,), ((0, 4),), -0.2, 0.2), -6.9, -2.3)
    output_gain = jnp.clip(1.0 + 0.18 * jax.random.normal(key_list[15], (DV,), jnp.float32), 0.099609375, 1.8984375).astype(jnp.bfloat16)
    output_proj = bell_draw(key_list[16], (H * DV, D), (H * DV // 4) ** -0.5, 0.25, ((0, 4), (1, 4)))
    second_gain = jnp.clip(1.0 + 0.18 * jax.random.normal(key_list[17], (D,), jnp.float32), 0.099609375, 1.8984375).astype(jnp.bfloat16)
    hidden_gate = bell_draw(key_list[18], (D, FF), D ** -0.5, 0.1875, ((0, 4), (1, 4)))
    hidden_up = bell_draw(key_list[19], (D, FF), D ** -0.5, 0.1875, ((0, 4), (1, 4)))
    hidden_down = bell_draw(key_list[20], (FF, D), FF ** -0.5, 0.109375, ((0, 4), (1, 4)))
    return {"inputs": inputs, "out_grad": out_grad, "seq_lengths": seq_lengths, "first_gain": first_gain, "query_proj": query_proj, "key_proj": key_proj, "value_proj": value_proj, "decay_proj": decay_proj, "beta_proj": beta_proj, "gate_proj": gate_proj, "query_conv": query_conv, "key_conv": key_conv, "value_conv": value_conv, "decay_log": decay_log, "step_bias": step_bias, "output_gain": output_gain, "output_proj": output_proj, "second_gain": second_gain, "hidden_gate": hidden_gate, "hidden_up": hidden_up, "hidden_down": hidden_down}


@jax.custom_vjp
def low(v):
    return lax.optimization_barrier(v.astype(jnp.bfloat16)).astype(jnp.float32)

@jax.custom_vjp
def low_back(v):
    return v

def low_keep(v):
    return (low(v), None)

def low_pass(kept, grad):
    return (grad,)

def back_keep(v):
    return (v, None)

def back_low(kept, grad):
    return (low(grad),)
low.defvjp(low_keep, low_pass)
low_back.defvjp(back_keep, back_low)
HIGHEST = lax.Precision.HIGHEST
NORM_EPS = 1e-05
UNIT_EPS = 1e-06

def causal_conv(values, kernel):
    length = values.shape[1]
    padded = jnp.pad(values, ((0, 0), (CONV - 1, 0), (0, 0)))
    summed = padded[:, 0:length] * kernel[0]
    for offset in range(1, CONV):
        summed = summed + padded[:, offset:offset + length] * kernel[offset]
    return jax.nn.silu(summed)

def unit_rows(values):
    return values * lax.rsqrt(lax.optimization_barrier(jnp.sum(values * values, axis=-1, keepdims=True)) + UNIT_EPS)

def delta_rule(queries, key_vecs, val_vecs, log_decay, beta_vals):
    seq_count, length, head_count = log_decay.shape
    blocks = length // SPAN

    def split_blocks(values):
        shaped = values.reshape((seq_count, blocks, SPAN, head_count) + values.shape[3:])
        return jnp.swapaxes(shaped, 2, 3)
    query_blk = split_blocks(queries)
    key_blk = split_blocks(key_vecs)
    value_blk = split_blocks(val_vecs)
    beta_blk = split_blocks(beta_vals)
    cumulative = jnp.cumsum(split_blocks(log_decay), axis=-1)
    log_gap = cumulative[..., :, None] - cumulative[..., None, :]
    row_ids = lax.broadcasted_iota(jnp.int32, (SPAN, SPAN), 0)
    col_ids = lax.broadcasted_iota(jnp.int32, (SPAN, SPAN), 1)
    lower_strict = row_ids > col_ids
    lower_incl = row_ids >= col_ids
    strict_fac = jnp.where(lower_strict, jnp.exp(jnp.where(lower_strict, log_gap, 0.0)), 0.0)
    incl_fac = jnp.where(lower_incl, jnp.exp(jnp.where(lower_incl, log_gap, 0.0)), 0.0)
    key_gram = jnp.einsum('sbhik,sbhjk->sbhij', key_blk, key_blk, precision=HIGHEST)
    coupling = beta_blk[..., None] * key_gram * strict_fac
    system = coupling + jnp.eye(SPAN, dtype=coupling.dtype)
    decayed = jnp.exp(cumulative)[..., None]
    right_side = jnp.concatenate([beta_blk[..., None] * value_blk, beta_blk[..., None] * decayed * key_blk], axis=-1)
    solved = jax.scipy.linalg.solve_triangular(system, right_side, lower=True, unit_diagonal=True)
    value_dim = value_blk.shape[-1]
    new_vals = solved[..., :value_dim]
    key_part = solved[..., value_dim:]
    scores = jnp.einsum('sbhik,sbhjk->sbhij', query_blk, key_blk, precision=HIGHEST) * incl_fac
    query_dec = query_blk * decayed
    key_dec = key_blk * jnp.exp(cumulative[..., -1:] - cumulative)[..., None]
    block_decay = jnp.exp(cumulative[..., -1])[..., None, None]
    stacked = tuple((jnp.moveaxis(piece, 1, 0) for piece in (new_vals, key_part, query_dec, scores, key_dec, block_decay)))

    def advance(carry_state, pieces):
        new_part, key_piece, query_piece, score_piece, keydec_piece, decay_piece = pieces
        updates = new_part - jnp.einsum('shck,shkv->shcv', key_piece, carry_state, precision=HIGHEST)
        output = jnp.einsum('shck,shkv->shcv', query_piece, carry_state, precision=HIGHEST)
        output = output + jnp.einsum('shij,shjv->shiv', score_piece, updates, precision=HIGHEST)
        carry_state = decay_piece * carry_state + jnp.einsum('shck,shcv->shkv', keydec_piece, updates, precision=HIGHEST)
        return (carry_state, output)
    initial = jnp.zeros((seq_count, head_count, key_blk.shape[-1], value_dim), queries.dtype)
    unused_state, outputs = lax.scan(advance, initial, stacked)
    return jnp.transpose(outputs, (1, 0, 3, 2, 4)).reshape(seq_count, length, head_count, value_dim)

def mixer(query_in, key_in, value_in, decay_in, beta_in, gate_in, query_conv, key_conv, value_conv, decay_log, step_bias, output_gain):
    seq_count, length = (query_in.shape[0], query_in.shape[1])
    head_count = decay_log.shape[0]
    queries = unit_rows(causal_conv(query_in, query_conv).reshape(seq_count, length, head_count, DK)) * DK ** (-0.5)
    key_vecs = unit_rows(causal_conv(key_in, key_conv).reshape(seq_count, length, head_count, DK))
    val_vecs = causal_conv(value_in, value_conv).reshape(seq_count, length, head_count, DV)
    beta_vals = jax.nn.sigmoid(beta_in)
    log_decay = -jnp.exp(decay_log) * jax.nn.softplus(decay_in + step_bias)
    mixer_out = delta_rule(queries, key_vecs, val_vecs, log_decay, beta_vals)
    normed = mixer_out * lax.rsqrt(lax.optimization_barrier(jnp.mean(mixer_out * mixer_out, axis=-1, keepdims=True)) + NORM_EPS)
    normed = normed * output_gain * jax.nn.silu(gate_in.reshape(seq_count, length, head_count, DV))
    return normed.reshape(seq_count, length, head_count * DV)

def layer(params, inputs, seq_lengths):
    first_gain, query_proj, key_proj, value_proj, decay_proj, beta_proj, gate_proj, query_conv, key_conv, value_conv, decay_log, step_bias, output_gain, output_proj, second_gain, hidden_gate, hidden_up, hidden_down = params
    seq_count, length = (inputs.shape[0], inputs.shape[1])
    positions = lax.broadcasted_iota(jnp.int32, (seq_count, length), 1)
    row_vals = inputs.reshape(seq_count * length, D)
    valid_mask = (positions < seq_lengths[:, None]).astype(row_vals.dtype).reshape(-1, 1)
    first_scale = lax.rsqrt(lax.optimization_barrier(jnp.mean(row_vals * row_vals, axis=-1, keepdims=True)) + NORM_EPS)
    normed_first = low(row_vals * first_scale * first_gain * valid_mask)

    def project(weight):
        return low_back(jnp.dot(normed_first, weight, precision=HIGHEST)).reshape(seq_count, length, weight.shape[1])
    mixer_out = mixer(project(query_proj), project(key_proj), project(value_proj), project(decay_proj), project(beta_proj), project(gate_proj), query_conv, key_conv, value_conv, decay_log, step_bias, output_gain)
    mixed_low = low(mixer_out).reshape(seq_count * length, -1)
    attention = low_back(jnp.dot(mixed_low, output_proj, precision=HIGHEST))
    hidden_res = row_vals + attention
    second_scale = lax.rsqrt(lax.optimization_barrier(jnp.mean(hidden_res * hidden_res, axis=-1, keepdims=True)) + NORM_EPS)
    normed_second = low(hidden_res * second_scale * second_gain * valid_mask)
    gate_act = low_back(jnp.dot(normed_second, hidden_gate, precision=HIGHEST))
    up_act = low_back(jnp.dot(normed_second, hidden_up, precision=HIGHEST))
    hidden_act = low(jax.nn.silu(gate_act) * up_act)
    feed_out = low_back(jnp.dot(hidden_act, hidden_down, precision=HIGHEST))
    return ((hidden_res + feed_out) * valid_mask).reshape(seq_count, length, D)

def reference(inputs, out_grad, seq_lengths, first_gain, query_proj, key_proj, value_proj, decay_proj, beta_proj, gate_proj, query_conv, key_conv, value_conv, decay_log, step_bias, output_gain, output_proj, second_gain, hidden_gate, hidden_up, hidden_down):
    params = jax.tree.map(lambda value: value.astype(jnp.float32), (first_gain, query_proj, key_proj, value_proj, decay_proj, beta_proj, gate_proj, query_conv, key_conv, value_conv, decay_log, step_bias, output_gain, output_proj, second_gain, hidden_gate, hidden_up, hidden_down))
    inputs_f = inputs.astype(jnp.float32)
    length_groups = seq_lengths.reshape(-1, SEQ_DEV).astype(jnp.int32)

    def forward(params_f, inputs_all):
        grouped = inputs_all.reshape(-1, SEQ_DEV, LEN, D)
        group_step = jax.checkpoint(lambda seq_pair: layer(params_f, seq_pair[0], seq_pair[1]))
        outputs = lax.map(group_step, (grouped, length_groups))
        return outputs.reshape(SEQS, LEN, D)
    result, backward = jax.vjp(forward, params, inputs_f)
    grads, input_grad = backward(out_grad.astype(jnp.float32))
    return (result.astype(jnp.bfloat16), input_grad, grads[0], grads[1], grads[2], grads[3], grads[4], grads[5], grads[6], grads[7], grads[8], grads[9], grads[10], grads[11], grads[12], grads[13], grads[14], grads[15], grads[16], grads[17])
```

```python
import functools
import jax
import jax.numpy as jnp
from jax import lax
from jax.experimental import pallas as pl
from jax.experimental.pallas import tpu as pltpu
from jax.sharding import PartitionSpec as P

DK = 128
DV = 256
CONV = 4
NORM_EPS = 1e-05
UNIT_EPS = 1e-06
BLK = 128
SUB = 32
F32 = jnp.float32
BF16 = jnp.bfloat16


def mm(a, b):
    return lax.dot_general(a, b, (((1,), (0,)), ((), ())), preferred_element_type=F32)


def mm_nt(a, b):
    return lax.dot_general(a, b, (((1,), (1,)), ((), ())), preferred_element_type=F32)


def halves(a):
    hi = a.astype(BF16)
    return hi, (a - hi.astype(F32)).astype(BF16)


def mm3(a, b):
    ah, al = halves(a)
    bh, bl = halves(b)
    return mm(ah, bh) + (mm(ah, bl) + mm(al, bh))


def sigm(v):
    return 1.0 / (1.0 + jnp.exp(-v))


def iota2(shape, axis):
    return lax.broadcasted_iota(jnp.int32, shape, axis)


def unit_lower_inverse(mats):
    groups = BLK // SUB
    lane = iota2((SUB, BLK), 1)
    sub = iota2((SUB, BLK), 0)
    lane_group = lane // SUB
    solved = []
    for b in range(groups):
        rows = slice(b * SUB, (b + 1) * SUB)
        packed = jnp.zeros((SUB, BLK), F32)
        for p, mat in enumerate(mats):
            piece = mat[rows]
            shift = (SUB * (p - b)) % BLK
            if shift:
                piece = pltpu.roll(piece, shift, 1)
            packed = jnp.where(lane_group == p, piece, packed)
        acc = jnp.where(lane - lane_group * SUB == sub, 1.0, 0.0).astype(F32)
        tiles = [acc[8 * t : 8 * t + 8] for t in range(SUB // 8)]
        coefs = [packed[8 * t : 8 * t + 8] for t in range(SUB // 8)]
        base = (iota2((8, BLK), 1) // SUB) * SUB
        for j in range(SUB - 1):
            row = jnp.broadcast_to(tiles[j // 8][j % 8 : j % 8 + 1], (8, BLK))
            for t in range((j + 1) // 8, SUB // 8):
                col = jnp.take_along_axis(coefs[t], base + j, axis=1)
                tiles[t] = tiles[t] - col * row
        solved.append(jnp.concatenate(tiles, axis=0))
    out = []
    row_i = iota2((BLK, BLK), 0)
    col_i = iota2((BLK, BLK), 1)
    for p, mat in enumerate(mats):
        blocks = []
        for b in range(groups):
            piece = solved[b]
            shift = (SUB * (b - p)) % BLK
            if shift:
                piece = pltpu.roll(piece, shift, 1)
            blocks.append(jnp.where(lane_group == b, piece, 0.0))
        inv = jnp.concatenate(blocks, axis=0)
        zero32 = jnp.zeros((SUB, BLK), F32)
        off = jnp.where((row_i // 64 == col_i // 64) & (row_i // SUB > col_i // SUB), mat, 0.0)
        lhs = jnp.concatenate([off[32:64], off[96:128]], axis=0)
        part = mm3(lhs, inv)
        placed = jnp.concatenate([zero32, part[:32], zero32, part[32:]], axis=0)
        lhs = jnp.concatenate([inv[32:64], inv[96:128]], axis=0)
        part = mm3(lhs, placed)
        inv = inv - jnp.concatenate([zero32, part[:32], zero32, part[32:]], axis=0)
        off = jnp.where(col_i[64:] < 64, mat[64:], 0.0)
        part = mm3(off, inv)
        zero64 = jnp.zeros((64, BLK), F32)
        part = mm3(inv[64:], jnp.concatenate([zero64, part], axis=0))
        inv = jnp.concatenate([inv[:64], inv[64:] - part], axis=0)
        out.append(inv)
    return out


def decay_terms(ab, neg_rate, bias, heads):
    pre = ab + bias
    soft = jnp.maximum(pre, 0.0) + jnp.log(1.0 + jnp.exp(-jnp.abs(pre)))
    log_decay = neg_rate * soft
    beta = sigm(ab)
    row_i = iota2((BLK, BLK), 0)
    col_i = iota2((BLK, BLK), 1)
    tri = jnp.where(row_i >= col_i, 1.0, 0.0).astype(BF16)
    hi = log_decay.astype(BF16)
    rest = log_decay - hi.astype(F32)
    mid = rest.astype(BF16)
    low = (rest - mid.astype(F32)).astype(BF16)
    cum = mm(tri, hi) + (mm(tri, mid) + mm(tri, low))
    return log_decay, beta, cum


def conv_taps(xs_ref, s, kernel):
    pre = xs_ref[s, 5 : 5 + BLK, :] * kernel[0:1]
    for i in range(1, CONV):
        pre = pre + xs_ref[s, 5 + i : 5 + i + BLK, :] * kernel[i : i + 1]
    return pre


def fwd_kernel(heads, nseq, proj_ref, conv_ref, rate_ref, gain_ref,
               mixed_ref, o_ref, u_ref, s_ref, t_ref, xs_ref, state_ref):
    qkv = heads * (2 * DK + DV)
    gate_at = qkv
    ab_at = qkv + heads * DV
    step = pl.program_id(1)

    @pl.when(step == 0)
    def _():
        xs_ref[:, 0:8, :] = jnp.zeros((nseq, 8, qkv), F32)
        state_ref[...] = jnp.zeros_like(state_ref)

    row_i = iota2((BLK, BLK), 0)
    col_i = iota2((BLK, BLK), 1)
    kernel = conv_ref[...]
    neg_rate = rate_ref[0:1]
    bias = rate_ref[1:2]
    gain = gain_ref[...]
    items = []
    for s in range(nseq):
        xs_ref[s, 8 : 8 + BLK, :] = proj_ref[s, :, 0:qkv]
        pre = conv_taps(xs_ref, s, kernel)
        xs_ref[s, 0:8, :] = xs_ref[s, BLK : BLK + 8, :]
        act = pre * sigm(pre)
        ab = proj_ref[s, :, ab_at : ab_at + 128]
        _, beta_all, cum_all = decay_terms(ab, neg_rate, bias, heads)
        cum_t = cum_all.T
        for h in range(heads):
            q = act[:, h * DK : (h + 1) * DK]
            k = act[:, (heads + h) * DK : (heads + h + 1) * DK]
            v = act[:, 2 * heads * DK + h * DV : 2 * heads * DK + (h + 1) * DV]
            qn = q * (lax.rsqrt(jnp.sum(q * q, axis=1, keepdims=True) + UNIT_EPS) * DK ** -0.5)
            kn = k * lax.rsqrt(jnp.sum(k * k, axis=1, keepdims=True) + UNIT_EPS)
            cum = cum_all[:, h : h + 1]
            cum_row = cum_t[h : h + 1, :]
            beta = beta_all[:, heads + h : heads + h + 1]
            ratio = jnp.exp(jnp.where(row_i >= col_i, cum - cum_row, -1e30))
            kb = kn.astype(BF16)
            kq = jnp.concatenate([kb, qn.astype(BF16)], axis=0)
            gram = mm_nt(kq, kb)
            a = jnp.where(row_i > col_i, gram[:BLK] * ratio * beta, 0.0)
            p = gram[BLK:] * ratio
            last = cum[BLK - 1 : BLK]
            kd = kn * jnp.exp(last - cum)
            items.append((s, h, kq, a, p, kd, v, beta, jnp.exp(cum), jnp.exp(last)))
    invs = []
    for at in range(0, len(items), 4):
        invs = invs + unit_lower_inverse([item[3] for item in items[at : at + 4]])
    for item, inv in zip(items, invs):
        s, h, kq, a, p, kd, v, beta, ecum, elast = item
        state = state_ref[s, h]
        low_state = state.astype(BF16)
        ks_qs = mm(kq, low_state)
        x = beta * (v - ecum * ks_qs[:BLK])
        inv_low = inv.astype(BF16)
        u = mm(inv_low, x.astype(BF16)).astype(BF16)
        pk = jnp.concatenate([p, kd.T], axis=0).astype(BF16)
        pu = mm(pk, u)
        o = ecum * ks_qs[BLK:] + pu[:BLK]
        state_ref[s, h] = elast * state + pu[BLK:]
        s_ref[s, 0, h] = low_state
        t_ref[s, 0, h] = inv_low
        cols = slice(h * DV, (h + 1) * DV)
        u_ref[s, :, cols] = u
        o_ref[s, :, cols] = o
        g = proj_ref[s, :, gate_at + h * DV : gate_at + (h + 1) * DV]
        norm = o * lax.rsqrt(jnp.mean(o * o, axis=1, keepdims=True) + NORM_EPS)
        mixed_ref[s, :, cols] = (norm * gain * (g * sigm(g))).astype(BF16)


def rate_rows(decay_log, step_bias):
    heads = decay_log.shape[0]
    pad = 128 - heads
    return jnp.stack([jnp.pad(-jnp.exp(decay_log), (0, pad)), jnp.pad(step_bias, (0, pad))])


def mixer_fwd(proj, conv, rates, gain, heads, nseq):
    seqs, length, width = proj.shape
    blocks = length // BLK
    qkv = heads * (2 * DK + DV)
    vals = heads * DV
    tok = lambda i, c: (i, c, 0)
    return pl.pallas_call(
        functools.partial(fwd_kernel, heads, nseq),
        out_shape=(
            jax.ShapeDtypeStruct((seqs, length, vals), BF16),
            jax.ShapeDtypeStruct((seqs, length, vals), F32),
            jax.ShapeDtypeStruct((seqs, length, vals), BF16),
            jax.ShapeDtypeStruct((seqs, blocks, heads, DK, DV), BF16),
            jax.ShapeDtypeStruct((seqs, blocks, heads, BLK, BLK), BF16),
        ),
        grid=(seqs // nseq, blocks),
        in_specs=[
            pl.BlockSpec((nseq, BLK, width), tok),
            pl.BlockSpec((CONV, qkv), lambda i, c: (0, 0)),
            pl.BlockSpec((2, 128), lambda i, c: (0, 0)),
            pl.BlockSpec((1, DV), lambda i, c: (0, 0)),
        ],
        out_specs=(
            pl.BlockSpec((nseq, BLK, vals), tok),
            pl.BlockSpec((nseq, BLK, vals), tok),
            pl.BlockSpec((nseq, BLK, vals), tok),
            pl.BlockSpec((nseq, 1, heads, DK, DV), lambda i, c: (i, c, 0, 0, 0)),
            pl.BlockSpec((nseq, 1, heads, BLK, BLK), lambda i, c: (i, c, 0, 0, 0)),
        ),
        scratch_shapes=[
            pltpu.VMEM((nseq, 8 + BLK, qkv), F32),
            pltpu.VMEM((nseq, heads, DK, DV), F32),
        ],
        compiler_params=pltpu.CompilerParams(dimension_semantics=("arbitrary", "arbitrary")),
        name="mixer_fwd",
    )(proj, conv, rates, gain)


def colsum(v):
    return jnp.sum(v.reshape(v.shape[0] // 8, 8, v.shape[1]), axis=0)


def bwd_kernel(heads, nseq, proj_ref, prev_ref, dmix_ref, o_ref, u_ref, s_ref, t_ref,
               conv_ref, rate_ref, gain_ref,
               dproj_ref, dots_ref, dconv_ref, drate_ref, dgain_ref, xs_ref, ds_ref, dstate_ref):
    qkv = heads * (2 * DK + DV)
    gate_at = qkv
    ab_at = qkv + heads * DV
    step = pl.program_id(1)
    first = pl.num_programs(1) - 1

    @pl.when(step == 0)
    def _():
        ds_ref[:, BLK : BLK + 8, :] = jnp.zeros((nseq, 8, qkv), F32)
        dstate_ref[...] = jnp.zeros_like(dstate_ref)

    @pl.when((step == 0) & (pl.program_id(0) == 0))
    def _():
        dconv_ref[...] = jnp.zeros_like(dconv_ref)
        drate_ref[...] = jnp.zeros_like(drate_ref)
        dgain_ref[...] = jnp.zeros_like(dgain_ref)

    row_i = iota2((BLK, BLK), 0)
    col_i = iota2((BLK, BLK), 1)
    lower = row_i >= col_i
    strict = row_i > col_i
    kernel = conv_ref[...]
    neg_rate = rate_ref[0:1]
    bias = rate_ref[1:2]
    gain = gain_ref[...]
    has_prev = jnp.where(step == first, 0.0, 1.0).astype(F32)
    lane1 = iota2((1, 128), 1)
    for s in range(nseq):
        xs_ref[s, 0:8, :] = prev_ref[s, :, 0:qkv] * has_prev
        xs_ref[s, 8 : 8 + BLK, :] = proj_ref[s, :, 0:qkv]
        pre = conv_taps(xs_ref, s, kernel)
        sig = sigm(pre)
        act = pre * sig
        dsilu = sig * (1.0 + pre * (1.0 - sig))
        ab = proj_ref[s, :, ab_at : ab_at + 128]
        log_decay, beta_all, cum_all = decay_terms(ab, neg_rate, bias, heads)
        cum_t = cum_all.T
        dots = jnp.zeros((BLK, 1), F32)
        dcum_all = jnp.zeros((BLK, 128), F32)
        dbeta_all = jnp.zeros((BLK, 128), F32)
        dact = [None] * (3 * heads)
        for h in range(heads):
            q = act[:, h * DK : (h + 1) * DK]
            k = act[:, (heads + h) * DK : (heads + h + 1) * DK]
            v = act[:, 2 * heads * DK + h * DV : 2 * heads * DK + (h + 1) * DV]
            rq = lax.rsqrt(jnp.sum(q * q, axis=1, keepdims=True) + UNIT_EPS)
            rk = lax.rsqrt(jnp.sum(k * k, axis=1, keepdims=True) + UNIT_EPS)
            qh = q * rq
            qn = qh * DK ** -0.5
            kn = k * rk
            cum = cum_all[:, h : h + 1]
            cum_row = cum_t[h : h + 1, :]
            beta = beta_all[:, heads + h : heads + h + 1]
            ecum = jnp.exp(cum)
            last = cum[BLK - 1 : BLK]
            elast = jnp.exp(last)
            ratio = jnp.exp(jnp.where(lower, cum - cum_row, -1e30))
            ktail = jnp.exp(last - cum)
            kb = kn.astype(BF16)
            qb = qn.astype(BF16)
            gram = mm_nt(jnp.concatenate([kb, qb], axis=0), kb)
            sfac = jnp.where(strict, ratio * beta, 0.0)
            kgr = gram[:BLK]
            p = gram[BLK:] * ratio
            cols = slice(h * DV, (h + 1) * DV)
            o = o_ref[s, :, cols]
            g = proj_ref[s, :, gate_at + h * DV : gate_at + (h + 1) * DV]
            dm = dmix_ref[s, :, cols].astype(F32)
            ro = lax.rsqrt(jnp.mean(o * o, axis=1, keepdims=True) + NORM_EPS)
            n = o * ro
            gs = sigm(g)
            gsil = g * gs
            dmn = dm * n
            dgain_ref[...] += colsum(dmn * gsil)
            dgate = dmn * gain * (gs * (1.0 + g * (1.0 - gs)))
            dproj_ref[s, :, gate_at + h * DV : gate_at + (h + 1) * DV] = dgate.astype(BF16)
            dots = dots + jnp.sum(dgate * g, axis=1, keepdims=True)
            dn = dm * gain * gsil
            do = ro * (dn - n * jnp.mean(dn * n, axis=1, keepdims=True))
            dob = do.astype(BF16)
            dstate = dstate_ref[s, h]
            dstb = dstate.astype(BF16)
            u = u_ref[s, :, cols]
            sb = s_ref[s, 0, h]
            tinv = t_ref[s, 0, h]
            kd = kn * ktail
            du = mm(jnp.concatenate([p.T, kd], axis=1).astype(BF16), jnp.concatenate([dob, dstb], axis=0))
            dx = mm(tinv.astype(F32).T.astype(BF16), du.astype(BF16))
            dxb = dx.astype(BF16)
            ddx = jnp.concatenate([dob, dxb], axis=0)
            both = mm_nt(ddx, jnp.concatenate([sb, u], axis=0))
            be = beta * ecum
            z = both[BLK:, :DK]
            dqi = ecum * both[:BLK, :DK]
            dki = -be * z
            dks = -be * dx
            lhs = jnp.concatenate([qn.T, kn.T], axis=1).astype(BF16)
            rhs = jnp.concatenate([(ecum * do).astype(BF16), dks.astype(BF16)], axis=0)
            dstate_ref[s, h] = elast * dstate + mm(lhs, rhs)
            dkd = mm_nt(u, dstb)
            dp = both[:BLK, DK:]
            da = -both[BLK:, DK:]
            dqk = dp * ratio
            dkg = da * sfac
            dlog = dp * p + dkg * kgr
            pair = jnp.concatenate([dqk, dkg + dkg.T], axis=0).astype(BF16)
            prod = mm(pair, kb)
            dqn = dqi + prod[:BLK]
            dkn = dki + prod[BLK:] + mm(dqk.T.astype(BF16), qb) + dkd * ktail
            kz = jnp.sum(kn * z, axis=1, keepdims=True)
            dkdk = jnp.sum(dkd * kd, axis=1, keepdims=True)
            row_sum = jnp.sum(dlog, axis=1, keepdims=True)
            col_sum = jnp.sum(dlog.T, axis=1, keepdims=True)
            dcum = row_sum - col_sum + jnp.sum(qn * dqi, axis=1, keepdims=True) - be * kz - dkdk
            tail = jnp.sum(dkdk, axis=0, keepdims=True) + elast * jnp.sum(
                jnp.sum(sb.astype(F32) * dstate, axis=1, keepdims=True), axis=0, keepdims=True)
            dcum = dcum + jnp.where(row_i[:, 0:1] == BLK - 1, tail, 0.0)
            kgl = jnp.sum(da * jnp.where(strict, ratio * kgr, 0.0), axis=1, keepdims=True)
            dbeta = jnp.sum(dx * v, axis=1, keepdims=True) - ecum * kz + kgl
            dcum_all = jnp.where(lane1 == h, dcum, dcum_all)
            dbeta_all = jnp.where(lane1 == heads + h, dbeta, dbeta_all)
            dact[h] = (DK ** -0.5 * rq) * (dqn - qh * jnp.sum(dqn * qh, axis=1, keepdims=True))
            dact[heads + h] = rk * (dkn - kn * jnp.sum(dkn * kn, axis=1, keepdims=True))
            dact[2 * heads + h] = beta * dx
        tri = jnp.where(col_i >= row_i, 1.0, 0.0).astype(BF16)
        hi, lo = halves(dcum_all)
        dlog_decay = mm(tri, hi) + mm(tri, lo)
        dpre_a = dlog_decay * neg_rate * sigm(ab + bias)
        dpre_b = dbeta_all * beta_all * (1.0 - beta_all)
        dproj_ref[s, :, ab_at : ab_at + 128] = (dpre_a + dpre_b).astype(BF16)
        dots = dots + jnp.sum((dpre_a + dpre_b) * ab, axis=1, keepdims=True)
        drate_ref[0:8, :] += colsum(dlog_decay * log_decay)
        drate_ref[8:16, :] += colsum(dpre_a)
        dpre = jnp.concatenate(dact, axis=1) * dsilu
        ds_ref[s, 0:BLK, :] = dpre
        dx_in = ds_ref[s, 3 : 3 + BLK, :] * kernel[0:1]
        for i in range(1, CONV):
            dx_in = dx_in + ds_ref[s, 3 - i : 3 - i + BLK, :] * kernel[i : i + 1]
        dproj_ref[s, :, 0:qkv] = dx_in.astype(BF16)
        dots = dots + jnp.sum(dx_in * xs_ref[s, 8 : 8 + BLK, :], axis=1, keepdims=True)
        dots_ref[s, 0] = jnp.broadcast_to(dots, (BLK, 128)).T[0:8]
        for i in range(CONV):
            dconv_ref[8 * i : 8 * i + 8, :] += colsum(dpre * xs_ref[s, 5 + i : 5 + i + BLK, :])
        ds_ref[s, BLK : BLK + 8, :] = ds_ref[s, 0:8, :]


def mixer_bwd(proj, dmixed, saved, conv, rates, gain, heads, nseq):
    o, u, states, invs = saved
    seqs, length, width = proj.shape
    blocks = length // BLK
    qkv = heads * (2 * DK + DV)
    vals = heads * DV
    tok = lambda i, c: (i, blocks - 1 - c, 0)
    whole = lambda i, c: (0, 0)
    dproj, dots, dconv, drate, dgain = pl.pallas_call(
        functools.partial(bwd_kernel, heads, nseq),
        out_shape=(
            jax.ShapeDtypeStruct((seqs, length, width), BF16),
            jax.ShapeDtypeStruct((seqs, blocks, 8, 128), F32),
            jax.ShapeDtypeStruct((8 * CONV, qkv), F32),
            jax.ShapeDtypeStruct((16, 128), F32),
            jax.ShapeDtypeStruct((8, DV), F32),
        ),
        grid=(seqs // nseq, blocks),
        in_specs=[
            pl.BlockSpec((nseq, BLK, width), tok),
            pl.BlockSpec((nseq, 8, qkv), lambda i, c: (i, jnp.maximum((blocks - 1 - c) * (BLK // 8) - 1, 0), 0)),
            pl.BlockSpec((nseq, BLK, vals), tok),
            pl.BlockSpec((nseq, BLK, vals), tok),
            pl.BlockSpec((nseq, BLK, vals), tok),
            pl.BlockSpec((nseq, 1, heads, DK, DV), lambda i, c: (i, blocks - 1 - c, 0, 0, 0)),
            pl.BlockSpec((nseq, 1, heads, BLK, BLK), lambda i, c: (i, blocks - 1 - c, 0, 0, 0)),
            pl.BlockSpec((CONV, qkv), whole),
            pl.BlockSpec((2, 128), whole),
            pl.BlockSpec((1, DV), whole),
        ],
        out_specs=(
            pl.BlockSpec((nseq, BLK, width), tok),
            pl.BlockSpec((nseq, 1, 8, 128), lambda i, c: (i, blocks - 1 - c, 0, 0)),
            pl.BlockSpec((8 * CONV, qkv), whole),
            pl.BlockSpec((16, 128), whole),
            pl.BlockSpec((8, DV), whole),
        ),
        scratch_shapes=[
            pltpu.VMEM((nseq, 8 + BLK, qkv), F32),
            pltpu.VMEM((nseq, BLK + 8, qkv), F32),
            pltpu.VMEM((nseq, heads, DK, DV), F32),
        ],
        compiler_params=pltpu.CompilerParams(dimension_semantics=("arbitrary", "arbitrary")),
        name="mixer_bwd",
    )(proj, proj, dmixed, o, u, states, invs, conv, rates, gain)
    dconv = jnp.sum(dconv.reshape(CONV, 8, qkv), axis=1)
    drate = jnp.sum(drate.reshape(2, 8, 128), axis=1)[:, :heads]
    dgain = jnp.sum(dgain, axis=0)
    return dproj, dots[:, :, 0, :], dconv, drate[0], drate[1], dgain


D = 1024
PARTS = 1


def contract_rows(left, right):
    return lax.dot_general(left, right, (((0,), (0,)), ((), ())), preferred_element_type=F32)


def xor_perm(size, bit):
    return [(i, i ^ bit) for i in range(size)]


def send_col(values, bit):
    return lax.ppermute(values, "col", xor_perm(4, bit))


def gather_features(values):
    half = values.shape[0] // 2
    from_x = send_col(values, 1)
    from_y = send_col(values, 2)
    far_top = send_col(from_y[:half], 1)
    far_low = send_col(from_x[half:], 2)
    return jnp.concatenate(
        [values, from_x, from_y, jnp.concatenate([far_top, far_low], axis=0)], axis=1
    )


def sum_features(partial):
    width = partial.shape[1] // 4
    half = partial.shape[0] // 2
    own, part_x, part_y, far = [partial[:, width * i : width * i + width] for i in range(4)]
    far = far.astype(BF16)
    via_x = send_col(far[:half], 1).astype(F32)
    via_y = send_col(far[half:], 2).astype(F32)
    to_y = jnp.concatenate([part_y[:half] + via_x, part_y[half:]], axis=0).astype(BF16)
    to_x = jnp.concatenate([part_x[:half], part_x[half:] + via_y], axis=0).astype(BF16)
    return own + send_col(to_x, 1).astype(F32) + send_col(to_y, 2).astype(F32)


def sum_scalars(values):
    total = values
    for bit in range(1, 4):
        total = total + send_col(values, bit)
    return total


def col_order(values, col):
    rows = values.shape[0] // 4
    return jnp.concatenate(
        [lax.dynamic_slice_in_dim(values, (col ^ b) * rows, rows, 0) for b in range(4)], axis=0
    )


def swap_cores(mine, dp):
    other = lax.ppermute(mine, "dp", [(0, 1), (1, 0)])
    return jnp.where(
        dp == 0, jnp.concatenate([mine, other], axis=0), jnp.concatenate([other, mine], axis=0)
    )


def gather_weight(block, dp, col):
    rows = block.shape[0] // 2
    half = lax.dynamic_slice_in_dim(block, dp * rows, rows, 0)
    return col_order(lax.all_gather(half, ("row", "dp"), axis=0, tiled=True), col)


def scatter_weight(grad, dp, col):
    mine = lax.psum_scatter(
        col_order(grad.astype(BF16), col), ("row", "dp"), scatter_dimension=0, tiled=True
    )
    return swap_cores(mine, dp).astype(F32)


def on_device(
    inputs,
    out_grad,
    seq_lengths,
    first_gain,
    query_proj,
    key_proj,
    value_proj,
    decay_proj,
    beta_proj,
    gate_proj,
    query_conv,
    key_conv,
    value_conv,
    decay_log,
    step_bias,
    output_gain,
    output_proj,
    second_gain,
    hidden_gate,
    hidden_up,
    hidden_down,
):
    seq_count, length, col_width = inputs.shape
    heads = decay_log.shape[0]
    parts = PARTS
    per_part = seq_count // parts
    tokens = per_part * length
    col = lax.axis_index("col")
    dp = lax.axis_index("dp")
    row_block = query_proj.shape[0]
    vals = heads * DV
    qkv = heads * (2 * DK + DV)
    ff_half = hidden_gate.shape[1]

    in_block = jnp.concatenate(
        [query_proj, key_proj, value_proj, gate_proj, decay_proj, beta_proj,
         jnp.zeros((row_block, 128 - 2 * heads), BF16)], axis=1)
    in_weights = gather_weight(in_block, dp, col)
    out_weights = gather_weight(output_proj.T, dp, col)
    ff_weights = gather_weight(
        jnp.concatenate([hidden_gate, hidden_up, hidden_down.T], axis=1), dp, col)
    up_weights = ff_weights[:, : 2 * ff_half]
    down_weights = ff_weights[:, 2 * ff_half :]

    conv = jnp.concatenate([query_conv, key_conv, value_conv], axis=1).astype(F32)
    rates = rate_rows(decay_log, step_bias)
    gain_row = output_gain.astype(F32)[None]
    first_order = col_order(first_gain.astype(F32), col)[None]
    second_order = col_order(second_gain.astype(F32), col)[None]
    first_local = first_order[:, :col_width]
    second_local = second_order[:, :col_width]
    positions = lax.broadcasted_iota(jnp.int32, (seq_count, length), 1)
    valid_all = (positions < seq_lengths[:, None]).astype(F32)

    state = []
    for part in range(parts):
        seqs = slice(part * per_part, (part + 1) * per_part)
        valid = valid_all[seqs].reshape(tokens, 1)
        local_low = inputs[seqs].reshape(tokens, col_width)
        full = gather_features(local_low).astype(F32)
        scale = lax.rsqrt(jnp.mean(full * full, axis=1, keepdims=True) + NORM_EPS)
        normed = (full * scale * first_order * valid).astype(BF16)
        grad_out = out_grad[seqs].reshape(tokens, col_width).astype(F32) * valid
        state.append(dict(valid=valid, local=local_low.astype(F32), scale=scale, normed=normed,
                          grad_out=grad_out))
    for st in state:
        proj = jnp.dot(st["normed"], in_weights, preferred_element_type=F32)
        st["proj"] = proj.reshape(per_part, length, -1)
        mixed, *st["saved"] = mixer_fwd(st["proj"], conv, rates, gain_row, heads, per_part)
        st["mixed"] = mixed.reshape(tokens, vals)
        attention = sum_features(mm_nt(st["mixed"], out_weights))
        st["hidden"] = st["local"] + attention
        st["grad_full"] = gather_features(st["grad_out"].astype(BF16))
    results = []
    ff_grad = 0.0
    second_gain_grad = 0.0
    for st in state:
        full = gather_features(st["hidden"].astype(BF16)).astype(F32)
        scale = lax.rsqrt(jnp.mean(full * full, axis=1, keepdims=True) + NORM_EPS)
        normed = (full * scale * second_order * st["valid"]).astype(BF16)
        gate_up = jnp.dot(normed, up_weights, preferred_element_type=F32)
        gate_act = gate_up[:, :ff_half]
        up_act = gate_up[:, ff_half:]
        sig = jax.nn.sigmoid(gate_act)
        silu = gate_act * sig
        act = (silu * up_act).astype(BF16)
        inner_grad = jnp.dot(st["grad_full"], down_weights, preferred_element_type=F32)
        gate_grad = (inner_grad * up_act * sig * (1.0 + gate_act * (1.0 - sig))).astype(BF16)
        up_grad = (inner_grad * silu).astype(BF16)
        both = jnp.concatenate([gate_grad, up_grad], axis=1)
        dots = sum_scalars(jnp.sum(
            gate_grad.astype(F32) * gate_act + up_grad.astype(F32) * up_act, axis=1))[:, None]
        second_grad = sum_features(mm_nt(both, up_weights)) * st["valid"]
        hat = st["hidden"] * scale
        second_gain_grad = second_gain_grad + jnp.sum(second_grad * hat, axis=0)
        st["hidden_grad"] = st["grad_out"] + scale * (
            second_grad * second_local - hat * (dots * (1.0 / D)))
        st["attn_grad"] = gather_features(st["hidden_grad"].astype(BF16))
        feed = sum_features(mm_nt(act, down_weights))
        results.append(((st["hidden"] + feed) * st["valid"]).astype(BF16))
        ff_grad = ff_grad + jnp.concatenate(
            [contract_rows(normed, both), contract_rows(st["grad_full"], act)], axis=1)
    ff_grad = scatter_weight(ff_grad, dp, col)
    out_weight_grad = 0.0
    in_weight_grad = 0.0
    first_gain_grad = 0.0
    input_grads = []
    small = 0.0
    for st in state:
        mixed_grad = jnp.dot(st["attn_grad"], out_weights, preferred_element_type=F32)
        out_weight_grad = out_weight_grad + contract_rows(st["attn_grad"], st["mixed"])
        dproj, dots, *grads = mixer_bwd(
            st["proj"], mixed_grad.reshape(per_part, length, vals), st["saved"], conv, rates,
            gain_row, heads, per_part)
        small = small + jnp.concatenate([grad.reshape(-1) for grad in grads])
        dproj = dproj.reshape(tokens, -1)
        dots = sum_scalars(dots)
        in_weight_grad = in_weight_grad + contract_rows(st["normed"], dproj)
        st["dots"] = dots.reshape(tokens, 1)
        first_grad = sum_features(mm_nt(dproj, in_weights)) * st["valid"]
        hat = st["local"] * st["scale"]
        first_gain_grad = first_gain_grad + jnp.sum(first_grad * hat, axis=0)
        input_grads.append(st["hidden_grad"] + st["scale"] * (
            first_grad * first_local - hat * (st["dots"] * (1.0 / D))))
    out_weight_grad = scatter_weight(out_weight_grad, dp, col)
    in_weight_grad = scatter_weight(in_weight_grad, dp, col)
    conv_size = CONV * qkv
    small_sums = lax.psum(
        jnp.concatenate([small[: conv_size + 2 * heads], second_gain_grad, first_gain_grad]),
        ("dp", "row"))
    conv_grad = small_sums[:conv_size].reshape(CONV, qkv)
    gain_out_grad = lax.psum(small[conv_size + 2 * heads :], ("dp", "row", "col"))
    at = conv_size + 2 * heads
    gate_at = qkv + vals
    qk = heads * DK
    return (
        jnp.concatenate(results, axis=0).reshape(seq_count, length, col_width),
        jnp.concatenate(input_grads, axis=0).reshape(seq_count, length, col_width),
        small_sums[at + col_width : at + 2 * col_width],
        in_weight_grad[:, :qk],
        in_weight_grad[:, qk : 2 * qk],
        in_weight_grad[:, 2 * qk : qkv],
        in_weight_grad[:, gate_at : gate_at + heads],
        in_weight_grad[:, gate_at + heads : gate_at + 2 * heads],
        in_weight_grad[:, qkv:gate_at],
        conv_grad[:, :qk],
        conv_grad[:, qk : 2 * qk],
        conv_grad[:, 2 * qk :],
        small_sums[conv_size : conv_size + heads],
        small_sums[conv_size + heads : at],
        gain_out_grad,
        out_weight_grad.T,
        small_sums[at : at + col_width],
        ff_grad[:, :ff_half],
        ff_grad[:, ff_half : 2 * ff_half],
        ff_grad[:, 2 * ff_half :].T,
    )


def solution(mesh):
    in_specs = (
        P(("dp", "row"), None, "col"),
        P(("dp", "row"), None, "col"),
        P(("dp", "row")),
        P(),
        P("row", "col"),
        P("row", "col"),
        P("row", "col"),
        P("row", "col"),
        P("row", "col"),
        P("row", "col"),
        P(None, "col"),
        P(None, "col"),
        P(None, "col"),
        P("col"),
        P("col"),
        P(),
        P("col", "row"),
        P(),
        P("row", "col"),
        P("row", "col"),
        P("col", "row"),
    )
    out_specs = (
        P(("dp", "row"), None, "col"),
        P(("dp", "row"), None, "col"),
        P("col"),
        P("row", "col"),
        P("row", "col"),
        P("row", "col"),
        P("row", "col"),
        P("row", "col"),
        P("row", "col"),
        P(None, "col"),
        P(None, "col"),
        P(None, "col"),
        P("col"),
        P("col"),
        P(),
        P("col", "row"),
        P("col"),
        P("row", "col"),
        P("row", "col"),
        P("col", "row"),
    )
    return jax.shard_map(
        on_device, mesh=mesh, in_specs=in_specs, out_specs=out_specs, check_vma=False
    )
```

```python
import functools
import jax
import jax.numpy as jnp
from jax import lax
from jax.experimental import pallas as pl
from jax.experimental.pallas import tpu as pltpu
from jax.sharding import PartitionSpec as P

DK = 128
DV = 256
CONV = 4
NORM_EPS = 1e-05
UNIT_EPS = 1e-06
BLK = 128
SUB = 32
F32 = jnp.float32
BF16 = jnp.bfloat16


def mm(a, b):
    return lax.dot_general(a, b, (((1,), (0,)), ((), ())), preferred_element_type=F32)


def mm_nt(a, b):
    return lax.dot_general(a, b, (((1,), (1,)), ((), ())), preferred_element_type=F32)


def halves(a):
    hi = a.astype(BF16)
    return hi, (a - hi.astype(F32)).astype(BF16)


def mm3(a, b):
    ah, al = halves(a)
    bh, bl = halves(b)
    return mm(ah, bh) + (mm(ah, bl) + mm(al, bh))


def sigm(v):
    return 1.0 / (1.0 + jnp.exp(-v))


def iota2(shape, axis):
    return lax.broadcasted_iota(jnp.int32, shape, axis)


def unit_lower_inverse(mats):
    groups = BLK // SUB
    lane = iota2((SUB, BLK), 1)
    sub = iota2((SUB, BLK), 0)
    lane_group = lane // SUB
    solved = []
    for b in range(groups):
        rows = slice(b * SUB, (b + 1) * SUB)
        packed = jnp.zeros((SUB, BLK), F32)
        for p, mat in enumerate(mats):
            piece = mat[rows]
            shift = (SUB * (p - b)) % BLK
            if shift:
                piece = pltpu.roll(piece, shift, 1)
            packed = jnp.where(lane_group == p, piece, packed)
        acc = jnp.where(lane - lane_group * SUB == sub, 1.0, 0.0).astype(F32)
        tiles = [acc[8 * t : 8 * t + 8] for t in range(SUB // 8)]
        coefs = [packed[8 * t : 8 * t + 8] for t in range(SUB // 8)]
        base = (iota2((8, BLK), 1) // SUB) * SUB
        for j in range(SUB - 1):
            row = jnp.broadcast_to(tiles[j // 8][j % 8 : j % 8 + 1], (8, BLK))
            for t in range((j + 1) // 8, SUB // 8):
                col = jnp.take_along_axis(coefs[t], base + j, axis=1)
                tiles[t] = tiles[t] - col * row
        solved.append(jnp.concatenate(tiles, axis=0))
    out = []
    row_i = iota2((BLK, BLK), 0)
    col_i = iota2((BLK, BLK), 1)
    for p, mat in enumerate(mats):
        blocks = []
        for b in range(groups):
            piece = solved[b]
            shift = (SUB * (b - p)) % BLK
            if shift:
                piece = pltpu.roll(piece, shift, 1)
            blocks.append(jnp.where(lane_group == b, piece, 0.0))
        inv = jnp.concatenate(blocks, axis=0)
        zero32 = jnp.zeros((SUB, BLK), F32)
        off = jnp.where((row_i // 64 == col_i // 64) & (row_i // SUB > col_i // SUB), mat, 0.0)
        lhs = jnp.concatenate([off[32:64], off[96:128]], axis=0)
        part = mm3(lhs, inv)
        placed = jnp.concatenate([zero32, part[:32], zero32, part[32:]], axis=0)
        lhs = jnp.concatenate([inv[32:64], inv[96:128]], axis=0)
        part = mm3(lhs, placed)
        inv = inv - jnp.concatenate([zero32, part[:32], zero32, part[32:]], axis=0)
        off = jnp.where(col_i[64:] < 64, mat[64:], 0.0)
        part = mm3(off, inv)
        zero64 = jnp.zeros((64, BLK), F32)
        part = mm3(inv[64:], jnp.concatenate([zero64, part], axis=0))
        inv = jnp.concatenate([inv[:64], inv[64:] - part], axis=0)
        out.append(inv)
    return out


def decay_terms(ab, neg_rate, bias, heads):
    pre = ab + bias
    soft = jnp.maximum(pre, 0.0) + jnp.log(1.0 + jnp.exp(-jnp.abs(pre)))
    log_decay = neg_rate * soft
    beta = sigm(ab)
    row_i = iota2((BLK, BLK), 0)
    col_i = iota2((BLK, BLK), 1)
    tri = jnp.where(row_i >= col_i, 1.0, 0.0).astype(BF16)
    hi = log_decay.astype(BF16)
    rest = log_decay - hi.astype(F32)
    mid = rest.astype(BF16)
    low = (rest - mid.astype(F32)).astype(BF16)
    cum = mm(tri, hi) + (mm(tri, mid) + mm(tri, low))
    return log_decay, beta, cum


def conv_taps(xs_ref, s, kernel):
    pre = xs_ref[s, 5 : 5 + BLK, :] * kernel[0:1]
    for i in range(1, CONV):
        pre = pre + xs_ref[s, 5 + i : 5 + i + BLK, :] * kernel[i : i + 1]
    return pre


def fwd_kernel(heads, nseq, proj_ref, conv_ref, rate_ref, gain_ref,
               mixed_ref, o_ref, u_ref, s_ref, t_ref, xs_ref, state_ref):
    qkv = heads * (2 * DK + DV)
    gate_at = qkv
    ab_at = qkv + heads * DV
    step = pl.program_id(1)

    @pl.when(step == 0)
    def _():
        xs_ref[:, 0:8, :] = jnp.zeros((nseq, 8, qkv), F32)
        state_ref[...] = jnp.zeros_like(state_ref)

    row_i = iota2((BLK, BLK), 0)
    col_i = iota2((BLK, BLK), 1)
    kernel = conv_ref[...]
    neg_rate = rate_ref[0:1]
    bias = rate_ref[1:2]
    gain = gain_ref[...]
    items = []
    for s in range(nseq):
        xs_ref[s, 8 : 8 + BLK, :] = proj_ref[s, :, 0:qkv]
        pre = conv_taps(xs_ref, s, kernel)
        xs_ref[s, 0:8, :] = xs_ref[s, BLK : BLK + 8, :]
        act = pre * sigm(pre)
        ab = proj_ref[s, :, ab_at : ab_at + 128]
        _, beta_all, cum_all = decay_terms(ab, neg_rate, bias, heads)
        cum_t = cum_all.T
        for h in range(heads):
            q = act[:, h * DK : (h + 1) * DK]
            k = act[:, (heads + h) * DK : (heads + h + 1) * DK]
            v = act[:, 2 * heads * DK + h * DV : 2 * heads * DK + (h + 1) * DV]
            qn = q * (lax.rsqrt(jnp.sum(q * q, axis=1, keepdims=True) + UNIT_EPS) * DK ** -0.5)
            kn = k * lax.rsqrt(jnp.sum(k * k, axis=1, keepdims=True) + UNIT_EPS)
            cum = cum_all[:, h : h + 1]
            cum_row = cum_t[h : h + 1, :]
            beta = beta_all[:, heads + h : heads + h + 1]
            ratio = jnp.exp(jnp.where(row_i >= col_i, cum - cum_row, -1e30))
            kb = kn.astype(BF16)
            kq = jnp.concatenate([kb, qn.astype(BF16)], axis=0)
            gram = mm_nt(kq, kb)
            a = jnp.where(row_i > col_i, gram[:BLK] * ratio * beta, 0.0)
            p = gram[BLK:] * ratio
            last = cum[BLK - 1 : BLK]
            kd = kn * jnp.exp(last - cum)
            items.append((s, h, kq, a, p, kd, v, beta, jnp.exp(cum), jnp.exp(last)))
    invs = []
    for at in range(0, len(items), 4):
        invs = invs + unit_lower_inverse([item[3] for item in items[at : at + 4]])
    for item, inv in zip(items, invs):
        s, h, kq, a, p, kd, v, beta, ecum, elast = item
        state = state_ref[s, h]
        low_state = state.astype(BF16)
        ks_qs = mm(kq, low_state)
        x = beta * (v - ecum * ks_qs[:BLK])
        inv_low = inv.astype(BF16)
        u = mm(inv_low, x.astype(BF16)).astype(BF16)
        pk = jnp.concatenate([p, kd.T], axis=0).astype(BF16)
        pu = mm(pk, u)
        o = ecum * ks_qs[BLK:] + pu[:BLK]
        state_ref[s, h] = elast * state + pu[BLK:]
        s_ref[s, 0, h] = low_state
        t_ref[s, 0, h] = inv_low
        cols = slice(h * DV, (h + 1) * DV)
        u_ref[s, :, cols] = u
        o_ref[s, :, cols] = o
        g = proj_ref[s, :, gate_at + h * DV : gate_at + (h + 1) * DV]
        norm = o * lax.rsqrt(jnp.mean(o * o, axis=1, keepdims=True) + NORM_EPS)
        mixed_ref[s, :, cols] = (norm * gain * (g * sigm(g))).astype(BF16)


def rate_rows(decay_log, step_bias):
    heads = decay_log.shape[0]
    pad = 128 - heads
    return jnp.stack([jnp.pad(-jnp.exp(decay_log), (0, pad)), jnp.pad(step_bias, (0, pad))])


def mixer_fwd(proj, conv, rates, gain, heads, nseq):
    seqs, length, width = proj.shape
    blocks = length // BLK
    qkv = heads * (2 * DK + DV)
    vals = heads * DV
    tok = lambda i, c: (i, c, 0)
    return pl.pallas_call(
        functools.partial(fwd_kernel, heads, nseq),
        out_shape=(
            jax.ShapeDtypeStruct((seqs, length, vals), BF16),
            jax.ShapeDtypeStruct((seqs, length, vals), F32),
            jax.ShapeDtypeStruct((seqs, length, vals), BF16),
            jax.ShapeDtypeStruct((seqs, blocks, heads, DK, DV), BF16),
            jax.ShapeDtypeStruct((seqs, blocks, heads, BLK, BLK), BF16),
        ),
        grid=(seqs // nseq, blocks),
        in_specs=[
            pl.BlockSpec((nseq, BLK, width), tok),
            pl.BlockSpec((CONV, qkv), lambda i, c: (0, 0)),
            pl.BlockSpec((2, 128), lambda i, c: (0, 0)),
            pl.BlockSpec((1, DV), lambda i, c: (0, 0)),
        ],
        out_specs=(
            pl.BlockSpec((nseq, BLK, vals), tok),
            pl.BlockSpec((nseq, BLK, vals), tok),
            pl.BlockSpec((nseq, BLK, vals), tok),
            pl.BlockSpec((nseq, 1, heads, DK, DV), lambda i, c: (i, c, 0, 0, 0)),
            pl.BlockSpec((nseq, 1, heads, BLK, BLK), lambda i, c: (i, c, 0, 0, 0)),
        ),
        scratch_shapes=[
            pltpu.VMEM((nseq, 8 + BLK, qkv), F32),
            pltpu.VMEM((nseq, heads, DK, DV), F32),
        ],
        compiler_params=pltpu.CompilerParams(dimension_semantics=("arbitrary", "arbitrary")),
        cost_estimate=pl.CostEstimate(
            flops=seqs * length * heads * 6_000_000, bytes_accessed=seqs * length * width * 8,
            transcendentals=0),
        name="mixer_fwd",
    )(proj, conv, rates, gain)


def colsum(v):
    return jnp.sum(v.reshape(v.shape[0] // 8, 8, v.shape[1]), axis=0)


def bwd_kernel(heads, nseq, proj_ref, prev_ref, dmix_ref, o_ref, u_ref, s_ref, t_ref,
               conv_ref, rate_ref, gain_ref,
               dproj_ref, dots_ref, dconv_ref, drate_ref, dgain_ref, xs_ref, ds_ref, dstate_ref):
    qkv = heads * (2 * DK + DV)
    gate_at = qkv
    ab_at = qkv + heads * DV
    step = pl.program_id(1)
    first = pl.num_programs(1) - 1

    @pl.when(step == 0)
    def _():
        ds_ref[:, BLK : BLK + 8, :] = jnp.zeros((nseq, 8, qkv), F32)
        dstate_ref[...] = jnp.zeros_like(dstate_ref)

    @pl.when((step == 0) & (pl.program_id(0) == 0))
    def _():
        dconv_ref[...] = jnp.zeros_like(dconv_ref)
        drate_ref[...] = jnp.zeros_like(drate_ref)
        dgain_ref[...] = jnp.zeros_like(dgain_ref)

    row_i = iota2((BLK, BLK), 0)
    col_i = iota2((BLK, BLK), 1)
    lower = row_i >= col_i
    strict = row_i > col_i
    kernel = conv_ref[...]
    neg_rate = rate_ref[0:1]
    bias = rate_ref[1:2]
    gain = gain_ref[...]
    has_prev = jnp.where(step == first, 0.0, 1.0).astype(F32)
    lane1 = iota2((1, 128), 1)
    for s in range(nseq):
        xs_ref[s, 0:8, :] = prev_ref[s, :, 0:qkv] * has_prev
        xs_ref[s, 8 : 8 + BLK, :] = proj_ref[s, :, 0:qkv]
        pre = conv_taps(xs_ref, s, kernel)
        sig = sigm(pre)
        act = pre * sig
        dsilu = sig * (1.0 + pre * (1.0 - sig))
        ab = proj_ref[s, :, ab_at : ab_at + 128]
        log_decay, beta_all, cum_all = decay_terms(ab, neg_rate, bias, heads)
        cum_t = cum_all.T
        dots = jnp.zeros((BLK, 1), F32)
        dcum_all = jnp.zeros((BLK, 128), F32)
        dbeta_all = jnp.zeros((BLK, 128), F32)
        dact = [None] * (3 * heads)
        for h in range(heads):
            q = act[:, h * DK : (h + 1) * DK]
            k = act[:, (heads + h) * DK : (heads + h + 1) * DK]
            v = act[:, 2 * heads * DK + h * DV : 2 * heads * DK + (h + 1) * DV]
            rq = lax.rsqrt(jnp.sum(q * q, axis=1, keepdims=True) + UNIT_EPS)
            rk = lax.rsqrt(jnp.sum(k * k, axis=1, keepdims=True) + UNIT_EPS)
            qh = q * rq
            qn = qh * DK ** -0.5
            kn = k * rk
            cum = cum_all[:, h : h + 1]
            cum_row = cum_t[h : h + 1, :]
            beta = beta_all[:, heads + h : heads + h + 1]
            ecum = jnp.exp(cum)
            last = cum[BLK - 1 : BLK]
            elast = jnp.exp(last)
            ratio = jnp.exp(jnp.where(lower, cum - cum_row, -1e30))
            ktail = jnp.exp(last - cum)
            kb = kn.astype(BF16)
            qb = qn.astype(BF16)
            gram = mm_nt(jnp.concatenate([kb, qb], axis=0), kb)
            sfac = jnp.where(strict, ratio * beta, 0.0)
            kgr = gram[:BLK]
            p = gram[BLK:] * ratio
            cols = slice(h * DV, (h + 1) * DV)
            o = o_ref[s, :, cols]
            g = proj_ref[s, :, gate_at + h * DV : gate_at + (h + 1) * DV]
            dm = dmix_ref[s, :, cols].astype(F32)
            ro = lax.rsqrt(jnp.mean(o * o, axis=1, keepdims=True) + NORM_EPS)
            n = o * ro
            gs = sigm(g)
            gsil = g * gs
            dmn = dm * n
            dgain_ref[...] += colsum(dmn * gsil)
            dgate = dmn * gain * (gs * (1.0 + g * (1.0 - gs)))
            dproj_ref[s, :, gate_at + h * DV : gate_at + (h + 1) * DV] = dgate.astype(BF16)
            dots = dots + jnp.sum(dgate * g, axis=1, keepdims=True)
            dn = dm * gain * gsil
            do = ro * (dn - n * jnp.mean(dn * n, axis=1, keepdims=True))
            dob = do.astype(BF16)
            dstate = dstate_ref[s, h]
            dstb = dstate.astype(BF16)
            u = u_ref[s, :, cols]
            sb = s_ref[s, 0, h]
            tinv = t_ref[s, 0, h]
            kd = kn * ktail
            du = mm(jnp.concatenate([p.T, kd], axis=1).astype(BF16), jnp.concatenate([dob, dstb], axis=0))
            dx = mm(tinv.astype(F32).T.astype(BF16), du.astype(BF16))
            dxb = dx.astype(BF16)
            ddx = jnp.concatenate([dob, dxb], axis=0)
            both = mm_nt(ddx, jnp.concatenate([sb, u], axis=0))
            be = beta * ecum
            z = both[BLK:, :DK]
            dqi = ecum * both[:BLK, :DK]
            dki = -be * z
            dks = -be * dx
            lhs = jnp.concatenate([qn.T, kn.T], axis=1).astype(BF16)
            rhs = jnp.concatenate([(ecum * do).astype(BF16), dks.astype(BF16)], axis=0)
            dstate_ref[s, h] = elast * dstate + mm(lhs, rhs)
            dkd = mm_nt(u, dstb)
            dp = both[:BLK, DK:]
            da = -both[BLK:, DK:]
            dqk = dp * ratio
            dkg = da * sfac
            dlog = dp * p + dkg * kgr
            pair = jnp.concatenate([dqk, dkg + dkg.T], axis=0).astype(BF16)
            prod = mm(pair, kb)
            dqn = dqi + prod[:BLK]
            dkn = dki + prod[BLK:] + mm(dqk.T.astype(BF16), qb) + dkd * ktail
            kz = jnp.sum(kn * z, axis=1, keepdims=True)
            dkdk = jnp.sum(dkd * kd, axis=1, keepdims=True)
            row_sum = jnp.sum(dlog, axis=1, keepdims=True)
            col_sum = jnp.sum(dlog.T, axis=1, keepdims=True)
            dcum = row_sum - col_sum + jnp.sum(qn * dqi, axis=1, keepdims=True) - be * kz - dkdk
            tail = jnp.sum(dkdk, axis=0, keepdims=True) + elast * jnp.sum(
                jnp.sum(sb.astype(F32) * dstate, axis=1, keepdims=True), axis=0, keepdims=True)
            dcum = dcum + jnp.where(row_i[:, 0:1] == BLK - 1, tail, 0.0)
            kgl = jnp.sum(da * jnp.where(strict, ratio * kgr, 0.0), axis=1, keepdims=True)
            dbeta = jnp.sum(dx * v, axis=1, keepdims=True) - ecum * kz + kgl
            dcum_all = jnp.where(lane1 == h, dcum, dcum_all)
            dbeta_all = jnp.where(lane1 == heads + h, dbeta, dbeta_all)
            dact[h] = (DK ** -0.5 * rq) * (dqn - qh * jnp.sum(dqn * qh, axis=1, keepdims=True))
            dact[heads + h] = rk * (dkn - kn * jnp.sum(dkn * kn, axis=1, keepdims=True))
            dact[2 * heads + h] = beta * dx
        tri = jnp.where(col_i >= row_i, 1.0, 0.0).astype(BF16)
        hi, lo = halves(dcum_all)
        dlog_decay = mm(tri, hi) + mm(tri, lo)
        dpre_a = dlog_decay * neg_rate * sigm(ab + bias)
        dpre_b = dbeta_all * beta_all * (1.0 - beta_all)
        dproj_ref[s, :, ab_at : ab_at + 128] = (dpre_a + dpre_b).astype(BF16)
        dots = dots + jnp.sum((dpre_a + dpre_b) * ab, axis=1, keepdims=True)
        drate_ref[0:8, :] += colsum(dlog_decay * log_decay)
        drate_ref[8:16, :] += colsum(dpre_a)
        dpre = jnp.concatenate(dact, axis=1) * dsilu
        ds_ref[s, 0:BLK, :] = dpre
        dx_in = ds_ref[s, 3 : 3 + BLK, :] * kernel[0:1]
        for i in range(1, CONV):
            dx_in = dx_in + ds_ref[s, 3 - i : 3 - i + BLK, :] * kernel[i : i + 1]
        dproj_ref[s, :, 0:qkv] = dx_in.astype(BF16)
        dots = dots + jnp.sum(dx_in * xs_ref[s, 8 : 8 + BLK, :], axis=1, keepdims=True)
        dots_ref[s, 0] = jnp.broadcast_to(dots, (BLK, 128)).T[0:8]
        for i in range(CONV):
            dconv_ref[8 * i : 8 * i + 8, :] += colsum(dpre * xs_ref[s, 5 + i : 5 + i + BLK, :])
        ds_ref[s, BLK : BLK + 8, :] = ds_ref[s, 0:8, :]


def mixer_bwd(proj, dmixed, saved, conv, rates, gain, heads, nseq):
    o, u, states, invs = saved
    seqs, length, width = proj.shape
    blocks = length // BLK
    qkv = heads * (2 * DK + DV)
    vals = heads * DV
    tok = lambda i, c: (i, blocks - 1 - c, 0)
    whole = lambda i, c: (0, 0)
    dproj, dots, dconv, drate, dgain = pl.pallas_call(
        functools.partial(bwd_kernel, heads, nseq),
        out_shape=(
            jax.ShapeDtypeStruct((seqs, length, width), BF16),
            jax.ShapeDtypeStruct((seqs, blocks, 8, 128), F32),
            jax.ShapeDtypeStruct((8 * CONV, qkv), F32),
            jax.ShapeDtypeStruct((16, 128), F32),
            jax.ShapeDtypeStruct((8, DV), F32),
        ),
        grid=(seqs // nseq, blocks),
        in_specs=[
            pl.BlockSpec((nseq, BLK, width), tok),
            pl.BlockSpec((nseq, 8, qkv), lambda i, c: (i, jnp.maximum((blocks - 1 - c) * (BLK // 8) - 1, 0), 0)),
            pl.BlockSpec((nseq, BLK, vals), tok),
            pl.BlockSpec((nseq, BLK, vals), tok),
            pl.BlockSpec((nseq, BLK, vals), tok),
            pl.BlockSpec((nseq, 1, heads, DK, DV), lambda i, c: (i, blocks - 1 - c, 0, 0, 0)),
            pl.BlockSpec((nseq, 1, heads, BLK, BLK), lambda i, c: (i, blocks - 1 - c, 0, 0, 0)),
            pl.BlockSpec((CONV, qkv), whole),
            pl.BlockSpec((2, 128), whole),
            pl.BlockSpec((1, DV), whole),
        ],
        out_specs=(
            pl.BlockSpec((nseq, BLK, width), tok),
            pl.BlockSpec((nseq, 1, 8, 128), lambda i, c: (i, blocks - 1 - c, 0, 0)),
            pl.BlockSpec((8 * CONV, qkv), whole),
            pl.BlockSpec((16, 128), whole),
            pl.BlockSpec((8, DV), whole),
        ),
        scratch_shapes=[
            pltpu.VMEM((nseq, 8 + BLK, qkv), F32),
            pltpu.VMEM((nseq, BLK + 8, qkv), F32),
            pltpu.VMEM((nseq, heads, DK, DV), F32),
        ],
        compiler_params=pltpu.CompilerParams(dimension_semantics=("arbitrary", "arbitrary")),
        cost_estimate=pl.CostEstimate(
            flops=seqs * length * heads * 10_000_000, bytes_accessed=seqs * length * width * 8,
            transcendentals=0),
        name="mixer_bwd",
    )(proj, proj, dmixed, o, u, states, invs, conv, rates, gain)
    dconv = jnp.sum(dconv.reshape(CONV, 8, qkv), axis=1)
    drate = jnp.sum(drate.reshape(2, 8, 128), axis=1)[:, :heads]
    dgain = jnp.sum(dgain, axis=0)
    return dproj, dots[:, :, 0, :], dconv, drate[0], drate[1], dgain


ROWS = 512


def piece_specs(blocks, width):
    half = blocks // 2
    here = pl.BlockSpec((ROWS, width), lambda i, *_: (i, 0))
    top = pl.BlockSpec((ROWS, width), lambda i, *_: (jnp.minimum(i, half - 1), 0))
    low = pl.BlockSpec((ROWS, width), lambda i, *_: (jnp.maximum(i - half, 0), 0))
    return [here, here, here, top, low]


def row_spec(width):
    return pl.BlockSpec((ROWS, width), lambda i, *_: (i, 0))


def whole_spec(shape):
    return pl.BlockSpec(shape, lambda i, *_: (0,) * len(shape))


def send_specs(tokens, width):
    shapes = (
        jax.ShapeDtypeStruct((tokens, width), F32),
        jax.ShapeDtypeStruct((3, tokens, width), BF16),
    )
    return shapes, (row_spec(width), pl.BlockSpec((3, ROWS, width), lambda i, *_: (0, i, 0)))


def block_cols(order_ref, b, width):
    return pl.ds(pl.multiple_of(order_ref[b] * width, width), width)


def read_pieces(refs, half):
    own_ref, x_ref, y_ref, top_ref, low_ref = refs
    far = jnp.where(pl.program_id(0) < half, top_ref[...], low_ref[...])
    return own_ref[...], x_ref[...], y_ref[...], far


def norm_into(refs, half, blocks_per_seq, lens_ref, order_ref, gain_ref, normed_ref, scale_ref):
    i = pl.program_id(0)
    pieces = [piece.astype(F32) for piece in read_pieces(refs, half)]
    width = pieces[0].shape[1]
    squares = pieces[0] * pieces[0]
    for piece in pieces[1:]:
        squares = squares + piece * piece
    scale = lax.rsqrt(jnp.sum(squares, axis=1, keepdims=True) * (1.0 / (4 * width)) + NORM_EPS)
    scale_ref[...] = scale
    at = lax.rem(i, blocks_per_seq) * ROWS + iota2((ROWS, 1), 0)
    masked = jnp.where(at < lens_ref[i // blocks_per_seq], scale, 0.0)
    for b, piece in enumerate(pieces):
        cols = block_cols(order_ref, b, width)
        normed_ref[:, cols] = (piece * masked * gain_ref[:, cols]).astype(BF16)


def send_blocks(order_ref, left, w_ref, cols, own_ref, send_ref):
    width = own_ref.shape[1]
    for b in range(4):
        part = mm_nt(left, w_ref[block_cols(order_ref, b, width), cols])
        if b == 0:
            own_ref[...] = part
        else:
            send_ref[b - 1] = part.astype(BF16)


def project_kernel(half, blocks_per_seq, lens_ref, order_ref, *refs):
    gain_ref, w_ref, proj_ref, normed_ref, scale_ref = refs[5:]
    norm_into(refs[:5], half, blocks_per_seq, lens_ref, order_ref, gain_ref, normed_ref, scale_ref)
    proj_ref[...] = mm(normed_ref[...], w_ref[...])


def norm_project(pieces, gain, weights, lens, order, length):
    tokens, width = pieces[0].shape
    blocks = tokens // ROWS
    full, out = weights.shape
    return pl.pallas_call(
        functools.partial(project_kernel, blocks // 2, length // ROWS),
        out_shape=(
            jax.ShapeDtypeStruct((tokens, out), F32),
            jax.ShapeDtypeStruct((tokens, full), BF16),
            jax.ShapeDtypeStruct((tokens, 1), F32),
        ),
        grid_spec=pltpu.PrefetchScalarGridSpec(
            num_scalar_prefetch=2,
            grid=(blocks,),
            in_specs=piece_specs(blocks, width) + [whole_spec((1, full)), whole_spec((full, out))],
            out_specs=(row_spec(out), row_spec(full), row_spec(1)),
        ),
        cost_estimate=pl.CostEstimate(
            flops=2 * tokens * full * out, bytes_accessed=tokens * (out * 4 + full * 4),
            transcendentals=tokens),
        name="norm_project",
    )(lens, order, *pieces, gain, weights)


def spread_kernel(order_ref, left_ref, w_ref, own_ref, send_ref):
    send_blocks(order_ref, left_ref[...], w_ref, slice(None), own_ref, send_ref)


def spread_product(left, weights, order):
    tokens, inner = left.shape
    full = weights.shape[0]
    shapes, specs = send_specs(tokens, full // 4)
    return pl.pallas_call(
        spread_kernel,
        out_shape=shapes,
        grid_spec=pltpu.PrefetchScalarGridSpec(
            num_scalar_prefetch=1,
            grid=(tokens // ROWS,),
            in_specs=[row_spec(inner), whole_spec((full, inner))],
            out_specs=specs,
        ),
        cost_estimate=pl.CostEstimate(
            flops=2 * tokens * full * inner, bytes_accessed=tokens * (full * 3 + inner * 2),
            transcendentals=0),
        name="spread_product",
    )(order, left, weights)


def feed_kernel(half, blocks_per_seq, lens_ref, order_ref, *refs):
    (grad_ref, gain_ref, w_ref, normed_ref, scale_ref, act_ref, both_ref, dots_ref,
     down_ref, down_send_ref, feed_ref, feed_send_ref) = refs[5:]
    ff = act_ref.shape[1]
    norm_into(refs[:5], half, blocks_per_seq, lens_ref, order_ref, gain_ref, normed_ref, scale_ref)
    gate_up = mm(normed_ref[...], w_ref[:, : 2 * ff])
    inner_grad = mm(grad_ref[...], w_ref[:, 2 * ff :])
    gate_act = gate_up[:, :ff]
    up_act = gate_up[:, ff:]
    sig = sigm(gate_act)
    silu = gate_act * sig
    act_ref[...] = (silu * up_act).astype(BF16)
    gate_grad = inner_grad * up_act * (sig * (1.0 + gate_act * (1.0 - sig)))
    up_grad = inner_grad * silu
    both_ref[:, :ff] = gate_grad.astype(BF16)
    both_ref[:, ff:] = up_grad.astype(BF16)
    dots = jnp.sum(gate_grad * gate_act + up_grad * up_act, axis=1, keepdims=True)
    dots_ref[0] = jnp.broadcast_to(dots, (ROWS, 128)).T[0:8]
    send_blocks(order_ref, both_ref[...], w_ref, slice(0, 2 * ff), down_ref, down_send_ref)
    send_blocks(order_ref, act_ref[...], w_ref, slice(2 * ff, 3 * ff), feed_ref, feed_send_ref)


def feed_forward(pieces, grad_full, gain, weights, lens, order, length):
    tokens, width = pieces[0].shape
    blocks = tokens // ROWS
    full, out = weights.shape
    ff = out // 3
    shapes, specs = send_specs(tokens, width)
    return pl.pallas_call(
        functools.partial(feed_kernel, blocks // 2, length // ROWS),
        out_shape=(
            jax.ShapeDtypeStruct((tokens, full), BF16),
            jax.ShapeDtypeStruct((tokens, 1), F32),
            jax.ShapeDtypeStruct((tokens, ff), BF16),
            jax.ShapeDtypeStruct((tokens, 2 * ff), BF16),
            jax.ShapeDtypeStruct((blocks, 8, ROWS), F32),
        ) + shapes + shapes,
        grid_spec=pltpu.PrefetchScalarGridSpec(
            num_scalar_prefetch=2,
            grid=(blocks,),
            in_specs=piece_specs(blocks, width)
            + [row_spec(full), whole_spec((1, full)), whole_spec((full, out))],
            out_specs=(row_spec(full), row_spec(1), row_spec(ff), row_spec(2 * ff),
                       pl.BlockSpec((1, 8, ROWS), lambda i, *_: (i, 0, 0))) + specs + specs,
        ),
        cost_estimate=pl.CostEstimate(
            flops=4 * tokens * full * out, bytes_accessed=tokens * full * 16,
            transcendentals=tokens * ff),
        name="feed_forward",
    )(lens, order, *pieces, grad_full, gain, weights)


def join_kernel(half, order_ref, *refs):
    w_ref, full_ref, out_ref = refs[5:]
    pieces = read_pieces(refs[:5], half)
    width = pieces[0].shape[1]
    for b, piece in enumerate(pieces):
        full_ref[:, block_cols(order_ref, b, width)] = piece
    out_ref[...] = mm(full_ref[...], w_ref[...])


def join_product(pieces, weights, order):
    tokens, width = pieces[0].shape
    blocks = tokens // ROWS
    full, out = weights.shape
    return pl.pallas_call(
        functools.partial(join_kernel, blocks // 2),
        out_shape=(
            jax.ShapeDtypeStruct((tokens, full), BF16),
            jax.ShapeDtypeStruct((tokens, out), F32),
        ),
        grid_spec=pltpu.PrefetchScalarGridSpec(
            num_scalar_prefetch=1,
            grid=(blocks,),
            in_specs=piece_specs(blocks, width) + [whole_spec((full, out))],
            out_specs=(row_spec(full), row_spec(out)),
        ),
        cost_estimate=pl.CostEstimate(
            flops=2 * tokens * full * out, bytes_accessed=tokens * (full * 4 + out * 4),
            transcendentals=0),
        name="join_product",
    )(order, *pieces, weights)


D = 1024
PARTS = 1


def contract_rows(left, right):
    return lax.dot_general(left, right, (((0,), (0,)), ((), ())), preferred_element_type=F32)


def after(value, *others):
    return lax.optimization_barrier((value,) + others)[0]


def xor_perm(size, bit):
    return [(i, i ^ bit) for i in range(size)]


def send_col(values, bit):
    return lax.ppermute(values, "col", xor_perm(4, bit))


def gather_features(values):
    half = values.shape[0] // 2
    from_x = send_col(values, 1)
    from_y = send_col(values, 2)
    far_top = send_col(from_y[:half], 1)
    far_low = send_col(from_x[half:], 2)
    return values, from_x, from_y, far_top, far_low


def sum_features(own, send, *earlier):
    half = own.shape[0] // 2
    via_x = send_col(send[2, :half], 1).astype(F32)
    via_y = send_col(send[2, half:], 2).astype(F32)
    if earlier:
        via_x = after(via_x, *earlier)
        via_y = after(via_y, *earlier)
    part_x = send[0].astype(F32)
    part_y = send[1].astype(F32)
    to_y = jnp.concatenate([part_y[:half] + via_x, part_y[half:]], axis=0).astype(BF16)
    to_x = jnp.concatenate([part_x[:half], part_x[half:] + via_y], axis=0).astype(BF16)
    return own + send_col(to_x, 1).astype(F32) + send_col(to_y, 2).astype(F32)


def sum_direct(own, send):
    total = own
    for bit in range(1, 4):
        total = total + send_col(send[bit - 1], bit).astype(F32)
    return total


def sum_scalars(values):
    values = values + send_col(values, 1)
    return values + send_col(values, 2)


def swap_cores(mine, dp):
    other = lax.ppermute(mine, "dp", [(0, 1), (1, 0)])
    return jnp.where(
        dp == 0, jnp.concatenate([mine, other], axis=0), jnp.concatenate([other, mine], axis=0)
    )


def gather_weight(block, dp, *earlier):
    rows = block.shape[0] // 2
    half = lax.dynamic_slice_in_dim(block, dp * rows, rows, 0)
    if earlier:
        half = after(half, *earlier)
    return lax.all_gather(half, ("row", "dp"), axis=0, tiled=True)


def scatter_weight(grad, dp):
    mine = lax.psum_scatter(grad, ("row", "dp"), scatter_dimension=0, tiled=True)
    return swap_cores(mine, dp).astype(F32)


def sum_small(values):
    count = lax.axis_size("row")
    if count != 4:
        return lax.psum(values, ("dp", "row"))
    size = values.shape[0]
    total = jnp.pad(values, (0, -size % 1024)).reshape(-1, 128)
    total = total + lax.ppermute(total, "dp", [(0, 1), (1, 0)])
    others = [lax.ppermute(total, "row", xor_perm(count, bit)) for bit in range(1, count)]
    return ((total + others[0]) + (others[1] + others[2])).reshape(-1)[:size]


def on_device(
    inputs,
    out_grad,
    seq_lengths,
    first_gain,
    query_proj,
    key_proj,
    value_proj,
    decay_proj,
    beta_proj,
    gate_proj,
    query_conv,
    key_conv,
    value_conv,
    decay_log,
    step_bias,
    output_gain,
    output_proj,
    second_gain,
    hidden_gate,
    hidden_up,
    hidden_down,
):
    seq_count, length, col_width = inputs.shape
    heads = decay_log.shape[0]
    parts = PARTS
    per_part = seq_count // parts
    tokens = per_part * length
    col = lax.axis_index("col")
    dp = lax.axis_index("dp")
    order = (col ^ jnp.arange(4, dtype=jnp.int32)).astype(jnp.int32)
    row_block = query_proj.shape[0]
    vals = heads * DV
    qkv = heads * (2 * DK + DV)
    ff = hidden_gate.shape[1]
    ff_pad = -ff % 128

    in_block = jnp.concatenate(
        [query_proj, key_proj, value_proj, gate_proj, decay_proj, beta_proj,
         jnp.zeros((row_block, 128 - 2 * heads), BF16)], axis=1)
    in_weights = gather_weight(in_block, dp)
    positions = lax.broadcasted_iota(jnp.int32, (seq_count, length), 1)
    valid_all = (positions < seq_lengths[:, None]).astype(F32)
    grad_all = out_grad.astype(F32) * valid_all[:, :, None]
    ff_block = jnp.concatenate(
        [jnp.pad(piece, ((0, 0), (0, ff_pad)))
         for piece in (hidden_gate, hidden_up, hidden_down.T)], axis=1)

    conv = jnp.concatenate([query_conv, key_conv, value_conv], axis=1).astype(F32)
    rates = rate_rows(decay_log, step_bias)
    gain_row = output_gain.astype(F32)[None]
    first_row = first_gain.astype(F32)[None]
    second_row = second_gain.astype(F32)[None]
    first_local = lax.dynamic_slice_in_dim(first_row, col * col_width, col_width, 1)
    second_local = lax.dynamic_slice_in_dim(second_row, col * col_width, col_width, 1)

    state = []
    for part in range(parts):
        seqs = slice(part * per_part, (part + 1) * per_part)
        local = inputs[seqs].reshape(tokens, col_width)
        state.append(dict(
            lens=seq_lengths[seqs], valid=valid_all[seqs].reshape(tokens, 1), local=local,
            grad_out=grad_all[seqs].reshape(tokens, col_width), pieces=gather_features(local)))
    out_weights = gather_weight(output_proj.T, dp, state[0]["pieces"][1])
    for st in state:
        proj, st["normed"], st["scale"] = norm_project(
            st["pieces"], first_row, in_weights, st["lens"], order, length)
        st["proj"] = proj.reshape(per_part, length, -1)
        if st is state[0]:
            grad_low = grad_all.astype(BF16).reshape(seq_count * length, col_width)
            grad_full = lax.all_gather(after(grad_low, st["scale"]), "col", axis=1, tiled=True)
            ff_weights = gather_weight(ff_block, dp, st["scale"])
        mixed, *st["saved"] = mixer_fwd(st["proj"], conv, rates, gain_row, heads, per_part)
        st["mixed"] = mixed.reshape(tokens, vals)
        attention = sum_features(*spread_product(st["mixed"], out_weights, order))
        st["hidden"] = st["local"].astype(F32) + attention
        st["pieces"] = gather_features(st["hidden"].astype(BF16))
    results = []
    gate_up_grad = 0.0
    down_grad = 0.0
    second_gain_grad = 0.0
    for part, st in enumerate(state):
        st["grad_full"] = grad_full[part * tokens : (part + 1) * tokens]
        (normed, scale, act, both, dots, second_own, second_send, feed_own, feed_send
         ) = feed_forward(st["pieces"], st["grad_full"], second_row, ff_weights, st["lens"], order,
                          length)
        dots = sum_scalars(dots)[:, 0, :].reshape(tokens, 1)
        second_grad = sum_features(second_own, second_send, dots) * st["valid"]
        hat = st["hidden"] * scale
        second_gain_grad = second_gain_grad + jnp.sum(second_grad * hat, axis=0)
        st["hidden_grad"] = st["grad_out"] + scale * (
            second_grad * second_local - hat * (dots * (1.0 / D)))
        st["pieces"] = gather_features(st["hidden_grad"].astype(BF16))
        hidden, feed_own, feed_send = lax.optimization_barrier(
            (st["hidden"], feed_own, feed_send, st["pieces"][4]))[:3]
        feed = sum_direct(feed_own, feed_send)
        results.append(((hidden + feed) * st["valid"]).astype(BF16))
        gate_up_grad = gate_up_grad + contract_rows(normed, both)
        down_grad = down_grad + contract_rows(st["grad_full"], act)
    gate_up_low = gate_up_grad.astype(BF16)
    down_low = down_grad.astype(BF16)
    gate_up_grad = scatter_weight(gate_up_low, dp)
    down_grad = scatter_weight(after(down_low, gate_up_low), dp)
    out_weight_grad = 0.0
    in_weight_grad = 0.0
    first_gain_grad = 0.0
    small = 0.0
    for st in state:
        own = after(st["pieces"][0], gate_up_low, down_low)
        st["attn_grad"], mixed_grad = join_product(
            (own,) + st["pieces"][1:], out_weights, order)
        out_weight_grad = out_weight_grad + contract_rows(st["attn_grad"], st["mixed"])
        if st is state[-1]:
            out_low = out_weight_grad.astype(BF16)
            mixed_grad = after(mixed_grad, out_low)
        dproj, dots, *grads = mixer_bwd(
            st["proj"], mixed_grad.reshape(per_part, length, vals), st["saved"], conv, rates,
            gain_row, heads, per_part)
        small = small + jnp.concatenate([grad.reshape(-1) for grad in grads])
        st["dproj"] = dproj.reshape(tokens, -1)
        st["dots"] = sum_scalars(dots)
        in_weight_grad = in_weight_grad + contract_rows(
            st["normed"], after(st["dproj"], *results))
    in_low = in_weight_grad.astype(BF16)
    in_weight_grad = scatter_weight(after(in_low, out_low), dp)
    at = CONV * qkv + 2 * heads
    gain_out = sum_scalars(small[at:].reshape(2, 128)).reshape(-1)
    small_sums = sum_small(jnp.concatenate([small[:at], second_gain_grad, gain_out]))
    input_grads = []
    for st in state:
        own, send = spread_product(after(st["dproj"], in_low, st["dots"]), in_weights, order)
        first_grad = sum_features(own, send, small_sums) * st["valid"]
        hat = st["local"].astype(F32) * st["scale"]
        first_gain_grad = first_gain_grad + jnp.sum(first_grad * hat, axis=0)
        input_grads.append(st["hidden_grad"] + st["scale"] * (
            first_grad * first_local - hat * (st["dots"].reshape(tokens, 1) * (1.0 / D))))
    out_weight_grad = scatter_weight(out_low, dp)
    first_gain_grad = sum_small(first_gain_grad)
    conv_grad = small_sums[: CONV * qkv].reshape(CONV, qkv)
    gate_at = qkv + vals
    qk = heads * DK
    return (
        jnp.concatenate(results, axis=0).reshape(seq_count, length, col_width),
        jnp.concatenate(input_grads, axis=0).reshape(seq_count, length, col_width),
        first_gain_grad,
        in_weight_grad[:, :qk],
        in_weight_grad[:, qk : 2 * qk],
        in_weight_grad[:, 2 * qk : qkv],
        in_weight_grad[:, gate_at : gate_at + heads],
        in_weight_grad[:, gate_at + heads : gate_at + 2 * heads],
        in_weight_grad[:, qkv:gate_at],
        conv_grad[:, :qk],
        conv_grad[:, qk : 2 * qk],
        conv_grad[:, 2 * qk :],
        small_sums[CONV * qkv : CONV * qkv + heads],
        small_sums[CONV * qkv + heads : at],
        small_sums[at + col_width :],
        out_weight_grad.T,
        small_sums[at : at + col_width],
        gate_up_grad[:, :ff],
        gate_up_grad[:, ff + ff_pad : 2 * ff + ff_pad],
        down_grad[:, :ff].T,
    )


def solution(mesh):
    in_specs = (
        P(("dp", "row"), None, "col"),
        P(("dp", "row"), None, "col"),
        P(("dp", "row")),
        P(),
        P("row", "col"),
        P("row", "col"),
        P("row", "col"),
        P("row", "col"),
        P("row", "col"),
        P("row", "col"),
        P(None, "col"),
        P(None, "col"),
        P(None, "col"),
        P("col"),
        P("col"),
        P(),
        P("col", "row"),
        P(),
        P("row", "col"),
        P("row", "col"),
        P("col", "row"),
    )
    out_specs = (
        P(("dp", "row"), None, "col"),
        P(("dp", "row"), None, "col"),
        P("col"),
        P("row", "col"),
        P("row", "col"),
        P("row", "col"),
        P("row", "col"),
        P("row", "col"),
        P("row", "col"),
        P(None, "col"),
        P(None, "col"),
        P(None, "col"),
        P("col"),
        P("col"),
        P(),
        P("col", "row"),
        P("col"),
        P("row", "col"),
        P("row", "col"),
        P("col", "row"),
    )
    return jax.shard_map(
        on_device, mesh=mesh, in_specs=in_specs, out_specs=out_specs, check_vma=False
    )
```

```python
import functools
import jax
import jax.numpy as jnp
from jax import lax
from jax.experimental import pallas as pl
from jax.experimental.pallas import tpu as pltpu
from jax.sharding import PartitionSpec as P

DK = 128
DV = 256
CONV = 4
NORM_EPS = 1e-05
UNIT_EPS = 1e-06
BLK = 128
SUB = 32
F32 = jnp.float32
BF16 = jnp.bfloat16


def mm1(a, b):
    return lax.dot_general(a, b, (((1,), (0,)), ((), ())), preferred_element_type=F32)


def nt1(a, b):
    return lax.dot_general(a, b, (((1,), (1,)), ((), ())), preferred_element_type=F32)


def halves(a):
    hi = a.astype(BF16)
    return hi, (a - hi.astype(F32)).astype(BF16)


def mm(a, b):
    ah, al = halves(a)
    bh, bl = halves(b)
    return mm1(jnp.concatenate([ah, al, ah], axis=1), jnp.concatenate([bh, bh, bl], axis=0))


def mm_nt(a, b):
    ah, al = halves(a)
    bh, bl = halves(b)
    return nt1(jnp.concatenate([ah, al, ah], axis=1), jnp.concatenate([bh, bh, bl], axis=1))


def mm_sum(a, b):
    ah, al = halves(a)
    bh, bl = halves(b)
    return mm1(ah, bh) + (mm1(ah, bl) + mm1(al, bh))


def mm_nt_sum(a, b):
    ah, al = halves(a)
    bh, bl = halves(b)
    return nt1(ah, bh) + (nt1(ah, bl) + nt1(al, bh))


def sigm(v):
    return 0.5 * jnp.tanh(0.5 * v) + 0.5


def iota2(shape, axis):
    return lax.broadcasted_iota(jnp.int32, shape, axis)


def unit_lower_inverse(mats):
    groups = BLK // SUB
    lane = iota2((SUB, BLK), 1)
    sub = iota2((SUB, BLK), 0)
    lane_group = lane // SUB
    solved = []
    for b in range(groups):
        rows = slice(b * SUB, (b + 1) * SUB)
        packed = jnp.zeros((SUB, BLK), F32)
        for p, mat in enumerate(mats):
            piece = mat[rows]
            shift = (SUB * (p - b)) % BLK
            if shift:
                piece = pltpu.roll(piece, shift, 1)
            packed = jnp.where(lane_group == p, piece, packed)
        acc = jnp.where(lane - lane_group * SUB == sub, 1.0, 0.0).astype(F32)
        tiles = [acc[8 * t : 8 * t + 8] for t in range(SUB // 8)]
        coefs = [packed[8 * t : 8 * t + 8] for t in range(SUB // 8)]
        base = (iota2((8, BLK), 1) // SUB) * SUB
        for j in range(SUB - 1):
            row = jnp.broadcast_to(tiles[j // 8][j % 8 : j % 8 + 1], (8, BLK))
            for t in range((j + 1) // 8, SUB // 8):
                col = jnp.take_along_axis(coefs[t], base + j, axis=1)
                tiles[t] = tiles[t] - col * row
        solved.append(jnp.concatenate(tiles, axis=0))
    out = []
    row_i = iota2((BLK, BLK), 0)
    col_i = iota2((BLK, BLK), 1)
    for p, mat in enumerate(mats):
        blocks = []
        for b in range(groups):
            piece = solved[b]
            shift = (SUB * (b - p)) % BLK
            if shift:
                piece = pltpu.roll(piece, shift, 1)
            blocks.append(jnp.where(lane_group == b, piece, 0.0))
        inv = jnp.concatenate(blocks, axis=0)
        zero32 = jnp.zeros((SUB, BLK), F32)
        off = jnp.where((row_i // 64 == col_i // 64) & (row_i // SUB > col_i // SUB), mat, 0.0)
        lhs = jnp.concatenate([off[32:64], off[96:128]], axis=0)
        part = mm(lhs, inv)
        placed = jnp.concatenate([zero32, part[:32], zero32, part[32:]], axis=0)
        lhs = jnp.concatenate([inv[32:64], inv[96:128]], axis=0)
        part = mm(lhs, placed)
        inv = inv - jnp.concatenate([zero32, part[:32], zero32, part[32:]], axis=0)
        off = jnp.where(col_i[64:] < 64, mat[64:], 0.0)
        part = mm(off, inv)
        zero64 = jnp.zeros((64, BLK), F32)
        part = mm(inv[64:], jnp.concatenate([zero64, part], axis=0))
        inv = jnp.concatenate([inv[:64], inv[64:] - part], axis=0)
        out.append(inv)
    return out


def decay_terms(ab, neg_rate, bias, heads):
    pre = ab + bias
    soft = jnp.maximum(pre, 0.0) + jnp.log(1.0 + jnp.exp(-jnp.abs(pre)))
    log_decay = neg_rate * soft
    beta = sigm(ab)
    row_i = iota2((BLK, BLK), 0)
    col_i = iota2((BLK, BLK), 1)
    tri = jnp.where(row_i >= col_i, 1.0, 0.0).astype(BF16)
    hi = log_decay.astype(BF16)
    rest = log_decay - hi.astype(F32)
    mid = rest.astype(BF16)
    low = (rest - mid.astype(F32)).astype(BF16)
    cum = mm1(tri, hi) + (mm1(tri, mid) + mm1(tri, low))
    return log_decay, beta, cum


def conv_taps(xs_ref, s, kernel):
    pre = xs_ref[s, 5 : 5 + BLK, :] * kernel[0:1]
    for i in range(1, CONV):
        pre = pre + xs_ref[s, 5 + i : 5 + i + BLK, :] * kernel[i : i + 1]
    return pre


def fwd_kernel(heads, nseq, proj_ref, conv_ref, rate_ref, gain_ref,
               mixed_ref, o_ref, u_ref, s_ref, t_ref, xs_ref, state_ref):
    qkv = heads * (2 * DK + DV)
    gate_at = qkv
    ab_at = qkv + heads * DV
    step = pl.program_id(1)

    @pl.when(step == 0)
    def _():
        xs_ref[:, 0:8, :] = jnp.zeros((nseq, 8, qkv), F32)
        state_ref[...] = jnp.zeros_like(state_ref)

    row_i = iota2((BLK, BLK), 0)
    col_i = iota2((BLK, BLK), 1)
    kernel = conv_ref[...]
    neg_rate = rate_ref[0:1]
    bias = rate_ref[1:2]
    gain = gain_ref[...]
    items = []
    for s in range(nseq):
        xs_ref[s, 8 : 8 + BLK, :] = proj_ref[s, :, 0:qkv]
        pre = conv_taps(xs_ref, s, kernel)
        xs_ref[s, 0:8, :] = xs_ref[s, BLK : BLK + 8, :]
        act = pre * sigm(pre)
        ab = proj_ref[s, :, ab_at : ab_at + 128]
        _, beta_all, cum_all = decay_terms(ab, neg_rate, bias, heads)
        cum_t = cum_all.T
        for h in range(heads):
            q = act[:, h * DK : (h + 1) * DK]
            k = act[:, (heads + h) * DK : (heads + h + 1) * DK]
            v = act[:, 2 * heads * DK + h * DV : 2 * heads * DK + (h + 1) * DV]
            qn = q * (lax.rsqrt(jnp.sum(q * q, axis=1, keepdims=True) + UNIT_EPS) * DK ** -0.5)
            kn = k * lax.rsqrt(jnp.sum(k * k, axis=1, keepdims=True) + UNIT_EPS)
            cum = cum_all[:, h : h + 1]
            cum_row = cum_t[h : h + 1, :]
            beta = beta_all[:, heads + h : heads + h + 1]
            ratio = jnp.exp(jnp.where(row_i >= col_i, cum - cum_row, -1e30))
            kb = kn
            kq = jnp.concatenate([kb, qn], axis=0)
            gram = mm_nt(kq, kb)
            a = jnp.where(row_i > col_i, gram[:BLK] * ratio * beta, 0.0)
            p = gram[BLK:] * ratio
            last = cum[BLK - 1 : BLK]
            kd = kn * jnp.exp(last - cum)
            items.append((s, h, kq, a, p, kd, v, beta, jnp.exp(cum), jnp.exp(last)))
    invs = []
    for at in range(0, len(items), 4):
        invs = invs + unit_lower_inverse([item[3] for item in items[at : at + 4]])
    for item, inv in zip(items, invs):
        s, h, kq, a, p, kd, v, beta, ecum, elast = item
        state = state_ref[s, h]
        low_state = state
        ks_qs = mm(kq, low_state)
        x = beta * (v - ecum * ks_qs[:BLK])
        inv_low = inv
        u = mm(inv_low, x)
        pk = jnp.concatenate([p, kd.T], axis=0)
        pu = mm(pk, u)
        o = ecum * ks_qs[BLK:] + pu[:BLK]
        state_ref[s, h] = elast * state + pu[BLK:]
        s_ref[s, 0, h] = low_state
        t_ref[s, 0, h] = inv_low
        cols = slice(h * DV, (h + 1) * DV)
        u_ref[s, :, cols] = u
        o_ref[s, :, cols] = o
        g = proj_ref[s, :, gate_at + h * DV : gate_at + (h + 1) * DV]
        norm = o * lax.rsqrt(jnp.mean(o * o, axis=1, keepdims=True) + NORM_EPS)
        mixed_ref[s, :, cols] = (norm * gain * (g * sigm(g))).astype(BF16)


def rate_rows(decay_log, step_bias):
    heads = decay_log.shape[0]
    pad = 128 - heads
    return jnp.stack([jnp.pad(-jnp.exp(decay_log), (0, pad)), jnp.pad(step_bias, (0, pad))])


def mixer_fwd(proj, conv, rates, gain, heads, nseq):
    seqs, length, width = proj.shape
    blocks = length // BLK
    qkv = heads * (2 * DK + DV)
    vals = heads * DV
    tok = lambda i, c: (i, c, 0)
    return pl.pallas_call(
        functools.partial(fwd_kernel, heads, nseq),
        out_shape=(
            jax.ShapeDtypeStruct((seqs, length, vals), BF16),
            jax.ShapeDtypeStruct((seqs, length, vals), F32),
            jax.ShapeDtypeStruct((seqs, length, vals), F32),
            jax.ShapeDtypeStruct((seqs, blocks, heads, DK, DV), F32),
            jax.ShapeDtypeStruct((seqs, blocks, heads, BLK, BLK), F32),
        ),
        grid=(seqs // nseq, blocks),
        in_specs=[
            pl.BlockSpec((nseq, BLK, width), tok),
            pl.BlockSpec((CONV, qkv), lambda i, c: (0, 0)),
            pl.BlockSpec((2, 128), lambda i, c: (0, 0)),
            pl.BlockSpec((1, DV), lambda i, c: (0, 0)),
        ],
        out_specs=(
            pl.BlockSpec((nseq, BLK, vals), tok),
            pl.BlockSpec((nseq, BLK, vals), tok),
            pl.BlockSpec((nseq, BLK, vals), tok),
            pl.BlockSpec((nseq, 1, heads, DK, DV), lambda i, c: (i, c, 0, 0, 0)),
            pl.BlockSpec((nseq, 1, heads, BLK, BLK), lambda i, c: (i, c, 0, 0, 0)),
        ),
        scratch_shapes=[
            pltpu.VMEM((nseq, 8 + BLK, qkv), F32),
            pltpu.VMEM((nseq, heads, DK, DV), F32),
        ],
        compiler_params=pltpu.CompilerParams(dimension_semantics=("arbitrary", "arbitrary")),
        cost_estimate=pl.CostEstimate(
            flops=seqs * length * heads * 6_000_000, bytes_accessed=seqs * length * width * 8,
            transcendentals=0),
        name="mixer_fwd",
    )(proj, conv, rates, gain)


def colsum(v):
    return jnp.sum(v.reshape(v.shape[0] // 8, 8, v.shape[1]), axis=0)


def bwd_kernel(heads, nseq, proj_ref, prev_ref, dmix_ref, o_ref, u_ref, s_ref, t_ref,
               conv_ref, rate_ref, gain_ref,
               dproj_ref, dots_ref, dconv_ref, drate_ref, dgain_ref, xs_ref, ds_ref, dstate_ref):
    qkv = heads * (2 * DK + DV)
    gate_at = qkv
    ab_at = qkv + heads * DV
    step = pl.program_id(1)
    first = pl.num_programs(1) - 1

    @pl.when(step == 0)
    def _():
        ds_ref[:, BLK : BLK + 8, :] = jnp.zeros((nseq, 8, qkv), F32)
        dstate_ref[...] = jnp.zeros_like(dstate_ref)

    @pl.when((step == 0) & (pl.program_id(0) == 0))
    def _():
        dconv_ref[...] = jnp.zeros_like(dconv_ref)
        drate_ref[...] = jnp.zeros_like(drate_ref)
        dgain_ref[...] = jnp.zeros_like(dgain_ref)

    row_i = iota2((BLK, BLK), 0)
    col_i = iota2((BLK, BLK), 1)
    lower = row_i >= col_i
    strict = row_i > col_i
    kernel = conv_ref[...]
    neg_rate = rate_ref[0:1]
    bias = rate_ref[1:2]
    gain = gain_ref[...]
    has_prev = jnp.where(step == first, 0.0, 1.0).astype(F32)
    lane1 = iota2((1, 128), 1)
    for s in range(nseq):
        xs_ref[s, 0:8, :] = prev_ref[s, :, 0:qkv] * has_prev
        xs_ref[s, 8 : 8 + BLK, :] = proj_ref[s, :, 0:qkv]
        pre = conv_taps(xs_ref, s, kernel)
        sig = sigm(pre)
        act = pre * sig
        dsilu = sig * (1.0 + pre * (1.0 - sig))
        ab = proj_ref[s, :, ab_at : ab_at + 128]
        log_decay, beta_all, cum_all = decay_terms(ab, neg_rate, bias, heads)
        cum_t = cum_all.T
        dots = jnp.zeros((BLK, 1), F32)
        dcum_all = jnp.zeros((BLK, 128), F32)
        dbeta_all = jnp.zeros((BLK, 128), F32)
        dact = [None] * (3 * heads)
        for h in range(heads):
            q = act[:, h * DK : (h + 1) * DK]
            k = act[:, (heads + h) * DK : (heads + h + 1) * DK]
            v = act[:, 2 * heads * DK + h * DV : 2 * heads * DK + (h + 1) * DV]
            rq = lax.rsqrt(jnp.sum(q * q, axis=1, keepdims=True) + UNIT_EPS)
            rk = lax.rsqrt(jnp.sum(k * k, axis=1, keepdims=True) + UNIT_EPS)
            qh = q * rq
            qn = qh * DK ** -0.5
            kn = k * rk
            cum = cum_all[:, h : h + 1]
            cum_row = cum_t[h : h + 1, :]
            beta = beta_all[:, heads + h : heads + h + 1]
            ecum = jnp.exp(cum)
            last = cum[BLK - 1 : BLK]
            elast = jnp.exp(last)
            ratio = jnp.exp(jnp.where(lower, cum - cum_row, -1e30))
            ktail = jnp.exp(last - cum)
            kb = kn
            qb = qn
            gram = mm_nt_sum(jnp.concatenate([kb, qb], axis=0), kb)
            sfac = jnp.where(strict, ratio * beta, 0.0)
            kgr = gram[:BLK]
            p = gram[BLK:] * ratio
            cols = slice(h * DV, (h + 1) * DV)
            o = o_ref[s, :, cols]
            g = proj_ref[s, :, gate_at + h * DV : gate_at + (h + 1) * DV]
            dm = dmix_ref[s, :, cols].astype(F32)
            ro = lax.rsqrt(jnp.mean(o * o, axis=1, keepdims=True) + NORM_EPS)
            n = o * ro
            gs = sigm(g)
            gsil = g * gs
            dmn = dm * n
            dgain_ref[...] += colsum(dmn * gsil)
            dgate = dmn * gain * (gs * (1.0 + g * (1.0 - gs)))
            dproj_ref[s, :, gate_at + h * DV : gate_at + (h + 1) * DV] = dgate.astype(BF16)
            dots = dots + jnp.sum(dgate * g, axis=1, keepdims=True)
            dn = dm * gain * gsil
            do = ro * (dn - n * jnp.mean(dn * n, axis=1, keepdims=True))
            dob = do
            dstate = dstate_ref[s, h]
            dstb = dstate
            u = u_ref[s, :, cols]
            sb = s_ref[s, 0, h]
            tinv = t_ref[s, 0, h]
            kd = kn * ktail
            du = mm_sum(jnp.concatenate([p.T, kd], axis=1), jnp.concatenate([dob, dstb], axis=0))
            dx = mm_sum(tinv.astype(F32).T, du)
            dxb = dx
            ddx = jnp.concatenate([dob, dxb], axis=0)
            both = mm_nt_sum(ddx, jnp.concatenate([sb, u], axis=0))
            be = beta * ecum
            z = both[BLK:, :DK]
            dqi = ecum * both[:BLK, :DK]
            dki = -be * z
            dks = -be * dx
            lhs = jnp.concatenate([qn.T, kn.T], axis=1)
            rhs = jnp.concatenate([(ecum * do), dks], axis=0)
            dstate_ref[s, h] = elast * dstate + mm_sum(lhs, rhs)
            dkd = mm_nt_sum(u, dstb)
            dp = both[:BLK, DK:]
            da = -both[BLK:, DK:]
            dqk = dp * ratio
            dkg = da * sfac
            dlog = dp * p + dkg * kgr
            pair = jnp.concatenate([dqk, dkg + dkg.T], axis=0)
            prod = mm_sum(pair, kb)
            dqn = dqi + prod[:BLK]
            dkn = dki + prod[BLK:] + mm_sum(dqk.T, qb) + dkd * ktail
            kz = jnp.sum(kn * z, axis=1, keepdims=True)
            dkdk = jnp.sum(dkd * kd, axis=1, keepdims=True)
            row_sum = jnp.sum(dlog, axis=1, keepdims=True)
            col_sum = jnp.sum(dlog.T, axis=1, keepdims=True)
            dcum = row_sum - col_sum + jnp.sum(qn * dqi, axis=1, keepdims=True) - be * kz - dkdk
            tail = jnp.sum(dkdk, axis=0, keepdims=True) + elast * jnp.sum(
                jnp.sum(sb.astype(F32) * dstate, axis=1, keepdims=True), axis=0, keepdims=True)
            dcum = dcum + jnp.where(row_i[:, 0:1] == BLK - 1, tail, 0.0)
            kgl = jnp.sum(da * jnp.where(strict, ratio * kgr, 0.0), axis=1, keepdims=True)
            dbeta = jnp.sum(dx * v, axis=1, keepdims=True) - ecum * kz + kgl
            dcum_all = jnp.where(lane1 == h, dcum, dcum_all)
            dbeta_all = jnp.where(lane1 == heads + h, dbeta, dbeta_all)
            dact[h] = (DK ** -0.5 * rq) * (dqn - qh * jnp.sum(dqn * qh, axis=1, keepdims=True))
            dact[heads + h] = rk * (dkn - kn * jnp.sum(dkn * kn, axis=1, keepdims=True))
            dact[2 * heads + h] = beta * dx
        tri = jnp.where(col_i >= row_i, 1.0, 0.0).astype(BF16)
        hi, lo = halves(dcum_all)
        dlog_decay = mm1(tri, hi) + mm1(tri, lo)
        dpre_a = dlog_decay * neg_rate * sigm(ab + bias)
        dpre_b = dbeta_all * beta_all * (1.0 - beta_all)
        dproj_ref[s, :, ab_at : ab_at + 128] = (dpre_a + dpre_b).astype(BF16)
        dots = dots + jnp.sum((dpre_a + dpre_b) * ab, axis=1, keepdims=True)
        drate_ref[0:8, :] += colsum(dlog_decay * log_decay)
        drate_ref[8:16, :] += colsum(dpre_a)
        dpre = jnp.concatenate(dact, axis=1) * dsilu
        ds_ref[s, 0:BLK, :] = dpre
        dx_in = ds_ref[s, 3 : 3 + BLK, :] * kernel[0:1]
        for i in range(1, CONV):
            dx_in = dx_in + ds_ref[s, 3 - i : 3 - i + BLK, :] * kernel[i : i + 1]
        dproj_ref[s, :, 0:qkv] = dx_in.astype(BF16)
        dots = dots + jnp.sum(dx_in * xs_ref[s, 8 : 8 + BLK, :], axis=1, keepdims=True)
        dots_ref[s, 0] = jnp.broadcast_to(dots, (BLK, 128)).T[0:8]
        for i in range(CONV):
            dconv_ref[8 * i : 8 * i + 8, :] += colsum(dpre * xs_ref[s, 5 + i : 5 + i + BLK, :])
        ds_ref[s, BLK : BLK + 8, :] = ds_ref[s, 0:8, :]


def mixer_bwd(proj, dmixed, saved, conv, rates, gain, heads, nseq, seq):
    o, u, states, invs = saved
    _, length, width = proj.shape
    seqs = dmixed.shape[0]
    first = seq // nseq
    blocks = length // BLK
    qkv = heads * (2 * DK + DV)
    vals = heads * DV
    tok = lambda i, c: (i, blocks - 1 - c, 0)
    all_tok = lambda i, c: (i + first, blocks - 1 - c, 0)
    all_blk = lambda i, c: (i + first, blocks - 1 - c, 0, 0, 0)
    whole = lambda i, c: (0, 0)
    dproj, dots, dconv, drate, dgain = pl.pallas_call(
        functools.partial(bwd_kernel, heads, nseq),
        out_shape=(
            jax.ShapeDtypeStruct((seqs, length, width), BF16),
            jax.ShapeDtypeStruct((seqs, blocks, 8, 128), F32),
            jax.ShapeDtypeStruct((8 * CONV, qkv), F32),
            jax.ShapeDtypeStruct((16, 128), F32),
            jax.ShapeDtypeStruct((8, DV), F32),
        ),
        grid=(seqs // nseq, blocks),
        in_specs=[
            pl.BlockSpec((nseq, BLK, width), all_tok),
            pl.BlockSpec((nseq, 8, qkv), lambda i, c: (
                i + first, jnp.maximum((blocks - 1 - c) * (BLK // 8) - 1, 0), 0)),
            pl.BlockSpec((nseq, BLK, vals), tok),
            pl.BlockSpec((nseq, BLK, vals), all_tok),
            pl.BlockSpec((nseq, BLK, vals), all_tok),
            pl.BlockSpec((nseq, 1, heads, DK, DV), all_blk),
            pl.BlockSpec((nseq, 1, heads, BLK, BLK), all_blk),
            pl.BlockSpec((CONV, qkv), whole),
            pl.BlockSpec((2, 128), whole),
            pl.BlockSpec((1, DV), whole),
        ],
        out_specs=(
            pl.BlockSpec((nseq, BLK, width), tok),
            pl.BlockSpec((nseq, 1, 8, 128), lambda i, c: (i, blocks - 1 - c, 0, 0)),
            pl.BlockSpec((8 * CONV, qkv), whole),
            pl.BlockSpec((16, 128), whole),
            pl.BlockSpec((8, DV), whole),
        ),
        scratch_shapes=[
            pltpu.VMEM((nseq, 8 + BLK, qkv), F32),
            pltpu.VMEM((nseq, BLK + 8, qkv), F32),
            pltpu.VMEM((nseq, heads, DK, DV), F32),
        ],
        compiler_params=pltpu.CompilerParams(dimension_semantics=("arbitrary", "arbitrary")),
        cost_estimate=pl.CostEstimate(
            flops=seqs * length * heads * 10_000_000, bytes_accessed=seqs * length * width * 8,
            transcendentals=0),
        name="mixer_bwd",
    )(proj, proj, dmixed, o, u, states, invs, conv, rates, gain)
    dconv = jnp.sum(dconv.reshape(CONV, 8, qkv), axis=1)
    drate = jnp.sum(drate.reshape(2, 8, 128), axis=1)[:, :heads]
    dgain = jnp.sum(dgain, axis=0)
    return dproj, dots[:, :, 0, :], dconv, drate[0], drate[1], dgain


ROWS = 512


def half_specs(blocks, width):
    half = blocks // 2
    top = pl.BlockSpec((ROWS, width), lambda i, *_: (jnp.minimum(i, half - 1), 0))
    low = pl.BlockSpec((ROWS, width), lambda i, *_: (jnp.maximum(i - half, 0), 0))
    return [top, low]


def piece_specs(blocks, width, count):
    here = [pl.BlockSpec((ROWS, width), lambda i, *_: (i, 0))]
    if count == 5:
        return here * 3 + half_specs(blocks, width)
    return here + half_specs(blocks, width) * 3


def row_spec(width):
    return pl.BlockSpec((ROWS, width), lambda i, *_: (i, 0))


def whole_spec(shape):
    return pl.BlockSpec(shape, lambda i, *_: (0,) * len(shape))


def send_specs(tokens, width):
    shapes = (
        jax.ShapeDtypeStruct((tokens, width), F32),
        jax.ShapeDtypeStruct((3, tokens, width), BF16),
    )
    return shapes, (row_spec(width), pl.BlockSpec((3, ROWS, width), lambda i, *_: (0, i, 0)))


def block_cols(order_ref, b, width):
    return pl.ds(pl.multiple_of(order_ref[b] * width, width), width)


def read_pieces(refs, half):
    upper = pl.program_id(0) < half
    first = 3 if len(refs) == 5 else 1
    halves = [jnp.where(upper, refs[i][...], refs[i + 1][...]) for i in range(first, len(refs), 2)]
    return [ref[...] for ref in refs[:first]] + halves


def norm_into(refs, half, blocks_per_seq, lens_ref, order_ref, gain_ref, normed_ref, scale_ref):
    i = pl.program_id(0)
    pieces = [piece.astype(F32) for piece in read_pieces(refs, half)]
    width = pieces[0].shape[1]
    squares = pieces[0] * pieces[0]
    for piece in pieces[1:]:
        squares = squares + piece * piece
    scale = lax.rsqrt(jnp.sum(squares, axis=1, keepdims=True) * (1.0 / (4 * width)) + NORM_EPS)
    scale_ref[...] = scale
    at = lax.rem(i, blocks_per_seq) * ROWS + iota2((ROWS, 1), 0)
    masked = jnp.where(at < lens_ref[i // blocks_per_seq], scale, 0.0)
    for b, piece in enumerate(pieces):
        cols = block_cols(order_ref, b, width)
        normed_ref[:, cols] = (piece * masked * gain_ref[:, cols]).astype(BF16)


def send_blocks(order_ref, left, w_ref, cols, own_ref, send_ref):
    width = own_ref.shape[1]
    for b in range(4):
        part = nt1(left, w_ref[block_cols(order_ref, b, width), cols])
        if b == 0:
            own_ref[...] = part
        else:
            send_ref[b - 1] = part.astype(BF16)


def project_kernel(half, blocks_per_seq, lens_ref, order_ref, *refs):
    gain_ref, w_ref, proj_ref, normed_ref, scale_ref = refs[5:]
    norm_into(refs[:5], half, blocks_per_seq, lens_ref, order_ref, gain_ref, normed_ref, scale_ref)
    proj_ref[...] = mm1(normed_ref[...], w_ref[...])


def norm_project(pieces, gain, weights, lens, order, length):
    tokens, width = pieces[0].shape
    blocks = tokens // ROWS
    full, out = weights.shape
    return pl.pallas_call(
        functools.partial(project_kernel, blocks // 2, length // ROWS),
        out_shape=(
            jax.ShapeDtypeStruct((tokens, out), F32),
            jax.ShapeDtypeStruct((tokens, full), BF16),
            jax.ShapeDtypeStruct((tokens, 1), F32),
        ),
        grid_spec=pltpu.PrefetchScalarGridSpec(
            num_scalar_prefetch=2,
            grid=(blocks,),
            in_specs=piece_specs(blocks, width, len(pieces)) + [whole_spec((1, full)), whole_spec((full, out))],
            out_specs=(row_spec(out), row_spec(full), row_spec(1)),
        ),
        cost_estimate=pl.CostEstimate(
            flops=2 * tokens * full * out, bytes_accessed=tokens * (out * 4 + full * 4),
            transcendentals=tokens),
        name="norm_project",
    )(lens, order, *pieces, gain, weights)


def spread_kernel(order_ref, left_ref, w_ref, own_ref, send_ref):
    send_blocks(order_ref, left_ref[...], w_ref, slice(None), own_ref, send_ref)


def spread_product(left, weights, order):
    tokens, inner = left.shape
    full = weights.shape[0]
    shapes, specs = send_specs(tokens, full // 4)
    return pl.pallas_call(
        spread_kernel,
        out_shape=shapes,
        grid_spec=pltpu.PrefetchScalarGridSpec(
            num_scalar_prefetch=1,
            grid=(tokens // ROWS,),
            in_specs=[row_spec(inner), whole_spec((full, inner))],
            out_specs=specs,
        ),
        cost_estimate=pl.CostEstimate(
            flops=2 * tokens * full * inner, bytes_accessed=tokens * (full * 3 + inner * 2),
            transcendentals=0),
        name="spread_product",
    )(order, left, weights)


def halves_blocks(half, order_ref, left, w_ref, cols, refs):
    width = refs[0].shape[1]
    parts = [nt1(left, w_ref[block_cols(order_ref, b, width), cols]) for b in range(4)]
    refs[0][...] = parts[0]
    upper = pl.program_id(0) < half

    @pl.when(upper)
    def _():
        for b in range(1, 4):
            refs[2 * b - 1][...] = parts[b].astype(BF16)

    @pl.when(jnp.logical_not(upper))
    def _():
        for b in range(1, 4):
            refs[2 * b][...] = parts[b].astype(BF16)


def halves_kernel(half, order_ref, left_ref, w_ref, *refs):
    halves_blocks(half, order_ref, left_ref[...], w_ref, slice(None), refs)


def spread_halves(left, weights, order):
    tokens, inner = left.shape
    full = weights.shape[0]
    blocks = tokens // ROWS
    part = jax.ShapeDtypeStruct((tokens // 2, full // 4), BF16)
    return pl.pallas_call(
        functools.partial(halves_kernel, blocks // 2),
        out_shape=(jax.ShapeDtypeStruct((tokens, full // 4), F32),) + (part,) * 6,
        grid_spec=pltpu.PrefetchScalarGridSpec(
            num_scalar_prefetch=1,
            grid=(blocks,),
            in_specs=[row_spec(inner), whole_spec((full, inner))],
            out_specs=tuple(piece_specs(blocks, full // 4, 7)),
        ),
        cost_estimate=pl.CostEstimate(
            flops=2 * tokens * full * inner, bytes_accessed=tokens * (full * 3 + inner * 2),
            transcendentals=0),
        name="spread_halves",
    )(order, left, weights)


def feed_kernel(half, blocks_per_seq, lens_ref, order_ref, *refs):
    (grad_ref, gain_ref, w_ref, normed_ref, scale_ref, act_ref, both_ref, dots_ref,
     feed_ref, feed_send_ref) = refs[7:17]
    ff = act_ref.shape[1]
    norm_into(refs[:7], half, blocks_per_seq, lens_ref, order_ref, gain_ref, normed_ref, scale_ref)
    gate_up = mm1(normed_ref[...], w_ref[:, : 2 * ff])
    inner_grad = mm1(grad_ref[...], w_ref[:, 2 * ff :])
    gate_act = gate_up[:, :ff]
    up_act = gate_up[:, ff:]
    sig = sigm(gate_act)
    silu = gate_act * sig
    act_ref[...] = (silu * up_act).astype(BF16)
    gate_grad = inner_grad * up_act * (sig * (1.0 + gate_act * (1.0 - sig)))
    up_grad = inner_grad * silu
    both_ref[:, :ff] = gate_grad.astype(BF16)
    both_ref[:, ff:] = up_grad.astype(BF16)
    dots = jnp.sum(gate_grad * gate_act + up_grad * up_act, axis=1, keepdims=True)
    dots_ref[0] = jnp.broadcast_to(dots, (ROWS, 128)).T[0:8]
    halves_blocks(half, order_ref, both_ref[...], w_ref, slice(0, 2 * ff), refs[17:])
    send_blocks(order_ref, act_ref[...], w_ref, slice(2 * ff, 3 * ff), feed_ref, feed_send_ref)


def feed_forward(pieces, grad_full, gain, weights, lens, order, length):
    tokens, width = pieces[0].shape
    blocks = tokens // ROWS
    full, out = weights.shape
    ff = out // 3
    shapes, specs = send_specs(tokens, width)
    return pl.pallas_call(
        functools.partial(feed_kernel, blocks // 2, length // ROWS),
        out_shape=(
            jax.ShapeDtypeStruct((tokens, full), BF16),
            jax.ShapeDtypeStruct((tokens, 1), F32),
            jax.ShapeDtypeStruct((tokens, ff), BF16),
            jax.ShapeDtypeStruct((tokens, 2 * ff), BF16),
            jax.ShapeDtypeStruct((blocks, 8, ROWS), F32),
        ) + shapes + (
            jax.ShapeDtypeStruct((tokens, width), F32),
        ) + (jax.ShapeDtypeStruct((tokens // 2, width), BF16),) * 6,
        grid_spec=pltpu.PrefetchScalarGridSpec(
            num_scalar_prefetch=2,
            grid=(blocks,),
            in_specs=piece_specs(blocks, width, len(pieces))
            + [row_spec(full), whole_spec((1, full)), whole_spec((full, out))],
            out_specs=(row_spec(full), row_spec(1), row_spec(ff), row_spec(2 * ff),
                       pl.BlockSpec((1, 8, ROWS), lambda i, *_: (i, 0, 0))) + specs
            + tuple(piece_specs(blocks, width, 7)),
        ),
        cost_estimate=pl.CostEstimate(
            flops=4 * tokens * full * out, bytes_accessed=tokens * full * 16,
            transcendentals=tokens * ff),
        name="feed_forward",
    )(lens, order, *pieces, grad_full, gain, weights)


def join_kernel(half, order_ref, *refs):
    w_ref, full_ref, out_ref = refs[7:]
    pieces = read_pieces(refs[:7], half)
    width = pieces[0].shape[1]
    for b, piece in enumerate(pieces):
        full_ref[:, block_cols(order_ref, b, width)] = piece
    out_ref[...] = mm1(full_ref[...], w_ref[...])


def join_product(pieces, weights, order):
    tokens, width = pieces[0].shape
    blocks = tokens // ROWS
    full, out = weights.shape
    return pl.pallas_call(
        functools.partial(join_kernel, blocks // 2),
        out_shape=(
            jax.ShapeDtypeStruct((tokens, full), BF16),
            jax.ShapeDtypeStruct((tokens, out), F32),
        ),
        grid_spec=pltpu.PrefetchScalarGridSpec(
            num_scalar_prefetch=1,
            grid=(blocks,),
            in_specs=piece_specs(blocks, width, len(pieces)) + [whole_spec((full, out))],
            out_specs=(row_spec(full), row_spec(out)),
        ),
        cost_estimate=pl.CostEstimate(
            flops=2 * tokens * full * out, bytes_accessed=tokens * (full * 4 + out * 4),
            transcendentals=0),
        name="join_product",
    )(order, *pieces, weights)


D = 1024
PARTS = 1


def contract_rows(left, right):
    return lax.dot_general(left, right, (((0,), (0,)), ((), ())), preferred_element_type=F32)


def after(value, *others):
    return lax.optimization_barrier((value,) + others)[0]


def xor_perm(size, bit):
    return [(i, i ^ bit) for i in range(size)]


def send_col(values, bit):
    return lax.ppermute(values, "col", xor_perm(4, bit))


def gather_features(values):
    half = values.shape[0] // 2
    from_x = send_col(values, 1)
    from_y = send_col(values, 2)
    far_top = send_col(from_y[:half], 1)
    far_low = send_col(from_x[half:], 2)
    return values, from_x, from_y, far_top, far_low


def sum_features(own, send, *earlier):
    half = own.shape[0] // 2
    via_x = send_col(send[2, :half], 1).astype(F32)
    via_y = send_col(send[2, half:], 2).astype(F32)
    if earlier:
        via_x = after(via_x, *earlier)
        via_y = after(via_y, *earlier)
    part_x = send[0].astype(F32)
    part_y = send[1].astype(F32)
    to_y = jnp.concatenate([part_y[:half] + via_x, part_y[half:]], axis=0).astype(BF16)
    to_x = jnp.concatenate([part_x[:half], part_x[half:] + via_y], axis=0).astype(BF16)
    return own + send_col(to_x, 1).astype(F32) + send_col(to_y, 2).astype(F32)


def sum_direct(own, send):
    total = own
    for bit in range(1, 4):
        total = total + send_col(send[bit - 1], bit).astype(F32)
    return total


def gather_halves(values):
    half = values.shape[0] // 2
    top, low = values[:half], values[half:]
    y_top = send_col(top, 2)
    x_low = send_col(low, 1)
    x_top = send_col(top, 1)
    y_low = send_col(low, 2)
    return values, x_top, x_low, y_top, y_low, send_col(y_top, 1), send_col(x_low, 2)


def sum_halves(own, x_top, x_low, y_top, y_low, far_top, far_low):
    via_x = send_col(far_top, 1).astype(F32)
    via_y = send_col(far_low, 2).astype(F32)
    x_top = send_col(x_top, 1)
    y_low = send_col(y_low, 2)
    x_low = send_col((x_low.astype(F32) + via_y).astype(BF16), 1)
    y_top = send_col((y_top.astype(F32) + via_x).astype(BF16), 2)
    top = x_top.astype(F32) + y_top.astype(F32)
    low = x_low.astype(F32) + y_low.astype(F32)
    return own + jnp.concatenate([top, low], axis=0)


def sum_scalars(values):
    return (values + send_col(values, 1)) + (send_col(values, 2) + send_col(values, 3))


def swap_cores(mine, dp):
    other = lax.ppermute(mine, "dp", [(0, 1), (1, 0)])
    return jnp.where(
        dp == 0, jnp.concatenate([mine, other], axis=0), jnp.concatenate([other, mine], axis=0)
    )


def gather_weight(block, dp, *earlier):
    rows = block.shape[0] // 2
    half = lax.dynamic_slice_in_dim(block, dp * rows, rows, 0)
    if earlier:
        half = after(half, *earlier)
    return lax.all_gather(half, ("row", "dp"), axis=0, tiled=True)


def scatter_weight(grad, dp):
    mine = lax.psum_scatter(grad, ("row", "dp"), scatter_dimension=0, tiled=True)
    return swap_cores(mine, dp).astype(F32)


def sum_small(values):
    count = lax.axis_size("row")
    if count != 4:
        return lax.psum(values, ("dp", "row"))
    size = values.shape[0]
    total = jnp.pad(values, (0, -size % 1024)).reshape(-1, 128)
    total = total + lax.ppermute(total, "dp", [(0, 1), (1, 0)])
    others = [lax.ppermute(total, "row", xor_perm(count, bit)) for bit in range(1, count)]
    return ((total + others[0]) + (others[1] + others[2])).reshape(-1)[:size]


def on_device(
    inputs,
    out_grad,
    seq_lengths,
    first_gain,
    query_proj,
    key_proj,
    value_proj,
    decay_proj,
    beta_proj,
    gate_proj,
    query_conv,
    key_conv,
    value_conv,
    decay_log,
    step_bias,
    output_gain,
    output_proj,
    second_gain,
    hidden_gate,
    hidden_up,
    hidden_down,
):
    seq_count, length, col_width = inputs.shape
    heads = decay_log.shape[0]
    parts = PARTS
    per_part = seq_count // parts
    tokens = per_part * length
    col = lax.axis_index("col")
    dp = lax.axis_index("dp")
    order = (col ^ jnp.arange(4, dtype=jnp.int32)).astype(jnp.int32)
    row_block = query_proj.shape[0]
    vals = heads * DV
    qkv = heads * (2 * DK + DV)
    ff = hidden_gate.shape[1]
    ff_pad = -ff % 128

    in_block = jnp.concatenate(
        [query_proj, key_proj, value_proj, gate_proj, decay_proj, beta_proj,
         jnp.zeros((row_block, 128 - 2 * heads), BF16)], axis=1)
    in_weights = gather_weight(in_block, dp)
    positions = lax.broadcasted_iota(jnp.int32, (seq_count, length), 1)
    valid_all = (positions < seq_lengths[:, None]).astype(F32)
    grad_all = out_grad.astype(F32) * valid_all[:, :, None]
    ff_block = jnp.concatenate(
        [jnp.pad(piece, ((0, 0), (0, ff_pad)))
         for piece in (hidden_gate, hidden_up, hidden_down.T)], axis=1)

    conv = jnp.concatenate([query_conv, key_conv, value_conv], axis=1).astype(F32)
    rates = rate_rows(decay_log, step_bias)
    gain_row = output_gain.astype(F32)[None]
    first_row = first_gain.astype(F32)[None]
    second_row = second_gain.astype(F32)[None]
    first_local = lax.dynamic_slice_in_dim(first_row, col * col_width, col_width, 1)
    second_local = lax.dynamic_slice_in_dim(second_row, col * col_width, col_width, 1)

    state = []
    for part in range(parts):
        seqs = slice(part * per_part, (part + 1) * per_part)
        local = inputs[seqs].reshape(tokens, col_width)
        state.append(dict(
            lens=seq_lengths[seqs], valid=valid_all[seqs].reshape(tokens, 1), local=local,
            grad_out=grad_all[seqs].reshape(tokens, col_width), pieces=gather_features(local)))
    out_weights = gather_weight(output_proj.T, dp, state[0]["pieces"][1])
    for st in state:
        proj, st["normed"], st["scale"] = norm_project(
            st["pieces"], first_row, in_weights, st["lens"], order, length)
        st["proj"] = proj.reshape(per_part, length, -1)
        if st is state[0]:
            grad_low = grad_all.astype(BF16).reshape(seq_count * length, col_width)
            grad_full = lax.all_gather(after(grad_low, st["scale"]), "col", axis=1, tiled=True)
            ff_weights = gather_weight(ff_block, dp, st["scale"])
        mixed, *st["saved"] = mixer_fwd(st["proj"], conv, rates, gain_row, heads, per_part)
        st["mixed"] = mixed.reshape(tokens, vals)
        attention = sum_halves(*spread_halves(st["mixed"], out_weights, order))
        st["hidden"] = st["local"].astype(F32) + attention
        st["pieces"] = gather_halves(st["hidden"].astype(BF16))
    results = []
    gate_up_grad = 0.0
    down_grad = 0.0
    second_gain_grad = 0.0
    for part, st in enumerate(state):
        st["grad_full"] = grad_full[part * tokens : (part + 1) * tokens]
        normed, scale, act, both, dots, feed_own, feed_send, *sends = feed_forward(st["pieces"], st["grad_full"], second_row, ff_weights, st["lens"], order,
                          length)
        dots = sum_scalars(dots)[:, 0, :].reshape(tokens, 1)
        second_grad = sum_halves(*sends) * st["valid"]
        hat = st["hidden"] * scale
        second_gain_grad = second_gain_grad + jnp.sum(second_grad * hat, axis=0)
        st["hidden_grad"] = st["grad_out"] + scale * (
            second_grad * second_local - hat * (dots * (1.0 / D)))
        st["pieces"] = gather_halves(st["hidden_grad"].astype(BF16))
        hidden, feed_own, feed_send = lax.optimization_barrier(
            (st["hidden"], feed_own, feed_send, st["pieces"][6]))[:3]
        feed = sum_direct(feed_own, feed_send)
        results.append(((hidden + feed) * st["valid"]).astype(BF16))
        gate_up_grad = gate_up_grad + contract_rows(normed, both)
        down_grad = down_grad + contract_rows(st["grad_full"], act)
    gate_up_low = gate_up_grad.astype(BF16)
    down_low = down_grad.astype(BF16)
    gate_up_grad = scatter_weight(gate_up_low, dp)
    down_grad = scatter_weight(after(down_low, gate_up_low), dp)
    out_weight_grad = 0.0
    in_weight_grad = 0.0
    first_gain_grad = 0.0
    small = 0.0
    for st in state:
        own = after(st["pieces"][0], gate_up_low, down_low)
        st["attn_grad"], mixed_grad = join_product(
            (own,) + st["pieces"][1:], out_weights, order)
        out_weight_grad = out_weight_grad + contract_rows(st["attn_grad"], st["mixed"])
        if st is state[-1]:
            out_low = out_weight_grad.astype(BF16)
            mixed_grad = after(mixed_grad, out_low)
        dproj, dots, *grads = mixer_bwd(
            st["proj"], mixed_grad.reshape(per_part, length, vals), st["saved"], conv, rates,
            gain_row, heads, per_part, 0)
        small = small + jnp.concatenate([grad.reshape(-1) for grad in grads])
        st["dproj"] = dproj.reshape(tokens, -1)
        st["dots"] = sum_scalars(dots)
        in_weight_grad = in_weight_grad + contract_rows(
            st["normed"], after(st["dproj"], *results))
    in_low = in_weight_grad.astype(BF16)
    in_weight_grad = scatter_weight(after(in_low, out_low), dp)
    at = CONV * qkv + 2 * heads
    gain_out = sum_scalars(small[at:].reshape(2, 128)).reshape(-1)
    small_sums = sum_small(jnp.concatenate([small[:at], second_gain_grad, gain_out]))
    input_grads = []
    for st in state:
        own, send = spread_product(after(st["dproj"], in_low, st["dots"]), in_weights, order)
        first_grad = sum_features(own, send, small_sums) * st["valid"]
        hat = st["local"].astype(F32) * st["scale"]
        first_gain_grad = first_gain_grad + jnp.sum(first_grad * hat, axis=0)
        input_grads.append(st["hidden_grad"] + st["scale"] * (
            first_grad * first_local - hat * (st["dots"].reshape(tokens, 1) * (1.0 / D))))
    out_weight_grad = scatter_weight(out_low, dp)
    first_gain_grad = sum_small(first_gain_grad)
    conv_grad = small_sums[: CONV * qkv].reshape(CONV, qkv)
    gate_at = qkv + vals
    qk = heads * DK
    return (
        jnp.concatenate(results, axis=0).reshape(seq_count, length, col_width),
        jnp.concatenate(input_grads, axis=0).reshape(seq_count, length, col_width),
        first_gain_grad,
        in_weight_grad[:, :qk],
        in_weight_grad[:, qk : 2 * qk],
        in_weight_grad[:, 2 * qk : qkv],
        in_weight_grad[:, gate_at : gate_at + heads],
        in_weight_grad[:, gate_at + heads : gate_at + 2 * heads],
        in_weight_grad[:, qkv:gate_at],
        conv_grad[:, :qk],
        conv_grad[:, qk : 2 * qk],
        conv_grad[:, 2 * qk :],
        small_sums[CONV * qkv : CONV * qkv + heads],
        small_sums[CONV * qkv + heads : at],
        small_sums[at + col_width :],
        out_weight_grad.T,
        small_sums[at : at + col_width],
        gate_up_grad[:, :ff],
        gate_up_grad[:, ff + ff_pad : 2 * ff + ff_pad],
        down_grad[:, :ff].T,
    )


def solution(mesh):
    in_specs = (
        P(("dp", "row"), None, "col"),
        P(("dp", "row"), None, "col"),
        P(("dp", "row")),
        P(),
        P("row", "col"),
        P("row", "col"),
        P("row", "col"),
        P("row", "col"),
        P("row", "col"),
        P("row", "col"),
        P(None, "col"),
        P(None, "col"),
        P(None, "col"),
        P("col"),
        P("col"),
        P(),
        P("col", "row"),
        P(),
        P("row", "col"),
        P("row", "col"),
        P("col", "row"),
    )
    out_specs = (
        P(("dp", "row"), None, "col"),
        P(("dp", "row"), None, "col"),
        P("col"),
        P("row", "col"),
        P("row", "col"),
        P("row", "col"),
        P("row", "col"),
        P("row", "col"),
        P("row", "col"),
        P(None, "col"),
        P(None, "col"),
        P(None, "col"),
        P("col"),
        P("col"),
        P(),
        P("col", "row"),
        P("col"),
        P("row", "col"),
        P("row", "col"),
        P("col", "row"),
    )
    return jax.shard_map(
        on_device, mesh=mesh, in_specs=in_specs, out_specs=out_specs, check_vma=False
    )
```

```python
import functools
import jax
import jax.numpy as jnp
from jax import lax
from jax.experimental import pallas as pl
from jax.experimental.pallas import tpu as pltpu
from jax.sharding import PartitionSpec as P

DK = 128
DV = 256
CONV = 4
NORM_EPS = 1e-05
UNIT_EPS = 1e-06
BLK = 128
SUB = 32
F32 = jnp.float32
BF16 = jnp.bfloat16


def mm1(a, b):
    return lax.dot_general(a, b, (((1,), (0,)), ((), ())), preferred_element_type=F32)


def nt1(a, b):
    return lax.dot_general(a, b, (((1,), (1,)), ((), ())), preferred_element_type=F32)


def halves(a):
    hi = a.astype(BF16)
    return hi, (a - hi.astype(F32)).astype(BF16)


def mm(a, b):
    ah, al = halves(a)
    bh, bl = halves(b)
    return mm1(jnp.concatenate([ah, al, ah], axis=1), jnp.concatenate([bh, bh, bl], axis=0))


def mm_nt(a, b):
    ah, al = halves(a)
    bh, bl = halves(b)
    return nt1(jnp.concatenate([ah, al, ah], axis=1), jnp.concatenate([bh, bh, bl], axis=1))


def mm_sum(a, b):
    ah, al = halves(a)
    bh, bl = halves(b)
    return mm1(ah, bh) + (mm1(ah, bl) + mm1(al, bh))


def mm_nt_sum(a, b):
    ah, al = halves(a)
    bh, bl = halves(b)
    return nt1(ah, bh) + (nt1(ah, bl) + nt1(al, bh))


def sigm(v):
    return 0.5 * jnp.tanh(0.5 * v) + 0.5


def iota2(shape, axis):
    return lax.broadcasted_iota(jnp.int32, shape, axis)


def unit_lower_inverse(mats):
    groups = BLK // SUB
    lane = iota2((SUB, BLK), 1)
    sub = iota2((SUB, BLK), 0)
    lane_group = lane // SUB
    solved = []
    for b in range(groups):
        rows = slice(b * SUB, (b + 1) * SUB)
        packed = jnp.zeros((SUB, BLK), F32)
        for p, mat in enumerate(mats):
            piece = mat[rows]
            shift = (SUB * (p - b)) % BLK
            if shift:
                piece = pltpu.roll(piece, shift, 1)
            packed = jnp.where(lane_group == p, piece, packed)
        acc = jnp.where(lane - lane_group * SUB == sub, 1.0, 0.0).astype(F32)
        tiles = [acc[8 * t : 8 * t + 8] for t in range(SUB // 8)]
        coefs = [packed[8 * t : 8 * t + 8] for t in range(SUB // 8)]
        base = (iota2((8, BLK), 1) // SUB) * SUB
        for j in range(SUB - 1):
            row = jnp.broadcast_to(tiles[j // 8][j % 8 : j % 8 + 1], (8, BLK))
            for t in range((j + 1) // 8, SUB // 8):
                col = jnp.take_along_axis(coefs[t], base + j, axis=1)
                tiles[t] = tiles[t] - col * row
        solved.append(jnp.concatenate(tiles, axis=0))
    out = []
    row_i = iota2((BLK, BLK), 0)
    col_i = iota2((BLK, BLK), 1)
    for p, mat in enumerate(mats):
        blocks = []
        for b in range(groups):
            piece = solved[b]
            shift = (SUB * (b - p)) % BLK
            if shift:
                piece = pltpu.roll(piece, shift, 1)
            blocks.append(jnp.where(lane_group == b, piece, 0.0))
        inv = jnp.concatenate(blocks, axis=0)
        zero32 = jnp.zeros((SUB, BLK), F32)
        off = jnp.where((row_i // 64 == col_i // 64) & (row_i // SUB > col_i // SUB), mat, 0.0)
        lhs = jnp.concatenate([off[32:64], off[96:128]], axis=0)
        part = mm(lhs, inv)
        placed = jnp.concatenate([zero32, part[:32], zero32, part[32:]], axis=0)
        lhs = jnp.concatenate([inv[32:64], inv[96:128]], axis=0)
        part = mm(lhs, placed)
        inv = inv - jnp.concatenate([zero32, part[:32], zero32, part[32:]], axis=0)
        off = jnp.where(col_i[64:] < 64, mat[64:], 0.0)
        part = mm(off, inv)
        zero64 = jnp.zeros((64, BLK), F32)
        part = mm(inv[64:], jnp.concatenate([zero64, part], axis=0))
        inv = jnp.concatenate([inv[:64], inv[64:] - part], axis=0)
        out.append(inv)
    return out


def decay_terms(ab, neg_rate, bias, heads):
    pre = ab + bias
    soft = jnp.maximum(pre, 0.0) + jnp.log(1.0 + jnp.exp(-jnp.abs(pre)))
    log_decay = neg_rate * soft
    beta = sigm(ab)
    row_i = iota2((BLK, BLK), 0)
    col_i = iota2((BLK, BLK), 1)
    tri = jnp.where(row_i >= col_i, 1.0, 0.0).astype(BF16)
    hi = log_decay.astype(BF16)
    rest = log_decay - hi.astype(F32)
    mid = rest.astype(BF16)
    low = (rest - mid.astype(F32)).astype(BF16)
    cum = mm1(tri, hi) + (mm1(tri, mid) + mm1(tri, low))
    return log_decay, beta, cum


def conv_taps(xs_ref, s, kernel):
    pre = xs_ref[s, 5 : 5 + BLK, :] * kernel[0:1]
    for i in range(1, CONV):
        pre = pre + xs_ref[s, 5 + i : 5 + i + BLK, :] * kernel[i : i + 1]
    return pre


def fwd_kernel(heads, nseq, proj_ref, conv_ref, rate_ref, gain_ref,
               mixed_ref, o_ref, u_ref, s_ref, t_ref, xs_ref, state_ref):
    qkv = heads * (2 * DK + DV)
    gate_at = qkv
    ab_at = qkv + heads * DV
    step = pl.program_id(1)

    @pl.when(step == 0)
    def _():
        xs_ref[:, 0:8, :] = jnp.zeros((nseq, 8, qkv), F32)
        state_ref[...] = jnp.zeros_like(state_ref)

    row_i = iota2((BLK, BLK), 0)
    col_i = iota2((BLK, BLK), 1)
    kernel = conv_ref[...]
    neg_rate = rate_ref[0:1]
    bias = rate_ref[1:2]
    gain = gain_ref[...]
    items = []
    for s in range(nseq):
        xs_ref[s, 8 : 8 + BLK, :] = proj_ref[s, :, 0:qkv]
        pre = conv_taps(xs_ref, s, kernel)
        xs_ref[s, 0:8, :] = xs_ref[s, BLK : BLK + 8, :]
        act = pre * sigm(pre)
        ab = proj_ref[s, :, ab_at : ab_at + 128]
        _, beta_all, cum_all = decay_terms(ab, neg_rate, bias, heads)
        cum_t = cum_all.T
        for h in range(heads):
            q = act[:, h * DK : (h + 1) * DK]
            k = act[:, (heads + h) * DK : (heads + h + 1) * DK]
            v = act[:, 2 * heads * DK + h * DV : 2 * heads * DK + (h + 1) * DV]
            qn = q * (lax.rsqrt(jnp.sum(q * q, axis=1, keepdims=True) + UNIT_EPS) * DK ** -0.5)
            kn = k * lax.rsqrt(jnp.sum(k * k, axis=1, keepdims=True) + UNIT_EPS)
            cum = cum_all[:, h : h + 1]
            cum_row = cum_t[h : h + 1, :]
            beta = beta_all[:, heads + h : heads + h + 1]
            ratio = jnp.exp(jnp.where(row_i >= col_i, cum - cum_row, -1e30))
            kb = kn
            kq = jnp.concatenate([kb, qn], axis=0)
            gram = mm_nt(kq, kb)
            a = jnp.where(row_i > col_i, gram[:BLK] * ratio * beta, 0.0)
            p = gram[BLK:] * ratio
            last = cum[BLK - 1 : BLK]
            kd = kn * jnp.exp(last - cum)
            items.append((s, h, kq, a, p, kd, v, beta, jnp.exp(cum), jnp.exp(last)))
    invs = []
    for at in range(0, len(items), 4):
        invs = invs + unit_lower_inverse([item[3] for item in items[at : at + 4]])
    for item, inv in zip(items, invs):
        s, h, kq, a, p, kd, v, beta, ecum, elast = item
        state = state_ref[s, h]
        low_state = state
        ks_qs = mm(kq, low_state)
        x = beta * (v - ecum * ks_qs[:BLK])
        inv_low = inv
        u = mm(inv_low, x)
        pk = jnp.concatenate([p, kd.T], axis=0)
        pu = mm(pk, u)
        o = ecum * ks_qs[BLK:] + pu[:BLK]
        state_ref[s, h] = elast * state + pu[BLK:]
        s_ref[s, 0, h] = low_state
        t_ref[s, 0, h] = inv_low
        cols = slice(h * DV, (h + 1) * DV)
        u_ref[s, :, cols] = u
        o_ref[s, :, cols] = o
        g = proj_ref[s, :, gate_at + h * DV : gate_at + (h + 1) * DV]
        norm = o * lax.rsqrt(jnp.mean(o * o, axis=1, keepdims=True) + NORM_EPS)
        mixed_ref[s, :, cols] = (norm * gain * (g * sigm(g))).astype(BF16)


def rate_rows(decay_log, step_bias):
    heads = decay_log.shape[0]
    pad = 128 - heads
    return jnp.stack([jnp.pad(-jnp.exp(decay_log), (0, pad)), jnp.pad(step_bias, (0, pad))])


def mixer_fwd(proj, conv, rates, gain, heads, nseq):
    seqs, length, width = proj.shape
    blocks = length // BLK
    qkv = heads * (2 * DK + DV)
    vals = heads * DV
    tok = lambda i, c: (i, c, 0)
    return pl.pallas_call(
        functools.partial(fwd_kernel, heads, nseq),
        out_shape=(
            jax.ShapeDtypeStruct((seqs, length, vals), BF16),
            jax.ShapeDtypeStruct((seqs, length, vals), F32),
            jax.ShapeDtypeStruct((seqs, length, vals), F32),
            jax.ShapeDtypeStruct((seqs, blocks, heads, DK, DV), F32),
            jax.ShapeDtypeStruct((seqs, blocks, heads, BLK, BLK), F32),
        ),
        grid=(seqs // nseq, blocks),
        in_specs=[
            pl.BlockSpec((nseq, BLK, width), tok),
            pl.BlockSpec((CONV, qkv), lambda i, c: (0, 0)),
            pl.BlockSpec((2, 128), lambda i, c: (0, 0)),
            pl.BlockSpec((1, DV), lambda i, c: (0, 0)),
        ],
        out_specs=(
            pl.BlockSpec((nseq, BLK, vals), tok),
            pl.BlockSpec((nseq, BLK, vals), tok),
            pl.BlockSpec((nseq, BLK, vals), tok),
            pl.BlockSpec((nseq, 1, heads, DK, DV), lambda i, c: (i, c, 0, 0, 0)),
            pl.BlockSpec((nseq, 1, heads, BLK, BLK), lambda i, c: (i, c, 0, 0, 0)),
        ),
        scratch_shapes=[
            pltpu.VMEM((nseq, 8 + BLK, qkv), F32),
            pltpu.VMEM((nseq, heads, DK, DV), F32),
        ],
        compiler_params=pltpu.CompilerParams(dimension_semantics=("arbitrary", "arbitrary")),
        cost_estimate=pl.CostEstimate(
            flops=seqs * length * heads * 6_000_000, bytes_accessed=seqs * length * width * 8,
            transcendentals=0),
        name="mixer_fwd",
    )(proj, conv, rates, gain)


def colsum(v):
    return jnp.sum(v.reshape(v.shape[0] // 8, 8, v.shape[1]), axis=0)


def bwd_kernel(heads, nseq, proj_ref, prev_ref, dmix_ref, o_ref, u_ref, s_ref, t_ref,
               conv_ref, rate_ref, gain_ref,
               dproj_ref, dots_ref, dotc_ref, dconv_ref, drate_ref, dgain_ref, xs_ref, ds_ref, dstate_ref):
    qkv = heads * (2 * DK + DV)
    gate_at = qkv
    ab_at = qkv + heads * DV
    step = pl.program_id(1)
    first = pl.num_programs(1) - 1

    @pl.when(step == 0)
    def _():
        ds_ref[:, BLK : BLK + 8, :] = jnp.zeros((nseq, 8, qkv), F32)
        dstate_ref[...] = jnp.zeros_like(dstate_ref)

    @pl.when((step == 0) & (pl.program_id(0) == 0))
    def _():
        dconv_ref[...] = jnp.zeros_like(dconv_ref)
        drate_ref[...] = jnp.zeros_like(drate_ref)
        dgain_ref[...] = jnp.zeros_like(dgain_ref)

    row_i = iota2((BLK, BLK), 0)
    col_i = iota2((BLK, BLK), 1)
    lower = row_i >= col_i
    strict = row_i > col_i
    kernel = conv_ref[...]
    neg_rate = rate_ref[0:1]
    bias = rate_ref[1:2]
    gain = gain_ref[...]
    has_prev = jnp.where(step == first, 0.0, 1.0).astype(F32)
    lane1 = iota2((1, 128), 1)
    for s in range(nseq):
        xs_ref[s, 0:8, :] = prev_ref[s, :, 0:qkv] * has_prev
        xs_ref[s, 8 : 8 + BLK, :] = proj_ref[s, :, 0:qkv]
        pre = conv_taps(xs_ref, s, kernel)
        sig = sigm(pre)
        act = pre * sig
        dsilu = sig * (1.0 + pre * (1.0 - sig))
        ab = proj_ref[s, :, ab_at : ab_at + 128]
        log_decay, beta_all, cum_all = decay_terms(ab, neg_rate, bias, heads)
        cum_t = cum_all.T
        dots = jnp.zeros((BLK, 1), F32)
        dcum_all = jnp.zeros((BLK, 128), F32)
        dbeta_all = jnp.zeros((BLK, 128), F32)
        dact = [None] * (3 * heads)
        for h in range(heads):
            q = act[:, h * DK : (h + 1) * DK]
            k = act[:, (heads + h) * DK : (heads + h + 1) * DK]
            v = act[:, 2 * heads * DK + h * DV : 2 * heads * DK + (h + 1) * DV]
            rq = lax.rsqrt(jnp.sum(q * q, axis=1, keepdims=True) + UNIT_EPS)
            rk = lax.rsqrt(jnp.sum(k * k, axis=1, keepdims=True) + UNIT_EPS)
            qh = q * rq
            qn = qh * DK ** -0.5
            kn = k * rk
            cum = cum_all[:, h : h + 1]
            cum_row = cum_t[h : h + 1, :]
            beta = beta_all[:, heads + h : heads + h + 1]
            ecum = jnp.exp(cum)
            last = cum[BLK - 1 : BLK]
            elast = jnp.exp(last)
            ratio = jnp.exp(jnp.where(lower, cum - cum_row, -1e30))
            ktail = jnp.exp(last - cum)
            kb = kn
            qb = qn
            gram = mm_nt_sum(jnp.concatenate([kb, qb], axis=0), kb)
            sfac = jnp.where(strict, ratio * beta, 0.0)
            kgr = gram[:BLK]
            p = gram[BLK:] * ratio
            cols = slice(h * DV, (h + 1) * DV)
            o = o_ref[s, :, cols]
            g = proj_ref[s, :, gate_at + h * DV : gate_at + (h + 1) * DV]
            dm = dmix_ref[s, :, cols].astype(F32)
            ro = lax.rsqrt(jnp.mean(o * o, axis=1, keepdims=True) + NORM_EPS)
            n = o * ro
            gs = sigm(g)
            gsil = g * gs
            dmn = dm * n
            dgain_ref[...] += colsum(dmn * gsil)
            dgate = dmn * gain * (gs * (1.0 + g * (1.0 - gs)))
            dproj_ref[s, :, gate_at + h * DV : gate_at + (h + 1) * DV] = dgate.astype(BF16)
            dots = dots + jnp.sum(dgate * g, axis=1, keepdims=True)
            dn = dm * gain * gsil
            do = ro * (dn - n * jnp.mean(dn * n, axis=1, keepdims=True))
            dob = do
            dstate = dstate_ref[s, h]
            dstb = dstate
            u = u_ref[s, :, cols]
            sb = s_ref[s, 0, h]
            tinv = t_ref[s, 0, h]
            kd = kn * ktail
            du = mm_sum(jnp.concatenate([p.T, kd], axis=1), jnp.concatenate([dob, dstb], axis=0))
            dx = mm_sum(tinv.astype(F32).T, du)
            dxb = dx
            ddx = jnp.concatenate([dob, dxb], axis=0)
            both = mm_nt_sum(ddx, jnp.concatenate([sb, u], axis=0))
            be = beta * ecum
            z = both[BLK:, :DK]
            dqi = ecum * both[:BLK, :DK]
            dki = -be * z
            dks = -be * dx
            lhs = jnp.concatenate([qn.T, kn.T], axis=1)
            rhs = jnp.concatenate([(ecum * do), dks], axis=0)
            dstate_ref[s, h] = elast * dstate + mm_sum(lhs, rhs)
            dkd = mm_nt_sum(u, dstb)
            dp = both[:BLK, DK:]
            da = -both[BLK:, DK:]
            dqk = dp * ratio
            dkg = da * sfac
            dlog = dp * p + dkg * kgr
            pair = jnp.concatenate([dqk, dkg + dkg.T], axis=0)
            prod = mm_sum(pair, kb)
            dqn = dqi + prod[:BLK]
            dkn = dki + prod[BLK:] + mm_sum(dqk.T, qb) + dkd * ktail
            kz = jnp.sum(kn * z, axis=1, keepdims=True)
            dkdk = jnp.sum(dkd * kd, axis=1, keepdims=True)
            row_sum = jnp.sum(dlog, axis=1, keepdims=True)
            col_sum = jnp.sum(dlog.T, axis=1, keepdims=True)
            dcum = row_sum - col_sum + jnp.sum(qn * dqi, axis=1, keepdims=True) - be * kz - dkdk
            tail = jnp.sum(dkdk, axis=0, keepdims=True) + elast * jnp.sum(
                jnp.sum(sb.astype(F32) * dstate, axis=1, keepdims=True), axis=0, keepdims=True)
            dcum = dcum + jnp.where(row_i[:, 0:1] == BLK - 1, tail, 0.0)
            kgl = jnp.sum(da * jnp.where(strict, ratio * kgr, 0.0), axis=1, keepdims=True)
            dbeta = jnp.sum(dx * v, axis=1, keepdims=True) - ecum * kz + kgl
            dcum_all = jnp.where(lane1 == h, dcum, dcum_all)
            dbeta_all = jnp.where(lane1 == heads + h, dbeta, dbeta_all)
            dact[h] = (DK ** -0.5 * rq) * (dqn - qh * jnp.sum(dqn * qh, axis=1, keepdims=True))
            dact[heads + h] = rk * (dkn - kn * jnp.sum(dkn * kn, axis=1, keepdims=True))
            dact[2 * heads + h] = beta * dx
        tri = jnp.where(col_i >= row_i, 1.0, 0.0).astype(BF16)
        hi, lo = halves(dcum_all)
        dlog_decay = mm1(tri, hi) + mm1(tri, lo)
        dpre_a = dlog_decay * neg_rate * sigm(ab + bias)
        dpre_b = dbeta_all * beta_all * (1.0 - beta_all)
        dproj_ref[s, :, ab_at : ab_at + 128] = (dpre_a + dpre_b).astype(BF16)
        dots = dots + jnp.sum((dpre_a + dpre_b) * ab, axis=1, keepdims=True)
        drate_ref[0:8, :] += colsum(dlog_decay * log_decay)
        drate_ref[8:16, :] += colsum(dpre_a)
        dpre = jnp.concatenate(dact, axis=1) * dsilu
        ds_ref[s, 0:BLK, :] = dpre
        dx_in = ds_ref[s, 3 : 3 + BLK, :] * kernel[0:1]
        for i in range(1, CONV):
            dx_in = dx_in + ds_ref[s, 3 - i : 3 - i + BLK, :] * kernel[i : i + 1]
        dproj_ref[s, :, 0:qkv] = dx_in.astype(BF16)
        dots = dots + jnp.sum(dx_in * xs_ref[s, 8 : 8 + BLK, :], axis=1, keepdims=True)
        dotc_ref[s] = dots
        dots_ref[s, 0] = jnp.broadcast_to(dots, (BLK, 128)).T[0:8]
        for i in range(CONV):
            dconv_ref[8 * i : 8 * i + 8, :] += colsum(dpre * xs_ref[s, 5 + i : 5 + i + BLK, :])
        ds_ref[s, BLK : BLK + 8, :] = ds_ref[s, 0:8, :]


def mixer_bwd(proj, dmixed, saved, conv, rates, gain, heads, nseq, seq):
    o, u, states, invs = saved
    _, length, width = proj.shape
    seqs = dmixed.shape[0]
    first = seq // nseq
    blocks = length // BLK
    qkv = heads * (2 * DK + DV)
    vals = heads * DV
    tok = lambda i, c: (i, blocks - 1 - c, 0)
    all_tok = lambda i, c: (i + first, blocks - 1 - c, 0)
    all_blk = lambda i, c: (i + first, blocks - 1 - c, 0, 0, 0)
    whole = lambda i, c: (0, 0)
    dproj, dots, dot_cols, dconv, drate, dgain = pl.pallas_call(
        functools.partial(bwd_kernel, heads, nseq),
        out_shape=(
            jax.ShapeDtypeStruct((seqs, length, width), BF16),
            jax.ShapeDtypeStruct((seqs, blocks, 8, 128), F32),
            jax.ShapeDtypeStruct((seqs, length, 1), F32),
            jax.ShapeDtypeStruct((8 * CONV, qkv), F32),
            jax.ShapeDtypeStruct((16, 128), F32),
            jax.ShapeDtypeStruct((8, DV), F32),
        ),
        grid=(seqs // nseq, blocks),
        in_specs=[
            pl.BlockSpec((nseq, BLK, width), all_tok),
            pl.BlockSpec((nseq, 8, qkv), lambda i, c: (
                i + first, jnp.maximum((blocks - 1 - c) * (BLK // 8) - 1, 0), 0)),
            pl.BlockSpec((nseq, BLK, vals), tok),
            pl.BlockSpec((nseq, BLK, vals), all_tok),
            pl.BlockSpec((nseq, BLK, vals), all_tok),
            pl.BlockSpec((nseq, 1, heads, DK, DV), all_blk),
            pl.BlockSpec((nseq, 1, heads, BLK, BLK), all_blk),
            pl.BlockSpec((CONV, qkv), whole),
            pl.BlockSpec((2, 128), whole),
            pl.BlockSpec((1, DV), whole),
        ],
        out_specs=(
            pl.BlockSpec((nseq, BLK, width), tok),
            pl.BlockSpec((nseq, 1, 8, 128), lambda i, c: (i, blocks - 1 - c, 0, 0)),
            pl.BlockSpec((nseq, BLK, 1), tok),
            pl.BlockSpec((8 * CONV, qkv), whole),
            pl.BlockSpec((16, 128), whole),
            pl.BlockSpec((8, DV), whole),
        ),
        scratch_shapes=[
            pltpu.VMEM((nseq, 8 + BLK, qkv), F32),
            pltpu.VMEM((nseq, BLK + 8, qkv), F32),
            pltpu.VMEM((nseq, heads, DK, DV), F32),
        ],
        compiler_params=pltpu.CompilerParams(dimension_semantics=("arbitrary", "arbitrary")),
        cost_estimate=pl.CostEstimate(
            flops=seqs * length * heads * 10_000_000, bytes_accessed=seqs * length * width * 8,
            transcendentals=0),
        name="mixer_bwd",
    )(proj, proj, dmixed, o, u, states, invs, conv, rates, gain)
    dconv = jnp.sum(dconv.reshape(CONV, 8, qkv), axis=1)
    drate = jnp.sum(drate.reshape(2, 8, 128), axis=1)[:, :heads]
    dgain = jnp.sum(dgain, axis=0)
    return dproj, dots[:, :, 0, :], dot_cols, dconv, drate[0], drate[1], dgain


ROWS = 512


def half_specs(blocks, width):
    half = blocks // 2
    top = pl.BlockSpec((ROWS, width), lambda i, *_: (jnp.minimum(i, half - 1), 0))
    low = pl.BlockSpec((ROWS, width), lambda i, *_: (jnp.maximum(i - half, 0), 0))
    return [top, low]


def piece_specs(blocks, width, count):
    here = [pl.BlockSpec((ROWS, width), lambda i, *_: (i, 0))]
    if count == 5:
        return here * 3 + half_specs(blocks, width)
    return here + half_specs(blocks, width) * 3


def row_spec(width):
    return pl.BlockSpec((ROWS, width), lambda i, *_: (i, 0))


def whole_spec(shape):
    return pl.BlockSpec(shape, lambda i, *_: (0,) * len(shape))


def send_specs(tokens, width):
    shapes = (
        jax.ShapeDtypeStruct((tokens, width), F32),
        jax.ShapeDtypeStruct((3, tokens, width), BF16),
    )
    return shapes, (row_spec(width), pl.BlockSpec((3, ROWS, width), lambda i, *_: (0, i, 0)))


def block_cols(order_ref, b, width):
    return pl.ds(pl.multiple_of(order_ref[b] * width, width), width)


def read_pieces(refs, half):
    upper = pl.program_id(0) < half
    first = 3 if len(refs) == 5 else 1
    halves = [jnp.where(upper, refs[i][...], refs[i + 1][...]) for i in range(first, len(refs), 2)]
    return [ref[...] for ref in refs[:first]] + halves


def norm_into(refs, half, blocks_per_seq, lens_ref, order_ref, gain_ref, normed_ref, scale_ref):
    i = pl.program_id(0)
    pieces = [piece.astype(F32) for piece in read_pieces(refs, half)]
    width = pieces[0].shape[1]
    squares = pieces[0] * pieces[0]
    for piece in pieces[1:]:
        squares = squares + piece * piece
    scale = lax.rsqrt(jnp.sum(squares, axis=1, keepdims=True) * (1.0 / (4 * width)) + NORM_EPS)
    scale_ref[...] = scale
    at = lax.rem(i, blocks_per_seq) * ROWS + iota2((ROWS, 1), 0)
    masked = jnp.where(at < lens_ref[i // blocks_per_seq], scale, 0.0)
    for b, piece in enumerate(pieces):
        cols = block_cols(order_ref, b, width)
        normed_ref[:, cols] = (piece * masked * gain_ref[:, cols]).astype(BF16)


def send_blocks(order_ref, left, w_ref, cols, own_ref, send_ref):
    width = own_ref.shape[1]
    for b in range(4):
        part = nt1(left, w_ref[block_cols(order_ref, b, width), cols])
        if b == 0:
            own_ref[...] = part
        else:
            send_ref[b - 1] = part.astype(BF16)


def project_kernel(half, blocks_per_seq, lens_ref, order_ref, *refs):
    gain_ref, w_ref, proj_ref, normed_ref, scale_ref = refs[5:]
    norm_into(refs[:5], half, blocks_per_seq, lens_ref, order_ref, gain_ref, normed_ref, scale_ref)
    proj_ref[...] = mm1(normed_ref[...], w_ref[...])


def norm_project(pieces, gain, weights, lens, order, length):
    tokens, width = pieces[0].shape
    blocks = tokens // ROWS
    full, out = weights.shape
    return pl.pallas_call(
        functools.partial(project_kernel, blocks // 2, length // ROWS),
        out_shape=(
            jax.ShapeDtypeStruct((tokens, out), F32),
            jax.ShapeDtypeStruct((tokens, full), BF16),
            jax.ShapeDtypeStruct((tokens, 1), F32),
        ),
        grid_spec=pltpu.PrefetchScalarGridSpec(
            num_scalar_prefetch=2,
            grid=(blocks,),
            in_specs=piece_specs(blocks, width, len(pieces)) + [whole_spec((1, full)), whole_spec((full, out))],
            out_specs=(row_spec(out), row_spec(full), row_spec(1)),
        ),
        cost_estimate=pl.CostEstimate(
            flops=2 * tokens * full * out, bytes_accessed=tokens * (out * 4 + full * 4),
            transcendentals=tokens),
        name="norm_project",
    )(lens, order, *pieces, gain, weights)


def spread_kernel(order_ref, left_ref, w_ref, normed_ref, gain_ref, dots_ref, own_ref, send_ref):
    width = own_ref.shape[1]
    left = left_ref[...]
    dots = dots_ref[...] * (1.0 / gain_ref.shape[1])
    for b in range(4):
        at = block_cols(order_ref, b, width)
        gain = gain_ref[:, at]
        part = nt1(left, w_ref[at, :])
        part = part - normed_ref[:, at].astype(F32) * (1.0 / (gain * gain)) * dots
        if b == 0:
            own_ref[...] = part
        else:
            send_ref[b - 1] = part.astype(BF16)


def spread_product(left, weights, order, normed, gain, dots):
    tokens, inner = left.shape
    full = weights.shape[0]
    shapes, specs = send_specs(tokens, full // 4)
    return pl.pallas_call(
        spread_kernel,
        out_shape=shapes,
        grid_spec=pltpu.PrefetchScalarGridSpec(
            num_scalar_prefetch=1,
            grid=(tokens // ROWS,),
            in_specs=[row_spec(inner), whole_spec((full, inner)), row_spec(full),
                      whole_spec((1, full)), row_spec(1)],
            out_specs=specs,
        ),
        cost_estimate=pl.CostEstimate(
            flops=2 * tokens * full * inner, bytes_accessed=tokens * (full * 3 + inner * 2),
            transcendentals=0),
        name="spread_product",
    )(order, left, weights, normed, gain, dots)


def halves_blocks(half, order_ref, left, w_ref, cols, refs, fix=None):
    width = refs[0].shape[1]
    parts = [nt1(left, w_ref[block_cols(order_ref, b, width), cols]) for b in range(4)]
    if fix is not None:
        normed_ref, gain_ref, dots = fix
        for b in range(4):
            at = block_cols(order_ref, b, width)
            gain = gain_ref[:, at]
            parts[b] = parts[b] - normed_ref[:, at].astype(F32) * (1.0 / (gain * gain)) * dots
    refs[0][...] = parts[0]
    upper = pl.program_id(0) < half

    @pl.when(upper)
    def _():
        for b in range(1, 4):
            refs[2 * b - 1][...] = parts[b].astype(BF16)

    @pl.when(jnp.logical_not(upper))
    def _():
        for b in range(1, 4):
            refs[2 * b][...] = parts[b].astype(BF16)


def halves_kernel(half, order_ref, left_ref, w_ref, *refs):
    halves_blocks(half, order_ref, left_ref[...], w_ref, slice(None), refs)


def spread_halves(left, weights, order):
    tokens, inner = left.shape
    full = weights.shape[0]
    blocks = tokens // ROWS
    part = jax.ShapeDtypeStruct((tokens // 2, full // 4), BF16)
    return pl.pallas_call(
        functools.partial(halves_kernel, blocks // 2),
        out_shape=(jax.ShapeDtypeStruct((tokens, full // 4), F32),) + (part,) * 6,
        grid_spec=pltpu.PrefetchScalarGridSpec(
            num_scalar_prefetch=1,
            grid=(blocks,),
            in_specs=[row_spec(inner), whole_spec((full, inner))],
            out_specs=tuple(piece_specs(blocks, full // 4, 7)),
        ),
        cost_estimate=pl.CostEstimate(
            flops=2 * tokens * full * inner, bytes_accessed=tokens * (full * 3 + inner * 2),
            transcendentals=0),
        name="spread_halves",
    )(order, left, weights)


def feed_kernel(half, blocks_per_seq, lens_ref, order_ref, *refs):
    (grad_ref, gain_ref, w_ref, normed_ref, scale_ref, act_ref, both_ref, dots_ref,
     feed_ref, feed_send_ref) = refs[7:17]
    ff = act_ref.shape[1]
    norm_into(refs[:7], half, blocks_per_seq, lens_ref, order_ref, gain_ref, normed_ref, scale_ref)
    gate_up = mm1(normed_ref[...], w_ref[:, : 2 * ff])
    inner_grad = mm1(grad_ref[...], w_ref[:, 2 * ff :])
    gate_act = gate_up[:, :ff]
    up_act = gate_up[:, ff:]
    sig = sigm(gate_act)
    silu = gate_act * sig
    act_ref[...] = (silu * up_act).astype(BF16)
    gate_grad = inner_grad * up_act * (sig * (1.0 + gate_act * (1.0 - sig)))
    up_grad = inner_grad * silu
    both_ref[:, :ff] = gate_grad.astype(BF16)
    both_ref[:, ff:] = up_grad.astype(BF16)
    dots = jnp.sum(gate_grad * gate_act + up_grad * up_act, axis=1, keepdims=True)
    dots_ref[0] = jnp.broadcast_to(dots, (ROWS, 128)).T[0:8]
    halves_blocks(half, order_ref, both_ref[...], w_ref, slice(0, 2 * ff), refs[17:],
                  (normed_ref, gain_ref, dots * (1.0 / gain_ref.shape[1])))
    send_blocks(order_ref, act_ref[...], w_ref, slice(2 * ff, 3 * ff), feed_ref, feed_send_ref)


def feed_forward(pieces, grad_full, gain, weights, lens, order, length):
    tokens, width = pieces[0].shape
    blocks = tokens // ROWS
    full, out = weights.shape
    ff = out // 3
    shapes, specs = send_specs(tokens, width)
    return pl.pallas_call(
        functools.partial(feed_kernel, blocks // 2, length // ROWS),
        out_shape=(
            jax.ShapeDtypeStruct((tokens, full), BF16),
            jax.ShapeDtypeStruct((tokens, 1), F32),
            jax.ShapeDtypeStruct((tokens, ff), BF16),
            jax.ShapeDtypeStruct((tokens, 2 * ff), BF16),
            jax.ShapeDtypeStruct((blocks, 8, ROWS), F32),
        ) + shapes + (
            jax.ShapeDtypeStruct((tokens, width), F32),
        ) + (jax.ShapeDtypeStruct((tokens // 2, width), BF16),) * 6,
        grid_spec=pltpu.PrefetchScalarGridSpec(
            num_scalar_prefetch=2,
            grid=(blocks,),
            in_specs=piece_specs(blocks, width, len(pieces))
            + [row_spec(full), whole_spec((1, full)), whole_spec((full, out))],
            out_specs=(row_spec(full), row_spec(1), row_spec(ff), row_spec(2 * ff),
                       pl.BlockSpec((1, 8, ROWS), lambda i, *_: (i, 0, 0))) + specs
            + tuple(piece_specs(blocks, width, 7)),
        ),
        cost_estimate=pl.CostEstimate(
            flops=4 * tokens * full * out, bytes_accessed=tokens * full * 16,
            transcendentals=tokens * ff),
        name="feed_forward",
    )(lens, order, *pieces, grad_full, gain, weights)


def join_kernel(half, order_ref, *refs):
    w_ref, full_ref, out_ref = refs[7:]
    pieces = read_pieces(refs[:7], half)
    width = pieces[0].shape[1]
    for b, piece in enumerate(pieces):
        full_ref[:, block_cols(order_ref, b, width)] = piece
    out_ref[...] = mm1(full_ref[...], w_ref[...])


def join_product(pieces, weights, order):
    tokens, width = pieces[0].shape
    blocks = tokens // ROWS
    full, out = weights.shape
    return pl.pallas_call(
        functools.partial(join_kernel, blocks // 2),
        out_shape=(
            jax.ShapeDtypeStruct((tokens, full), BF16),
            jax.ShapeDtypeStruct((tokens, out), F32),
        ),
        grid_spec=pltpu.PrefetchScalarGridSpec(
            num_scalar_prefetch=1,
            grid=(blocks,),
            in_specs=piece_specs(blocks, width, len(pieces)) + [whole_spec((full, out))],
            out_specs=(row_spec(full), row_spec(out)),
        ),
        cost_estimate=pl.CostEstimate(
            flops=2 * tokens * full * out, bytes_accessed=tokens * (full * 4 + out * 4),
            transcendentals=0),
        name="join_product",
    )(order, *pieces, weights)


D = 1024
PARTS = 1


def contract_rows(left, right):
    return lax.dot_general(left, right, (((0,), (0,)), ((), ())), preferred_element_type=F32)


def after(value, *others):
    return lax.optimization_barrier((value,) + others)[0]


def xor_perm(size, bit):
    return [(i, i ^ bit) for i in range(size)]


def send_col(values, bit):
    return lax.ppermute(values, "col", xor_perm(4, bit))


def gather_features(values):
    half = values.shape[0] // 2
    from_x = send_col(values, 1)
    from_y = send_col(values, 2)
    far_top = send_col(from_y[:half], 1)
    far_low = send_col(from_x[half:], 2)
    return values, from_x, from_y, far_top, far_low


def sum_features(own, send, *earlier):
    half = own.shape[0] // 2
    via_x = send_col(send[2, :half], 1).astype(F32)
    via_y = send_col(send[2, half:], 2).astype(F32)
    if earlier:
        via_x = after(via_x, *earlier)
        via_y = after(via_y, *earlier)
    part_x = send[0].astype(F32)
    part_y = send[1].astype(F32)
    to_y = jnp.concatenate([part_y[:half] + via_x, part_y[half:]], axis=0).astype(BF16)
    to_x = jnp.concatenate([part_x[:half], part_x[half:] + via_y], axis=0).astype(BF16)
    return own + send_col(to_x, 1).astype(F32) + send_col(to_y, 2).astype(F32)


def sum_direct(own, send):
    total = own
    for bit in range(1, 4):
        total = total + send_col(send[bit - 1], bit).astype(F32)
    return total


def gather_halves(values):
    half = values.shape[0] // 2
    top, low = values[:half], values[half:]
    y_top = send_col(top, 2)
    x_low = send_col(low, 1)
    x_top = send_col(top, 1)
    y_low = send_col(low, 2)
    return values, x_top, x_low, y_top, y_low, send_col(y_top, 1), send_col(x_low, 2)


def sum_halves(own, x_top, x_low, y_top, y_low, far_top, far_low):
    via_x = send_col(far_top, 1).astype(F32)
    via_y = send_col(far_low, 2).astype(F32)
    x_top = send_col(x_top, 1)
    y_low = send_col(y_low, 2)
    x_low = send_col((x_low.astype(F32) + via_y).astype(BF16), 1)
    y_top = send_col((y_top.astype(F32) + via_x).astype(BF16), 2)
    top = x_top.astype(F32) + y_top.astype(F32)
    low = x_low.astype(F32) + y_low.astype(F32)
    return own + jnp.concatenate([top, low], axis=0)


def sum_scalars(values):
    return (values + send_col(values, 1)) + (send_col(values, 2) + send_col(values, 3))


def swap_cores(mine, dp):
    other = lax.ppermute(mine, "dp", [(0, 1), (1, 0)])
    return jnp.where(
        dp == 0, jnp.concatenate([mine, other], axis=0), jnp.concatenate([other, mine], axis=0)
    )


def gather_weight(block, dp, *earlier):
    rows = block.shape[0] // 2
    half = lax.dynamic_slice_in_dim(block, dp * rows, rows, 0)
    if earlier:
        half = after(half, *earlier)
    return lax.all_gather(half, ("row", "dp"), axis=0, tiled=True)


def scatter_weight(grad, dp):
    mine = lax.psum_scatter(grad, ("row", "dp"), scatter_dimension=0, tiled=True)
    return swap_cores(mine, dp).astype(F32)


def sum_small(values):
    count = lax.axis_size("row")
    if count != 4:
        return lax.psum(values, ("dp", "row"))
    size = values.shape[0]
    total = jnp.pad(values, (0, -size % 1024)).reshape(-1, 128)
    total = total + lax.ppermute(total, "dp", [(0, 1), (1, 0)])
    others = [lax.ppermute(total, "row", xor_perm(count, bit)) for bit in range(1, count)]
    return ((total + others[0]) + (others[1] + others[2])).reshape(-1)[:size]


def on_device(
    inputs,
    out_grad,
    seq_lengths,
    first_gain,
    query_proj,
    key_proj,
    value_proj,
    decay_proj,
    beta_proj,
    gate_proj,
    query_conv,
    key_conv,
    value_conv,
    decay_log,
    step_bias,
    output_gain,
    output_proj,
    second_gain,
    hidden_gate,
    hidden_up,
    hidden_down,
):
    seq_count, length, col_width = inputs.shape
    heads = decay_log.shape[0]
    parts = PARTS
    per_part = seq_count // parts
    tokens = per_part * length
    col = lax.axis_index("col")
    dp = lax.axis_index("dp")
    order = (col ^ jnp.arange(4, dtype=jnp.int32)).astype(jnp.int32)
    row_block = query_proj.shape[0]
    vals = heads * DV
    qkv = heads * (2 * DK + DV)
    ff = hidden_gate.shape[1]
    ff_pad = -ff % 128

    in_block = jnp.concatenate(
        [query_proj, key_proj, value_proj, gate_proj, decay_proj, beta_proj,
         jnp.zeros((row_block, 128 - 2 * heads), BF16)], axis=1)
    in_weights = gather_weight(in_block, dp)
    positions = lax.broadcasted_iota(jnp.int32, (seq_count, length), 1)
    valid_all = (positions < seq_lengths[:, None]).astype(F32)
    grad_all = out_grad.astype(F32) * valid_all[:, :, None]
    ff_block = jnp.concatenate(
        [jnp.pad(piece, ((0, 0), (0, ff_pad)))
         for piece in (hidden_gate, hidden_up, hidden_down.T)], axis=1)

    conv = jnp.concatenate([query_conv, key_conv, value_conv], axis=1).astype(F32)
    rates = rate_rows(decay_log, step_bias)
    gain_row = output_gain.astype(F32)[None]
    first_row = first_gain.astype(F32)[None]
    second_row = second_gain.astype(F32)[None]
    first_local = lax.dynamic_slice_in_dim(first_row, col * col_width, col_width, 1)
    second_local = lax.dynamic_slice_in_dim(second_row, col * col_width, col_width, 1)

    state = []
    for part in range(parts):
        seqs = slice(part * per_part, (part + 1) * per_part)
        local = inputs[seqs].reshape(tokens, col_width)
        state.append(dict(
            lens=seq_lengths[seqs], valid=valid_all[seqs].reshape(tokens, 1), local=local,
            grad_out=grad_all[seqs].reshape(tokens, col_width), pieces=gather_features(local)))
    out_weights = gather_weight(output_proj.T, dp, state[0]["pieces"][1])
    for st in state:
        proj, st["normed"], st["scale"] = norm_project(
            st["pieces"], first_row, in_weights, st["lens"], order, length)
        st["proj"] = proj.reshape(per_part, length, -1)
        if st is state[0]:
            grad_low = grad_all.astype(BF16).reshape(seq_count * length, col_width)
            grad_full = lax.all_gather(after(grad_low, st["scale"]), "col", axis=1, tiled=True)
            ff_weights = gather_weight(ff_block, dp, st["scale"])
        mixed, *st["saved"] = mixer_fwd(st["proj"], conv, rates, gain_row, heads, per_part)
        st["mixed"] = mixed.reshape(tokens, vals)
        attention = sum_halves(*spread_halves(st["mixed"], out_weights, order))
        st["hidden"] = st["local"].astype(F32) + attention
        st["pieces"] = gather_halves(st["hidden"].astype(BF16))
    results = []
    gate_up_grad = 0.0
    down_grad = 0.0
    second_gain_grad = 0.0
    for part, st in enumerate(state):
        st["grad_full"] = grad_full[part * tokens : (part + 1) * tokens]
        normed, scale, act, both, dots, feed_own, feed_send, *sends = feed_forward(st["pieces"], st["grad_full"], second_row, ff_weights, st["lens"], order,
                          length)
        dots = sum_scalars(dots)[:, 0, :].reshape(tokens, 1)
        second_grad = sum_halves(*sends) * st["valid"]
        hat = st["hidden"] * scale
        st["hidden_grad"] = st["grad_out"] + scale * (second_grad * second_local)
        st["pieces"] = gather_halves(st["hidden_grad"].astype(BF16))
        hidden, feed_own, feed_send = lax.optimization_barrier(
            (st["hidden"], feed_own, feed_send, st["pieces"][6]))[:3]
        feed = sum_direct(feed_own, feed_send)
        results.append(((hidden + feed) * st["valid"]).astype(BF16))
        second_gain_grad = second_gain_grad + jnp.sum(
            (second_grad + hat * dots / (D * second_local)) * hat, axis=0)
        gate_up_grad = gate_up_grad + contract_rows(normed, both)
        down_grad = down_grad + contract_rows(st["grad_full"], act)
    gate_up_low = gate_up_grad.astype(BF16)
    down_low = down_grad.astype(BF16)
    gate_up_grad = scatter_weight(gate_up_low, dp)
    down_grad = scatter_weight(after(down_low, gate_up_low), dp)
    out_weight_grad = 0.0
    in_weight_grad = 0.0
    first_gain_grad = 0.0
    small = 0.0
    for st in state:
        own = after(st["pieces"][0], gate_up_low, down_low)
        st["attn_grad"], mixed_grad = join_product(
            (own,) + st["pieces"][1:], out_weights, order)
        out_weight_grad = out_weight_grad + contract_rows(st["attn_grad"], st["mixed"])
        if st is state[-1]:
            out_low = out_weight_grad.astype(BF16)
            mixed_grad = after(mixed_grad, out_low)
        dproj, dots, dot_cols, *grads = mixer_bwd(
            st["proj"], mixed_grad.reshape(per_part, length, vals), st["saved"], conv, rates,
            gain_row, heads, per_part, 0)
        small = small + jnp.concatenate([grad.reshape(-1) for grad in grads])
        st["dproj"] = dproj.reshape(tokens, -1)
        st["dots"] = sum_scalars(dots)
        st["dot_cols"] = dot_cols.reshape(tokens, 1)
        in_weight_grad = in_weight_grad + contract_rows(
            st["normed"], after(st["dproj"], *results))
    in_low = in_weight_grad.astype(BF16)
    in_weight_grad = scatter_weight(after(in_low, out_low), dp)
    at = CONV * qkv + 2 * heads
    input_grads = []
    for st in state:
        own, send = spread_product(after(st["dproj"], in_low), in_weights, order, st["normed"],
                                   first_row, st["dot_cols"])
        first_grad = sum_features(own, send) * st["valid"]
        hat = st["local"].astype(F32) * st["scale"]
        total = st["dots"].reshape(tokens, 1)
        first_gain_grad = first_gain_grad + jnp.sum(
            (first_grad + hat * total / (D * first_local)) * hat, axis=0)
        input_grads.append(st["hidden_grad"] + st["scale"] * (first_grad * first_local))
    out_weight_grad = scatter_weight(out_low, dp)
    small_sums = sum_small(
        jnp.concatenate([small[:at], second_gain_grad, small[at:], first_gain_grad]))
    gain_out = sum_scalars(small_sums[at + col_width : at + col_width + DV].reshape(2, 128))
    conv_grad = small_sums[: CONV * qkv].reshape(CONV, qkv)
    gate_at = qkv + vals
    qk = heads * DK
    return (
        jnp.concatenate(results, axis=0).reshape(seq_count, length, col_width),
        jnp.concatenate(input_grads, axis=0).reshape(seq_count, length, col_width),
        small_sums[at + col_width + DV :],
        in_weight_grad[:, :qk],
        in_weight_grad[:, qk : 2 * qk],
        in_weight_grad[:, 2 * qk : qkv],
        in_weight_grad[:, gate_at : gate_at + heads],
        in_weight_grad[:, gate_at + heads : gate_at + 2 * heads],
        in_weight_grad[:, qkv:gate_at],
        conv_grad[:, :qk],
        conv_grad[:, qk : 2 * qk],
        conv_grad[:, 2 * qk :],
        small_sums[CONV * qkv : CONV * qkv + heads],
        small_sums[CONV * qkv + heads : at],
        gain_out.reshape(-1),
        out_weight_grad.T,
        small_sums[at : at + col_width],
        gate_up_grad[:, :ff],
        gate_up_grad[:, ff + ff_pad : 2 * ff + ff_pad],
        down_grad[:, :ff].T,
    )


def solution(mesh):
    in_specs = (
        P(("dp", "row"), None, "col"),
        P(("dp", "row"), None, "col"),
        P(("dp", "row")),
        P(),
        P("row", "col"),
        P("row", "col"),
        P("row", "col"),
        P("row", "col"),
        P("row", "col"),
        P("row", "col"),
        P(None, "col"),
        P(None, "col"),
        P(None, "col"),
        P("col"),
        P("col"),
        P(),
        P("col", "row"),
        P(),
        P("row", "col"),
        P("row", "col"),
        P("col", "row"),
    )
    out_specs = (
        P(("dp", "row"), None, "col"),
        P(("dp", "row"), None, "col"),
        P("col"),
        P("row", "col"),
        P("row", "col"),
        P("row", "col"),
        P("row", "col"),
        P("row", "col"),
        P("row", "col"),
        P(None, "col"),
        P(None, "col"),
        P(None, "col"),
        P("col"),
        P("col"),
        P(),
        P("col", "row"),
        P("col"),
        P("row", "col"),
        P("row", "col"),
        P("col", "row"),
    )
    return jax.shard_map(
        on_device, mesh=mesh, in_specs=in_specs, out_specs=out_specs, check_vma=False
    )
```

```python
import functools
import jax
import jax.numpy as jnp
from jax import lax
from jax.experimental import pallas as pl
from jax.experimental.pallas import tpu as pltpu
from jax.sharding import PartitionSpec as P

DK = 128
DV = 256
CONV = 4
NORM_EPS = 1e-05
UNIT_EPS = 1e-06
BLK = 128
SUB = 32
F32 = jnp.float32
BF16 = jnp.bfloat16


def mm1(a, b):
    return lax.dot_general(a, b, (((1,), (0,)), ((), ())), preferred_element_type=F32)


def nt1(a, b):
    return lax.dot_general(a, b, (((1,), (1,)), ((), ())), preferred_element_type=F32)


def halves(a):
    hi = a.astype(BF16)
    return hi, (a - hi.astype(F32)).astype(BF16)


def mm(a, b):
    ah, al = halves(a)
    bh, bl = halves(b)
    return mm1(jnp.concatenate([ah, al, ah], axis=1), jnp.concatenate([bh, bh, bl], axis=0))


def mm_nt(a, b):
    ah, al = halves(a)
    bh, bl = halves(b)
    return nt1(jnp.concatenate([ah, al, ah], axis=1), jnp.concatenate([bh, bh, bl], axis=1))


def mm_sum(a, b):
    ah, al = halves(a)
    bh, bl = halves(b)
    return mm1(ah, bh) + (mm1(ah, bl) + mm1(al, bh))


def mm_nt_sum(a, b):
    ah, al = halves(a)
    bh, bl = halves(b)
    return nt1(ah, bh) + (nt1(ah, bl) + nt1(al, bh))


def sigm(v):
    return 0.5 * jnp.tanh(0.5 * v) + 0.5


def iota2(shape, axis):
    return lax.broadcasted_iota(jnp.int32, shape, axis)


def unit_lower_inverse(mats):
    groups = BLK // SUB
    lane = iota2((SUB, BLK), 1)
    sub = iota2((SUB, BLK), 0)
    lane_group = lane // SUB
    solved = []
    for b in range(groups):
        rows = slice(b * SUB, (b + 1) * SUB)
        packed = jnp.zeros((SUB, BLK), F32)
        for p, mat in enumerate(mats):
            piece = mat[rows]
            shift = (SUB * (p - b)) % BLK
            if shift:
                piece = pltpu.roll(piece, shift, 1)
            packed = jnp.where(lane_group == p, piece, packed)
        acc = jnp.where(lane - lane_group * SUB == sub, 1.0, 0.0).astype(F32)
        tiles = [acc[8 * t : 8 * t + 8] for t in range(SUB // 8)]
        coefs = [packed[8 * t : 8 * t + 8] for t in range(SUB // 8)]
        base = (iota2((8, BLK), 1) // SUB) * SUB
        for j in range(SUB - 1):
            row = jnp.broadcast_to(tiles[j // 8][j % 8 : j % 8 + 1], (8, BLK))
            for t in range((j + 1) // 8, SUB // 8):
                col = jnp.take_along_axis(coefs[t], base + j, axis=1)
                tiles[t] = tiles[t] - col * row
        solved.append(jnp.concatenate(tiles, axis=0))
    out = []
    row_i = iota2((BLK, BLK), 0)
    col_i = iota2((BLK, BLK), 1)
    for p, mat in enumerate(mats):
        blocks = []
        for b in range(groups):
            piece = solved[b]
            shift = (SUB * (b - p)) % BLK
            if shift:
                piece = pltpu.roll(piece, shift, 1)
            blocks.append(jnp.where(lane_group == b, piece, 0.0))
        inv = jnp.concatenate(blocks, axis=0)
        zero32 = jnp.zeros((SUB, BLK), F32)
        off = jnp.where((row_i // 64 == col_i // 64) & (row_i // SUB > col_i // SUB), mat, 0.0)
        lhs = jnp.concatenate([off[32:64], off[96:128]], axis=0)
        part = mm(lhs, inv)
        placed = jnp.concatenate([zero32, part[:32], zero32, part[32:]], axis=0)
        lhs = jnp.concatenate([inv[32:64], inv[96:128]], axis=0)
        part = mm(lhs, placed)
        inv = inv - jnp.concatenate([zero32, part[:32], zero32, part[32:]], axis=0)
        off = jnp.where(col_i[64:] < 64, mat[64:], 0.0)
        part = mm(off, inv)
        zero64 = jnp.zeros((64, BLK), F32)
        part = mm(inv[64:], jnp.concatenate([zero64, part], axis=0))
        inv = jnp.concatenate([inv[:64], inv[64:] - part], axis=0)
        out.append(inv)
    return out


def decay_terms(ab, neg_rate, bias, heads):
    pre = ab + bias
    soft = jnp.maximum(pre, 0.0) + jnp.log(1.0 + jnp.exp(-jnp.abs(pre)))
    log_decay = neg_rate * soft
    beta = sigm(ab)
    row_i = iota2((BLK, BLK), 0)
    col_i = iota2((BLK, BLK), 1)
    tri = jnp.where(row_i >= col_i, 1.0, 0.0).astype(BF16)
    hi = log_decay.astype(BF16)
    rest = log_decay - hi.astype(F32)
    mid = rest.astype(BF16)
    low = (rest - mid.astype(F32)).astype(BF16)
    cum = mm1(tri, hi) + (mm1(tri, mid) + mm1(tri, low))
    return log_decay, beta, cum


def conv_taps(xs_ref, s, kernel):
    pre = xs_ref[s, 5 : 5 + BLK, :] * kernel[0:1]
    for i in range(1, CONV):
        pre = pre + xs_ref[s, 5 + i : 5 + i + BLK, :] * kernel[i : i + 1]
    return pre


def fwd_kernel(heads, nseq, proj_ref, conv_ref, rate_ref, gain_ref,
               mixed_ref, o_ref, u_ref, s_ref, t_ref, xs_ref, state_ref):
    qkv = heads * (2 * DK + DV)
    gate_at = qkv
    ab_at = qkv + heads * DV
    step = pl.program_id(1)

    @pl.when(step == 0)
    def _():
        xs_ref[:, 0:8, :] = jnp.zeros((nseq, 8, qkv), F32)
        state_ref[...] = jnp.zeros_like(state_ref)

    row_i = iota2((BLK, BLK), 0)
    col_i = iota2((BLK, BLK), 1)
    kernel = conv_ref[...]
    neg_rate = rate_ref[0:1]
    bias = rate_ref[1:2]
    gain = gain_ref[...]
    items = []
    for s in range(nseq):
        xs_ref[s, 8 : 8 + BLK, :] = proj_ref[s, :, 0:qkv]
        pre = conv_taps(xs_ref, s, kernel)
        xs_ref[s, 0:8, :] = xs_ref[s, BLK : BLK + 8, :]
        act = pre * sigm(pre)
        ab = proj_ref[s, :, ab_at : ab_at + 128]
        _, beta_all, cum_all = decay_terms(ab, neg_rate, bias, heads)
        cum_t = cum_all.T
        for h in range(heads):
            q = act[:, h * DK : (h + 1) * DK]
            k = act[:, (heads + h) * DK : (heads + h + 1) * DK]
            v = act[:, 2 * heads * DK + h * DV : 2 * heads * DK + (h + 1) * DV]
            qn = q * (lax.rsqrt(jnp.sum(q * q, axis=1, keepdims=True) + UNIT_EPS) * DK ** -0.5)
            kn = k * lax.rsqrt(jnp.sum(k * k, axis=1, keepdims=True) + UNIT_EPS)
            cum = cum_all[:, h : h + 1]
            cum_row = cum_t[h : h + 1, :]
            beta = beta_all[:, heads + h : heads + h + 1]
            ratio = jnp.exp(jnp.where(row_i >= col_i, cum - cum_row, -1e30))
            kb = kn
            kq = jnp.concatenate([kb, qn], axis=0)
            gram = mm_nt(kq, kb)
            a = jnp.where(row_i > col_i, gram[:BLK] * ratio * beta, 0.0)
            p = gram[BLK:] * ratio
            last = cum[BLK - 1 : BLK]
            kd = kn * jnp.exp(last - cum)
            items.append((s, h, kq, a, p, kd, v, beta, jnp.exp(cum), jnp.exp(last)))
    invs = []
    for at in range(0, len(items), 4):
        invs = invs + unit_lower_inverse([item[3] for item in items[at : at + 4]])
    for item, inv in zip(items, invs):
        s, h, kq, a, p, kd, v, beta, ecum, elast = item
        state = state_ref[s, h]
        low_state = state
        ks_qs = mm(kq, low_state)
        x = beta * (v - ecum * ks_qs[:BLK])
        inv_low = inv
        u = mm(inv_low, x)
        pk = jnp.concatenate([p, kd.T], axis=0)
        pu = mm(pk, u)
        o = ecum * ks_qs[BLK:] + pu[:BLK]
        state_ref[s, h] = elast * state + pu[BLK:]
        s_ref[s, 0, h] = low_state
        t_ref[s, 0, h] = inv_low
        cols = slice(h * DV, (h + 1) * DV)
        u_ref[s, :, cols] = u
        o_ref[s, :, cols] = o
        g = proj_ref[s, :, gate_at + h * DV : gate_at + (h + 1) * DV]
        norm = o * lax.rsqrt(jnp.mean(o * o, axis=1, keepdims=True) + NORM_EPS)
        mixed_ref[s, :, cols] = (norm * gain * (g * sigm(g))).astype(BF16)


def rate_rows(decay_log, step_bias):
    heads = decay_log.shape[0]
    pad = 128 - heads
    return jnp.stack([jnp.pad(-jnp.exp(decay_log), (0, pad)), jnp.pad(step_bias, (0, pad))])


def mixer_fwd(proj, conv, rates, gain, heads, nseq):
    seqs, length, width = proj.shape
    blocks = length // BLK
    qkv = heads * (2 * DK + DV)
    vals = heads * DV
    tok = lambda i, c: (i, c, 0)
    return pl.pallas_call(
        functools.partial(fwd_kernel, heads, nseq),
        out_shape=(
            jax.ShapeDtypeStruct((seqs, length, vals), BF16),
            jax.ShapeDtypeStruct((seqs, length, vals), F32),
            jax.ShapeDtypeStruct((seqs, length, vals), F32),
            jax.ShapeDtypeStruct((seqs, blocks, heads, DK, DV), F32),
            jax.ShapeDtypeStruct((seqs, blocks, heads, BLK, BLK), F32),
        ),
        grid=(seqs // nseq, blocks),
        in_specs=[
            pl.BlockSpec((nseq, BLK, width), tok),
            pl.BlockSpec((CONV, qkv), lambda i, c: (0, 0)),
            pl.BlockSpec((2, 128), lambda i, c: (0, 0)),
            pl.BlockSpec((1, DV), lambda i, c: (0, 0)),
        ],
        out_specs=(
            pl.BlockSpec((nseq, BLK, vals), tok),
            pl.BlockSpec((nseq, BLK, vals), tok),
            pl.BlockSpec((nseq, BLK, vals), tok),
            pl.BlockSpec((nseq, 1, heads, DK, DV), lambda i, c: (i, c, 0, 0, 0)),
            pl.BlockSpec((nseq, 1, heads, BLK, BLK), lambda i, c: (i, c, 0, 0, 0)),
        ),
        scratch_shapes=[
            pltpu.VMEM((nseq, 8 + BLK, qkv), F32),
            pltpu.VMEM((nseq, heads, DK, DV), F32),
        ],
        compiler_params=pltpu.CompilerParams(dimension_semantics=("arbitrary", "arbitrary")),
        cost_estimate=pl.CostEstimate(
            flops=seqs * length * heads * 6_000_000, bytes_accessed=seqs * length * width * 8,
            transcendentals=0),
        name="mixer_fwd",
    )(proj, conv, rates, gain)


def colsum(v):
    return jnp.sum(v.reshape(v.shape[0] // 8, 8, v.shape[1]), axis=0)


def bwd_kernel(heads, nseq, proj_ref, prev_ref, dmix_ref, o_ref, u_ref, s_ref, t_ref,
               conv_ref, rate_ref, gain_ref,
               dproj_ref, dots_ref, dotc_ref, dconv_ref, drate_ref, dgain_ref, xs_ref, ds_ref, dstate_ref):
    qkv = heads * (2 * DK + DV)
    gate_at = qkv
    ab_at = qkv + heads * DV
    step = pl.program_id(1)
    first = pl.num_programs(1) - 1

    @pl.when(step == 0)
    def _():
        ds_ref[:, BLK : BLK + 8, :] = jnp.zeros((nseq, 8, qkv), F32)
        dstate_ref[...] = jnp.zeros_like(dstate_ref)

    @pl.when((step == 0) & (pl.program_id(0) == 0))
    def _():
        dconv_ref[...] = jnp.zeros_like(dconv_ref)
        drate_ref[...] = jnp.zeros_like(drate_ref)
        dgain_ref[...] = jnp.zeros_like(dgain_ref)

    row_i = iota2((BLK, BLK), 0)
    col_i = iota2((BLK, BLK), 1)
    lower = row_i >= col_i
    strict = row_i > col_i
    kernel = conv_ref[...]
    neg_rate = rate_ref[0:1]
    bias = rate_ref[1:2]
    gain = gain_ref[...]
    has_prev = jnp.where(step == first, 0.0, 1.0).astype(F32)
    lane1 = iota2((1, 128), 1)
    for s in range(nseq):
        xs_ref[s, 0:8, :] = prev_ref[s, :, 0:qkv] * has_prev
        xs_ref[s, 8 : 8 + BLK, :] = proj_ref[s, :, 0:qkv]
        pre = conv_taps(xs_ref, s, kernel)
        sig = sigm(pre)
        act = pre * sig
        dsilu = sig * (1.0 + pre * (1.0 - sig))
        ab = proj_ref[s, :, ab_at : ab_at + 128]
        log_decay, beta_all, cum_all = decay_terms(ab, neg_rate, bias, heads)
        cum_t = cum_all.T
        dots = jnp.zeros((BLK, 1), F32)
        dcum_all = jnp.zeros((BLK, 128), F32)
        dbeta_all = jnp.zeros((BLK, 128), F32)
        dact = [None] * (3 * heads)
        for h in range(heads):
            q = act[:, h * DK : (h + 1) * DK]
            k = act[:, (heads + h) * DK : (heads + h + 1) * DK]
            v = act[:, 2 * heads * DK + h * DV : 2 * heads * DK + (h + 1) * DV]
            rq = lax.rsqrt(jnp.sum(q * q, axis=1, keepdims=True) + UNIT_EPS)
            rk = lax.rsqrt(jnp.sum(k * k, axis=1, keepdims=True) + UNIT_EPS)
            qh = q * rq
            qn = qh * DK ** -0.5
            kn = k * rk
            cum = cum_all[:, h : h + 1]
            cum_row = cum_t[h : h + 1, :]
            beta = beta_all[:, heads + h : heads + h + 1]
            ecum = jnp.exp(cum)
            last = cum[BLK - 1 : BLK]
            elast = jnp.exp(last)
            ratio = jnp.exp(jnp.where(lower, cum - cum_row, -1e30))
            ktail = jnp.exp(last - cum)
            kb = kn
            qb = qn
            gram = mm_nt_sum(jnp.concatenate([kb, qb], axis=0), kb)
            sfac = jnp.where(strict, ratio * beta, 0.0)
            kgr = gram[:BLK]
            p = gram[BLK:] * ratio
            cols = slice(h * DV, (h + 1) * DV)
            o = o_ref[s, :, cols]
            g = proj_ref[s, :, gate_at + h * DV : gate_at + (h + 1) * DV]
            dm = dmix_ref[s, :, cols].astype(F32)
            ro = lax.rsqrt(jnp.mean(o * o, axis=1, keepdims=True) + NORM_EPS)
            n = o * ro
            gs = sigm(g)
            gsil = g * gs
            dmn = dm * n
            dgain_ref[...] += colsum(dmn * gsil)
            dgate = dmn * gain * (gs * (1.0 + g * (1.0 - gs)))
            dproj_ref[s, :, gate_at + h * DV : gate_at + (h + 1) * DV] = dgate.astype(BF16)
            dots = dots + jnp.sum(dgate * g, axis=1, keepdims=True)
            dn = dm * gain * gsil
            do = ro * (dn - n * jnp.mean(dn * n, axis=1, keepdims=True))
            dob = do
            dstate = dstate_ref[s, h]
            dstb = dstate
            u = u_ref[s, :, cols]
            sb = s_ref[s, 0, h]
            tinv = t_ref[s, 0, h]
            kd = kn * ktail
            du = mm_sum(jnp.concatenate([p.T, kd], axis=1), jnp.concatenate([dob, dstb], axis=0))
            dx = mm_sum(tinv.astype(F32).T, du)
            dxb = dx
            ddx = jnp.concatenate([dob, dxb], axis=0)
            both = mm_nt_sum(ddx, jnp.concatenate([sb, u], axis=0))
            be = beta * ecum
            z = both[BLK:, :DK]
            dqi = ecum * both[:BLK, :DK]
            dki = -be * z
            dks = -be * dx
            lhs = jnp.concatenate([qn.T, kn.T], axis=1)
            rhs = jnp.concatenate([(ecum * do), dks], axis=0)
            dstate_ref[s, h] = elast * dstate + mm_sum(lhs, rhs)
            dkd = mm_nt_sum(u, dstb)
            dp = both[:BLK, DK:]
            da = -both[BLK:, DK:]
            dqk = dp * ratio
            dkg = da * sfac
            dlog = dp * p + dkg * kgr
            pair = jnp.concatenate([dqk, dkg + dkg.T], axis=0)
            prod = mm_sum(pair, kb)
            dqn = dqi + prod[:BLK]
            dkn = dki + prod[BLK:] + mm_sum(dqk.T, qb) + dkd * ktail
            kz = jnp.sum(kn * z, axis=1, keepdims=True)
            dkdk = jnp.sum(dkd * kd, axis=1, keepdims=True)
            row_sum = jnp.sum(dlog, axis=1, keepdims=True)
            col_sum = jnp.sum(dlog.T, axis=1, keepdims=True)
            dcum = row_sum - col_sum + jnp.sum(qn * dqi, axis=1, keepdims=True) - be * kz - dkdk
            tail = jnp.sum(dkdk, axis=0, keepdims=True) + elast * jnp.sum(
                jnp.sum(sb.astype(F32) * dstate, axis=1, keepdims=True), axis=0, keepdims=True)
            dcum = dcum + jnp.where(row_i[:, 0:1] == BLK - 1, tail, 0.0)
            kgl = jnp.sum(da * jnp.where(strict, ratio * kgr, 0.0), axis=1, keepdims=True)
            dbeta = jnp.sum(dx * v, axis=1, keepdims=True) - ecum * kz + kgl
            dcum_all = jnp.where(lane1 == h, dcum, dcum_all)
            dbeta_all = jnp.where(lane1 == heads + h, dbeta, dbeta_all)
            dact[h] = (DK ** -0.5 * rq) * (dqn - qh * jnp.sum(dqn * qh, axis=1, keepdims=True))
            dact[heads + h] = rk * (dkn - kn * jnp.sum(dkn * kn, axis=1, keepdims=True))
            dact[2 * heads + h] = beta * dx
        tri = jnp.where(col_i >= row_i, 1.0, 0.0).astype(BF16)
        hi, lo = halves(dcum_all)
        dlog_decay = mm1(tri, hi) + mm1(tri, lo)
        dpre_a = dlog_decay * neg_rate * sigm(ab + bias)
        dpre_b = dbeta_all * beta_all * (1.0 - beta_all)
        dproj_ref[s, :, ab_at : ab_at + 128] = (dpre_a + dpre_b).astype(BF16)
        dots = dots + jnp.sum((dpre_a + dpre_b) * ab, axis=1, keepdims=True)
        drate_ref[0:8, :] += colsum(dlog_decay * log_decay)
        drate_ref[8:16, :] += colsum(dpre_a)
        dpre = jnp.concatenate(dact, axis=1) * dsilu
        ds_ref[s, 0:BLK, :] = dpre
        dx_in = ds_ref[s, 3 : 3 + BLK, :] * kernel[0:1]
        for i in range(1, CONV):
            dx_in = dx_in + ds_ref[s, 3 - i : 3 - i + BLK, :] * kernel[i : i + 1]
        dproj_ref[s, :, 0:qkv] = dx_in.astype(BF16)
        dots = dots + jnp.sum(dx_in * xs_ref[s, 8 : 8 + BLK, :], axis=1, keepdims=True)
        dotc_ref[s] = dots
        dots_ref[s, 0] = jnp.broadcast_to(dots, (BLK, 128)).T[0:8]
        for i in range(CONV):
            dconv_ref[8 * i : 8 * i + 8, :] += colsum(dpre * xs_ref[s, 5 + i : 5 + i + BLK, :])
        ds_ref[s, BLK : BLK + 8, :] = ds_ref[s, 0:8, :]


def mixer_bwd(proj, dmixed, saved, conv, rates, gain, heads, nseq, seq):
    o, u, states, invs = saved
    _, length, width = proj.shape
    seqs = dmixed.shape[0]
    first = seq // nseq
    blocks = length // BLK
    qkv = heads * (2 * DK + DV)
    vals = heads * DV
    tok = lambda i, c: (i, blocks - 1 - c, 0)
    all_tok = lambda i, c: (i + first, blocks - 1 - c, 0)
    all_blk = lambda i, c: (i + first, blocks - 1 - c, 0, 0, 0)
    whole = lambda i, c: (0, 0)
    dproj, dots, dot_cols, dconv, drate, dgain = pl.pallas_call(
        functools.partial(bwd_kernel, heads, nseq),
        out_shape=(
            jax.ShapeDtypeStruct((seqs, length, width), BF16),
            jax.ShapeDtypeStruct((seqs, blocks, 8, 128), F32),
            jax.ShapeDtypeStruct((seqs, length, 1), F32),
            jax.ShapeDtypeStruct((8 * CONV, qkv), F32),
            jax.ShapeDtypeStruct((16, 128), F32),
            jax.ShapeDtypeStruct((8, DV), F32),
        ),
        grid=(seqs // nseq, blocks),
        in_specs=[
            pl.BlockSpec((nseq, BLK, width), all_tok),
            pl.BlockSpec((nseq, 8, qkv), lambda i, c: (
                i + first, jnp.maximum((blocks - 1 - c) * (BLK // 8) - 1, 0), 0)),
            pl.BlockSpec((nseq, BLK, vals), tok),
            pl.BlockSpec((nseq, BLK, vals), all_tok),
            pl.BlockSpec((nseq, BLK, vals), all_tok),
            pl.BlockSpec((nseq, 1, heads, DK, DV), all_blk),
            pl.BlockSpec((nseq, 1, heads, BLK, BLK), all_blk),
            pl.BlockSpec((CONV, qkv), whole),
            pl.BlockSpec((2, 128), whole),
            pl.BlockSpec((1, DV), whole),
        ],
        out_specs=(
            pl.BlockSpec((nseq, BLK, width), tok),
            pl.BlockSpec((nseq, 1, 8, 128), lambda i, c: (i, blocks - 1 - c, 0, 0)),
            pl.BlockSpec((nseq, BLK, 1), tok),
            pl.BlockSpec((8 * CONV, qkv), whole),
            pl.BlockSpec((16, 128), whole),
            pl.BlockSpec((8, DV), whole),
        ),
        scratch_shapes=[
            pltpu.VMEM((nseq, 8 + BLK, qkv), F32),
            pltpu.VMEM((nseq, BLK + 8, qkv), F32),
            pltpu.VMEM((nseq, heads, DK, DV), F32),
        ],
        compiler_params=pltpu.CompilerParams(dimension_semantics=("arbitrary", "arbitrary")),
        cost_estimate=pl.CostEstimate(
            flops=seqs * length * heads * 10_000_000, bytes_accessed=seqs * length * width * 8,
            transcendentals=0),
        name="mixer_bwd",
    )(proj, proj, dmixed, o, u, states, invs, conv, rates, gain)
    dconv = jnp.sum(dconv.reshape(CONV, 8, qkv), axis=1)
    drate = jnp.sum(drate.reshape(2, 8, 128), axis=1)[:, :heads]
    dgain = jnp.sum(dgain, axis=0)
    return dproj, dots[:, :, 0, :], dot_cols, dconv, drate[0], drate[1], dgain


ROWS = 512


def half_specs(blocks, width):
    half = blocks // 2
    top = pl.BlockSpec((ROWS, width), lambda i, *_: (jnp.minimum(i, half - 1), 0))
    low = pl.BlockSpec((ROWS, width), lambda i, *_: (jnp.maximum(i - half, 0), 0))
    return [top, low]


def piece_specs(blocks, width, count):
    here = [pl.BlockSpec((ROWS, width), lambda i, *_: (i, 0))]
    if count == 5:
        return here * 3 + half_specs(blocks, width)
    return here + half_specs(blocks, width) * 3


def row_spec(width):
    return pl.BlockSpec((ROWS, width), lambda i, *_: (i, 0))


def whole_spec(shape):
    return pl.BlockSpec(shape, lambda i, *_: (0,) * len(shape))


def send_specs(tokens, width):
    shapes = (
        jax.ShapeDtypeStruct((tokens, width), F32),
        jax.ShapeDtypeStruct((3, tokens, width), BF16),
    )
    return shapes, (row_spec(width), pl.BlockSpec((3, ROWS, width), lambda i, *_: (0, i, 0)))


def block_cols(order_ref, b, width):
    return pl.ds(pl.multiple_of(order_ref[b] * width, width), width)


def read_pieces(refs, half):
    upper = pl.program_id(0) < half
    first = 3 if len(refs) == 5 else 1
    halves = [jnp.where(upper, refs[i][...], refs[i + 1][...]) for i in range(first, len(refs), 2)]
    return [ref[...] for ref in refs[:first]] + halves


def norm_into(refs, half, blocks_per_seq, lens_ref, order_ref, gain_ref, normed_ref, scale_ref):
    i = pl.program_id(0)
    pieces = [piece.astype(F32) for piece in read_pieces(refs, half)]
    width = pieces[0].shape[1]
    squares = pieces[0] * pieces[0]
    for piece in pieces[1:]:
        squares = squares + piece * piece
    scale = lax.rsqrt(jnp.sum(squares, axis=1, keepdims=True) * (1.0 / (4 * width)) + NORM_EPS)
    scale_ref[...] = scale
    at = lax.rem(i, blocks_per_seq) * ROWS + iota2((ROWS, 1), 0)
    masked = jnp.where(at < lens_ref[i // blocks_per_seq], scale, 0.0)
    for b, piece in enumerate(pieces):
        cols = block_cols(order_ref, b, width)
        normed_ref[:, cols] = (piece * masked * gain_ref[:, cols]).astype(BF16)


def send_blocks(order_ref, left, w_ref, cols, own_ref, send_ref):
    width = own_ref.shape[1]
    for b in range(4):
        part = nt1(left, w_ref[block_cols(order_ref, b, width), cols])
        if b == 0:
            own_ref[...] = part
        else:
            send_ref[b - 1] = part.astype(BF16)


def project_kernel(half, blocks_per_seq, lens_ref, order_ref, *refs):
    gain_ref, w_ref, proj_ref, normed_ref, scale_ref = refs[5:]
    norm_into(refs[:5], half, blocks_per_seq, lens_ref, order_ref, gain_ref, normed_ref, scale_ref)
    proj_ref[...] = mm1(normed_ref[...], w_ref[...])


def norm_project(pieces, gain, weights, lens, order, length):
    tokens, width = pieces[0].shape
    blocks = tokens // ROWS
    full, out = weights.shape
    return pl.pallas_call(
        functools.partial(project_kernel, blocks // 2, length // ROWS),
        out_shape=(
            jax.ShapeDtypeStruct((tokens, out), F32),
            jax.ShapeDtypeStruct((tokens, full), BF16),
            jax.ShapeDtypeStruct((tokens, 1), F32),
        ),
        grid_spec=pltpu.PrefetchScalarGridSpec(
            num_scalar_prefetch=2,
            grid=(blocks,),
            in_specs=piece_specs(blocks, width, len(pieces)) + [whole_spec((1, full)), whole_spec((full, out))],
            out_specs=(row_spec(out), row_spec(full), row_spec(1)),
        ),
        cost_estimate=pl.CostEstimate(
            flops=2 * tokens * full * out, bytes_accessed=tokens * (out * 4 + full * 4),
            transcendentals=tokens),
        name="norm_project",
    )(lens, order, *pieces, gain, weights)


def spread_kernel(order_ref, left_ref, w_ref, normed_ref, gain_ref, dots_ref, own_ref, send_ref):
    width = own_ref.shape[1]
    left = left_ref[...]
    dots = dots_ref[...] * (1.0 / gain_ref.shape[1])
    for b in range(4):
        at = block_cols(order_ref, b, width)
        gain = gain_ref[:, at]
        part = nt1(left, w_ref[at, :])
        part = part - normed_ref[:, at].astype(F32) * (1.0 / (gain * gain)) * dots
        if b == 0:
            own_ref[...] = part
        else:
            send_ref[b - 1] = part.astype(BF16)


def spread_product(left, weights, order, normed, gain, dots):
    tokens, inner = left.shape
    full = weights.shape[0]
    shapes, specs = send_specs(tokens, full // 4)
    return pl.pallas_call(
        spread_kernel,
        out_shape=shapes,
        grid_spec=pltpu.PrefetchScalarGridSpec(
            num_scalar_prefetch=1,
            grid=(tokens // ROWS,),
            in_specs=[row_spec(inner), whole_spec((full, inner)), row_spec(full),
                      whole_spec((1, full)), row_spec(1)],
            out_specs=specs,
        ),
        cost_estimate=pl.CostEstimate(
            flops=2 * tokens * full * inner, bytes_accessed=tokens * (full * 3 + inner * 2),
            transcendentals=0),
        name="spread_product",
    )(order, left, weights, normed, gain, dots)


def halves_blocks(half, order_ref, left, w_ref, cols, refs, fix=None):
    width = refs[0].shape[1]
    parts = [nt1(left, w_ref[block_cols(order_ref, b, width), cols]) for b in range(4)]
    if fix is not None:
        normed_ref, gain_ref, dots = fix
        for b in range(4):
            at = block_cols(order_ref, b, width)
            gain = gain_ref[:, at]
            parts[b] = parts[b] - normed_ref[:, at].astype(F32) * (1.0 / (gain * gain)) * dots
    refs[0][...] = parts[0]
    upper = pl.program_id(0) < half

    @pl.when(upper)
    def _():
        for b in range(1, 4):
            refs[2 * b - 1][...] = parts[b].astype(BF16)

    @pl.when(jnp.logical_not(upper))
    def _():
        for b in range(1, 4):
            refs[2 * b][...] = parts[b].astype(BF16)


def halves_kernel(half, order_ref, left_ref, w_ref, *refs):
    halves_blocks(half, order_ref, left_ref[...], w_ref, slice(None), refs)


def spread_halves(left, weights, order):
    tokens, inner = left.shape
    full = weights.shape[0]
    blocks = tokens // ROWS
    part = jax.ShapeDtypeStruct((tokens // 2, full // 4), BF16)
    return pl.pallas_call(
        functools.partial(halves_kernel, blocks // 2),
        out_shape=(jax.ShapeDtypeStruct((tokens, full // 4), F32),) + (part,) * 6,
        grid_spec=pltpu.PrefetchScalarGridSpec(
            num_scalar_prefetch=1,
            grid=(blocks,),
            in_specs=[row_spec(inner), whole_spec((full, inner))],
            out_specs=tuple(piece_specs(blocks, full // 4, 7)),
        ),
        cost_estimate=pl.CostEstimate(
            flops=2 * tokens * full * inner, bytes_accessed=tokens * (full * 3 + inner * 2),
            transcendentals=0),
        name="spread_halves",
    )(order, left, weights)


def feed_kernel(half, blocks_per_seq, lens_ref, order_ref, *refs):
    (grad_ref, gain_ref, w_ref, normed_ref, scale_ref, act_ref, both_ref, dots_ref,
     feed_ref, feed_send_ref) = refs[7:17]
    ff = act_ref.shape[1]
    norm_into(refs[:7], half, blocks_per_seq, lens_ref, order_ref, gain_ref, normed_ref, scale_ref)
    gate_up = mm1(normed_ref[...], w_ref[:, : 2 * ff])
    inner_grad = mm1(grad_ref[...], w_ref[:, 2 * ff :])
    gate_act = gate_up[:, :ff]
    up_act = gate_up[:, ff:]
    sig = sigm(gate_act)
    silu = gate_act * sig
    act_ref[...] = (silu * up_act).astype(BF16)
    gate_grad = inner_grad * up_act * (sig * (1.0 + gate_act * (1.0 - sig)))
    up_grad = inner_grad * silu
    both_ref[:, :ff] = gate_grad.astype(BF16)
    both_ref[:, ff:] = up_grad.astype(BF16)
    dots = jnp.sum(gate_grad * gate_act + up_grad * up_act, axis=1, keepdims=True)
    dots_ref[0] = jnp.broadcast_to(dots, (ROWS, 128)).T[0:8]
    halves_blocks(half, order_ref, both_ref[...], w_ref, slice(0, 2 * ff), refs[17:],
                  (normed_ref, gain_ref, dots * (1.0 / gain_ref.shape[1])))
    send_blocks(order_ref, act_ref[...], w_ref, slice(2 * ff, 3 * ff), feed_ref, feed_send_ref)


def feed_forward(pieces, grad_full, gain, weights, lens, order, length):
    tokens, width = pieces[0].shape
    blocks = tokens // ROWS
    full, out = weights.shape
    ff = out // 3
    shapes, specs = send_specs(tokens, width)
    return pl.pallas_call(
        functools.partial(feed_kernel, blocks // 2, length // ROWS),
        out_shape=(
            jax.ShapeDtypeStruct((tokens, full), BF16),
            jax.ShapeDtypeStruct((tokens, 1), F32),
            jax.ShapeDtypeStruct((tokens, ff), BF16),
            jax.ShapeDtypeStruct((tokens, 2 * ff), BF16),
            jax.ShapeDtypeStruct((blocks, 8, ROWS), F32),
        ) + shapes + (
            jax.ShapeDtypeStruct((tokens, width), F32),
        ) + (jax.ShapeDtypeStruct((tokens // 2, width), BF16),) * 6,
        grid_spec=pltpu.PrefetchScalarGridSpec(
            num_scalar_prefetch=2,
            grid=(blocks,),
            in_specs=piece_specs(blocks, width, len(pieces))
            + [row_spec(full), whole_spec((1, full)), whole_spec((full, out))],
            out_specs=(row_spec(full), row_spec(1), row_spec(ff), row_spec(2 * ff),
                       pl.BlockSpec((1, 8, ROWS), lambda i, *_: (i, 0, 0))) + specs
            + tuple(piece_specs(blocks, width, 7)),
        ),
        cost_estimate=pl.CostEstimate(
            flops=4 * tokens * full * out, bytes_accessed=tokens * full * 16,
            transcendentals=tokens * ff),
        name="feed_forward",
    )(lens, order, *pieces, grad_full, gain, weights)


def join_kernel(half, order_ref, *refs):
    w_ref, full_ref, out_ref = refs[7:]
    pieces = read_pieces(refs[:7], half)
    width = pieces[0].shape[1]
    for b, piece in enumerate(pieces):
        full_ref[:, block_cols(order_ref, b, width)] = piece
    out_ref[...] = mm1(full_ref[...], w_ref[...])


def join_product(pieces, weights, order):
    tokens, width = pieces[0].shape
    blocks = tokens // ROWS
    full, out = weights.shape
    return pl.pallas_call(
        functools.partial(join_kernel, blocks // 2),
        out_shape=(
            jax.ShapeDtypeStruct((tokens, full), BF16),
            jax.ShapeDtypeStruct((tokens, out), F32),
        ),
        grid_spec=pltpu.PrefetchScalarGridSpec(
            num_scalar_prefetch=1,
            grid=(blocks,),
            in_specs=piece_specs(blocks, width, len(pieces)) + [whole_spec((full, out))],
            out_specs=(row_spec(full), row_spec(out)),
        ),
        cost_estimate=pl.CostEstimate(
            flops=2 * tokens * full * out, bytes_accessed=tokens * (full * 4 + out * 4),
            transcendentals=0),
        name="join_product",
    )(order, *pieces, weights)


D = 1024
PARTS = 1


def contract_rows(left, right):
    return lax.dot_general(left, right, (((0,), (0,)), ((), ())), preferred_element_type=F32)


def after(value, *others):
    return lax.optimization_barrier((value,) + others)[0]


def xor_perm(size, bit):
    return [(i, i ^ bit) for i in range(size)]


def send_col(values, bit):
    return lax.ppermute(values, "col", xor_perm(4, bit))


def gather_features(values):
    half = values.shape[0] // 2
    from_x = send_col(values, 1)
    from_y = send_col(values, 2)
    far_top = send_col(from_y[:half], 1)
    far_low = send_col(from_x[half:], 2)
    return values, from_x, from_y, far_top, far_low


def sum_features(own, send, *earlier):
    half = own.shape[0] // 2
    via_x = send_col(send[2, :half], 1).astype(F32)
    via_y = send_col(send[2, half:], 2).astype(F32)
    if earlier:
        via_x = after(via_x, *earlier)
        via_y = after(via_y, *earlier)
    part_x = send[0].astype(F32)
    part_y = send[1].astype(F32)
    to_y = jnp.concatenate([part_y[:half] + via_x, part_y[half:]], axis=0).astype(BF16)
    to_x = jnp.concatenate([part_x[:half], part_x[half:] + via_y], axis=0).astype(BF16)
    return own + send_col(to_x, 1).astype(F32) + send_col(to_y, 2).astype(F32)


def sum_direct(own, send):
    total = own
    for bit in range(1, 4):
        total = total + send_col(send[bit - 1], bit).astype(F32)
    return total


def gather_halves(values):
    half = values.shape[0] // 2
    top, low = values[:half], values[half:]
    y_top = send_col(top, 2)
    x_low = send_col(low, 1)
    x_top = send_col(top, 1)
    y_low = send_col(low, 2)
    return values, x_top, x_low, y_top, y_low, send_col(y_top, 1), send_col(x_low, 2)


def sum_halves(own, x_top, x_low, y_top, y_low, far_top, far_low):
    via_x = send_col(far_top, 1).astype(F32)
    via_y = send_col(far_low, 2).astype(F32)
    x_top = send_col(x_top, 1)
    y_low = send_col(y_low, 2)
    x_low = send_col((x_low.astype(F32) + via_y).astype(BF16), 1)
    y_top = send_col((y_top.astype(F32) + via_x).astype(BF16), 2)
    top = x_top.astype(F32) + y_top.astype(F32)
    low = x_low.astype(F32) + y_low.astype(F32)
    return own + jnp.concatenate([top, low], axis=0)


def sum_scalars(values):
    return (values + send_col(values, 1)) + (send_col(values, 2) + send_col(values, 3))


def swap_cores(mine, dp):
    other = lax.ppermute(mine, "dp", [(0, 1), (1, 0)])
    return jnp.where(
        dp == 0, jnp.concatenate([mine, other], axis=0), jnp.concatenate([other, mine], axis=0)
    )


def gather_weight(block, dp, *earlier):
    rows = block.shape[0] // 2
    half = lax.dynamic_slice_in_dim(block, dp * rows, rows, 0)
    if earlier:
        half = after(half, *earlier)
    return lax.all_gather(half, ("row", "dp"), axis=0, tiled=True)


def scatter_weight(grad, dp):
    mine = lax.psum_scatter(grad, ("row", "dp"), scatter_dimension=0, tiled=True)
    return swap_cores(mine, dp).astype(F32)


def sum_small(values):
    count = lax.axis_size("row")
    if count != 4:
        return lax.psum(values, ("dp", "row"))
    size = values.shape[0]
    total = jnp.pad(values, (0, -size % 1024)).reshape(-1, 128)
    total = total + lax.ppermute(total, "dp", [(0, 1), (1, 0)])
    others = [lax.ppermute(total, "row", xor_perm(count, bit)) for bit in range(1, count)]
    return ((total + others[0]) + (others[1] + others[2])).reshape(-1)[:size]


def on_device(
    inputs,
    out_grad,
    seq_lengths,
    first_gain,
    query_proj,
    key_proj,
    value_proj,
    decay_proj,
    beta_proj,
    gate_proj,
    query_conv,
    key_conv,
    value_conv,
    decay_log,
    step_bias,
    output_gain,
    output_proj,
    second_gain,
    hidden_gate,
    hidden_up,
    hidden_down,
):
    seq_count, length, col_width = inputs.shape
    heads = decay_log.shape[0]
    parts = PARTS
    per_part = seq_count // parts
    tokens = per_part * length
    col = lax.axis_index("col")
    dp = lax.axis_index("dp")
    order = (col ^ jnp.arange(4, dtype=jnp.int32)).astype(jnp.int32)
    row_block = query_proj.shape[0]
    vals = heads * DV
    qkv = heads * (2 * DK + DV)
    ff = hidden_gate.shape[1]
    ff_pad = -ff % 128

    in_block = jnp.concatenate(
        [query_proj, key_proj, value_proj, gate_proj, decay_proj, beta_proj,
         jnp.zeros((row_block, 128 - 2 * heads), BF16)], axis=1)
    in_weights = gather_weight(in_block, dp)
    positions = lax.broadcasted_iota(jnp.int32, (seq_count, length), 1)
    valid_all = (positions < seq_lengths[:, None]).astype(F32)
    grad_all = out_grad.astype(F32) * valid_all[:, :, None]
    ff_block = jnp.concatenate(
        [jnp.pad(piece, ((0, 0), (0, ff_pad)))
         for piece in (hidden_gate, hidden_up, hidden_down.T)], axis=1)

    conv = jnp.concatenate([query_conv, key_conv, value_conv], axis=1).astype(F32)
    rates = rate_rows(decay_log, step_bias)
    gain_row = output_gain.astype(F32)[None]
    first_row = first_gain.astype(F32)[None]
    second_row = second_gain.astype(F32)[None]
    first_local = lax.dynamic_slice_in_dim(first_row, col * col_width, col_width, 1)
    second_local = lax.dynamic_slice_in_dim(second_row, col * col_width, col_width, 1)

    state = []
    for part in range(parts):
        seqs = slice(part * per_part, (part + 1) * per_part)
        local = inputs[seqs].reshape(tokens, col_width)
        state.append(dict(
            lens=seq_lengths[seqs], valid=valid_all[seqs].reshape(tokens, 1), local=local,
            grad_out=grad_all[seqs].reshape(tokens, col_width), pieces=gather_features(local)))
    out_weights = gather_weight(output_proj.T, dp, state[0]["pieces"][1])
    for st in state:
        proj, st["normed"], st["scale"] = norm_project(
            st["pieces"], first_row, in_weights, st["lens"], order, length)
        st["proj"] = proj.reshape(per_part, length, -1)
        if st is state[0]:
            grad_low = grad_all.astype(BF16).reshape(seq_count * length, col_width)
            grad_full = lax.all_gather(after(grad_low, st["scale"]), "col", axis=1, tiled=True)
            ff_weights = gather_weight(ff_block, dp, st["scale"])
        mixed, *st["saved"] = mixer_fwd(st["proj"], conv, rates, gain_row, heads, per_part)
        st["mixed"] = mixed.reshape(tokens, vals)
        attention = sum_halves(*spread_halves(st["mixed"], out_weights, order))
        st["hidden"] = st["local"].astype(F32) + attention
        st["pieces"] = gather_halves(st["hidden"].astype(BF16))
    results = []
    gate_up_grad = 0.0
    down_grad = 0.0
    second_gain_grad = 0.0
    for part, st in enumerate(state):
        st["grad_full"] = grad_full[part * tokens : (part + 1) * tokens]
        normed, scale, act, both, dots, feed_own, feed_send, *sends = feed_forward(st["pieces"], st["grad_full"], second_row, ff_weights, st["lens"], order,
                          length)
        dots = sum_scalars(dots)[:, 0, :].reshape(tokens, 1)
        second_grad = sum_halves(*sends) * st["valid"]
        hat = st["hidden"] * scale
        st["hidden_grad"] = st["grad_out"] + scale * (second_grad * second_local)
        st["pieces"] = gather_halves(st["hidden_grad"].astype(BF16))
        hidden, feed_own, feed_send = lax.optimization_barrier(
            (st["hidden"], feed_own, feed_send, st["pieces"][6]))[:3]
        feed = sum_direct(feed_own, feed_send)
        results.append(((hidden + feed) * st["valid"]).astype(BF16))
        second_gain_grad = second_gain_grad + jnp.sum(
            (second_grad + hat * dots / (D * second_local)) * hat, axis=0)
        gate_up_grad = gate_up_grad + contract_rows(normed, both)
        down_grad = down_grad + contract_rows(st["grad_full"], act)
    gate_up_low = gate_up_grad.astype(BF16)
    down_low = down_grad.astype(BF16)
    gate_up_grad = scatter_weight(gate_up_low, dp)
    down_grad = scatter_weight(after(down_low, gate_up_low), dp)
    out_weight_grad = 0.0
    in_weight_grad = 0.0
    first_gain_grad = 0.0
    small = 0.0
    for st in state:
        own = after(st["pieces"][0], gate_up_low, down_low)
        st["attn_grad"], mixed_grad = join_product(
            (own,) + st["pieces"][1:], out_weights, order)
        out_weight_grad = out_weight_grad + contract_rows(st["attn_grad"], st["mixed"])
        if st is state[-1]:
            out_low = out_weight_grad.astype(BF16)
            mixed_grad = after(mixed_grad, out_low)
        dproj, dots, dot_cols, *grads = mixer_bwd(
            st["proj"], mixed_grad.reshape(per_part, length, vals), st["saved"], conv, rates,
            gain_row, heads, per_part, 0)
        small = small + jnp.concatenate([grad.reshape(-1) for grad in grads])
        st["dproj"] = dproj.reshape(tokens, -1)
        st["dots"] = sum_scalars(dots)
        st["dot_cols"] = dot_cols.reshape(tokens, 1)
        in_weight_grad = in_weight_grad + contract_rows(
            st["normed"], after(st["dproj"], *results))
    in_low = in_weight_grad.astype(BF16)
    in_weight_grad = scatter_weight(after(in_low, out_low), dp)
    at = CONV * qkv + 2 * heads
    input_grads = []
    for st in state:
        own, send = spread_product(after(st["dproj"], in_low), in_weights, order, st["normed"],
                                   first_row, st["dot_cols"])
        first_grad = sum_features(own, send) * st["valid"]
        hat = st["local"].astype(F32) * st["scale"]
        total = st["dots"].reshape(tokens, 1)
        first_gain_grad = first_gain_grad + jnp.sum(
            (first_grad + hat * total / (D * first_local)) * hat, axis=0)
        input_grads.append(st["hidden_grad"] + st["scale"] * (first_grad * first_local))
    out_weight_grad = scatter_weight(out_low, dp)
    gain_out = sum_scalars(small[at:].reshape(2, 128)).reshape(-1)
    small_sums = sum_small(
        jnp.concatenate([small[:at], second_gain_grad, gain_out, first_gain_grad]))
    conv_grad = small_sums[: CONV * qkv].reshape(CONV, qkv)
    gate_at = qkv + vals
    qk = heads * DK
    return (
        jnp.concatenate(results, axis=0).reshape(seq_count, length, col_width),
        jnp.concatenate(input_grads, axis=0).reshape(seq_count, length, col_width),
        small_sums[at + col_width + DV :],
        in_weight_grad[:, :qk],
        in_weight_grad[:, qk : 2 * qk],
        in_weight_grad[:, 2 * qk : qkv],
        in_weight_grad[:, gate_at : gate_at + heads],
        in_weight_grad[:, gate_at + heads : gate_at + 2 * heads],
        in_weight_grad[:, qkv:gate_at],
        conv_grad[:, :qk],
        conv_grad[:, qk : 2 * qk],
        conv_grad[:, 2 * qk :],
        small_sums[CONV * qkv : CONV * qkv + heads],
        small_sums[CONV * qkv + heads : at],
        small_sums[at + col_width : at + col_width + DV],
        out_weight_grad.T,
        small_sums[at : at + col_width],
        gate_up_grad[:, :ff],
        gate_up_grad[:, ff + ff_pad : 2 * ff + ff_pad],
        down_grad[:, :ff].T,
    )


def solution(mesh):
    in_specs = (
        P(("dp", "row"), None, "col"),
        P(("dp", "row"), None, "col"),
        P(("dp", "row")),
        P(),
        P("row", "col"),
        P("row", "col"),
        P("row", "col"),
        P("row", "col"),
        P("row", "col"),
        P("row", "col"),
        P(None, "col"),
        P(None, "col"),
        P(None, "col"),
        P("col"),
        P("col"),
        P(),
        P("col", "row"),
        P(),
        P("row", "col"),
        P("row", "col"),
        P("col", "row"),
    )
    out_specs = (
        P(("dp", "row"), None, "col"),
        P(("dp", "row"), None, "col"),
        P("col"),
        P("row", "col"),
        P("row", "col"),
        P("row", "col"),
        P("row", "col"),
        P("row", "col"),
        P("row", "col"),
        P(None, "col"),
        P(None, "col"),
        P(None, "col"),
        P("col"),
        P("col"),
        P(),
        P("col", "row"),
        P("col"),
        P("row", "col"),
        P("row", "col"),
        P("col", "row"),
    )
    return jax.shard_map(
        on_device, mesh=mesh, in_specs=in_specs, out_specs=out_specs, check_vma=False
    )
```
